32 devices in a mesh: leaf: 8 (over y, x, core), front: 4 (over z).
Axes of the slice: x: 2, y: 2, z: 4, core: 2. Of those that a mesh axis runs over, the one named last changes fastest.
Arguments:
- leaf_rhs: float32 [8, 64, 256], P('leaf', None, 'front'), may hold values from -6 to 6
- sep_rhs: float32 [8, 64, 256], P('leaf', None, 'front'), may hold values from -6 to 6
- leaf_inverse: float32 [8, 256, 256], P('leaf', 'front'), as said below
- sep_inverse: float32 [8, 256, 256], P('leaf', 'front'), as said below
- leaf_block: float32 [8, 32, 256], P('leaf', None, 'front'), may hold values from -0.375 to 0.375
- sep_block: float32 [8, 32, 256], P('leaf', None, 'front'), may hold values from -0.375 to 0.375
- pattern: int32 [2, 8, 32], replicated, may hold values from 0 to 255, as said below
- outer_solution: float32 [64, 256], P(None, 'front'), may hold values from -6 to 6
Outputs:
- solution: float32 [2, 8, 64, 256], P(None, 'leaf', None, 'front')
The draws below stay inside these ranges and needn't reach their ends.
Inputs may be any that keep to these rules, and one draw needn't show every extreme that they name: `pattern`: within one supernode the 32 entries are distinct and rising, the first is 0 and the last is 255. `leaf_inverse`: each leaf block is lower triangular with its diagonal bounded away from zero. `sep_inverse`: each separator inverse assembled as in the reference program is lower triangular with its diagonal bounded away from zero.
All inputs are finite; a program needn't handle non-finite values.
Results may differ from the reference program's by a relative error of at most 0.0003.
Values sent between devices are 32-bit elements; how exact they have to be, the bound alone decides.
No kernel may reach another device: no remote copies, remote signals or barrier semaphores. Data moves between devices by JAX's collectives and lax.ppermute only.
A program may use at most 64 MiB of HBM per device.

```python
import math
import jax
import jax.numpy as jnp
from jax import lax

RHS = 64
SNDEV = 64
SN = 256
UPD = 32
LEVELS = 3
N_LEAF = 8
N_FRONT = 4


def lower_matrix(key, row_pos, col_pos):
    key_diag, key_off = jax.random.split(key, 2)
    full_shape = (N_LEAF, SN, SN)
    diagonal_part = jax.random.uniform(key_diag, (N_LEAF, SN, 1), jnp.float32, 0.6, 1.4)
    off_part = jax.random.normal(key_off, full_shape, jnp.float32) * (0.6 / math.sqrt(SN))
    matrix = jnp.where(row_pos == col_pos, diagonal_part, jnp.where(col_pos < row_pos, off_part, 0.0))
    return matrix.astype(jnp.float32)


def draw_leaf_inverse(key, part):
    full_shape = (N_LEAF, SN, SN)
    row_pos = lax.broadcasted_iota(jnp.int32, full_shape, 1)
    col_pos = lax.broadcasted_iota(jnp.int32, full_shape, 2)
    return lower_matrix(jax.random.fold_in(key, 11), row_pos, col_pos)


def draw_sep_inverse(key, part):
    full_shape = (N_LEAF, SN, SN)
    group_pos = lax.broadcasted_iota(jnp.int32, full_shape, 0)
    packed_pos = lax.broadcasted_iota(jnp.int32, full_shape, 1)
    col_pos = lax.broadcasted_iota(jnp.int32, full_shape, 2)
    front_part = packed_pos // SNDEV
    inner = packed_pos % SNDEV
    natural = jnp.zeros(full_shape, jnp.int32)
    for level in range(1, LEVELS + 2):
        blocks = 2 ** min(level, LEVELS)
        share = SNDEV // blocks
        offset = SNDEV - (SNDEV >> level - 1)
        inside = (inner >= offset) & (inner < offset + share)
        spot = front_part * SNDEV + group_pos % blocks * share + inner - offset
        natural = jnp.where(inside, spot, natural)
    return lower_matrix(jax.random.fold_in(key, 23), natural, col_pos)


def draw_pattern(key, part):
    inner_count = SN - 2
    scores = jax.random.randint(key, (2, N_LEAF, inner_count), 0, 2 ** 16) * inner_count
    scores = scores + lax.broadcasted_iota(jnp.int32, (2, N_LEAF, inner_count), 2)
    ranking = jnp.argsort(scores, axis=-1).astype(jnp.int32)
    chosen = jnp.sort(ranking[..., :UPD - 2], axis=-1) + 1
    first_row = jnp.zeros((2, N_LEAF, 1), jnp.int32)
    last_row = jnp.full((2, N_LEAF, 1), SN - 1, jnp.int32)
    return jnp.concatenate([first_row, chosen, last_row], axis=-1).astype(jnp.int32)


def block_levels(own_key, dims, pieces, least, top_value):
    factor_of, own = 1.0, jax.random.fold_in(own_key, 6)
    for axis_at, blocks in pieces:
        heights = jnp.exp(jax.random.uniform(jax.random.fold_in(own, axis_at), (blocks,), jnp.float32, least / len(pieces), top_value / len(pieces)))
        factor_of = factor_of * jnp.repeat(heights, dims[axis_at] // blocks).reshape([-1 if axis == axis_at else 1 for axis in range(len(dims))])
    return factor_of


def normal_values(stream_key, dims, spread, most, shards=(), held_as=jnp.bfloat16):
    level = block_levels(stream_key, dims, shards, -0.22, 0.18) if shards else 1.0
    array = jax.random.normal(stream_key, dims, jnp.float32) * spread * level
    return jnp.minimum(jnp.maximum(array, -most), most).astype(held_as)


def setup_inputs(seed: int = 0) -> dict:
    key_list = jax.random.split(jax.random.key(seed), 9)
    return {
        "leaf_rhs": normal_values(key_list[0], (N_LEAF, RHS, SN), 1.0, 6.0, ((0, 8), (2, 4)), jnp.float32),
        "sep_rhs": normal_values(key_list[1], (N_LEAF, RHS, SN), 1.0, 6.0, ((0, 8), (2, 4)), jnp.float32),
        "leaf_inverse": draw_leaf_inverse(jax.random.fold_in(key_list[8], 71), 0),
        "sep_inverse": draw_sep_inverse(jax.random.fold_in(key_list[8], 71), 0),
        "leaf_block": normal_values(key_list[4], (N_LEAF, UPD, SN), SN ** -0.5, 0.375, ((0, 8), (2, 4)), jnp.float32),
        "sep_block": normal_values(key_list[5], (N_LEAF, UPD, SN), SN ** -0.5, 0.375, ((0, 8), (2, 4)), jnp.float32),
        "pattern": draw_pattern(jax.random.fold_in(key_list[8], 71), 0),
        "outer_solution": normal_values(key_list[7], (RHS, SN), 1.0, 6.0, ((1, 4),), jnp.float32),
    }


def times_rows(vectors, matrix):
    return jnp.dot(vectors, matrix, precision=lax.Precision.HIGHEST, preferred_element_type=jnp.float32)


def lowest_bit(group):
    return (group & -group).bit_length() - 1


def level_of(label):
    if label == 0:
        return LEVELS + 1
    return lowest_bit(label) + 1


def children_of(group):
    if group == 0:
        return [(1, N_LEAF // 2)]
    height = lowest_bit(group)
    if height == 0:
        return [(0, group - 1), (0, group)]
    reach = 2 ** (height - 1)
    return [(1, group - reach), (1, group + reach)]


def unpack(packed, label):
    level = level_of(label)
    blocks = 2 ** min(level, LEVELS)
    share = SNDEV // blocks
    offset = SNDEV - (SNDEV >> (level - 1))
    first = 0 if label == 0 else label - 2 ** (level - 1)
    width = packed.shape[2]
    piece = packed[first:first + blocks].reshape(blocks, N_FRONT, SNDEV, width)[:, :, offset:offset + share, :]
    return jnp.transpose(piece, (1, 0, 2, 3)).reshape(SN, width)


def reference(leaf_rhs, sep_rhs, leaf_inverse, sep_inverse, leaf_block, sep_block, pattern, outer_solution):
    rhs_cols = jnp.swapaxes(sep_rhs, 1, 2)
    block_cols = jnp.swapaxes(sep_block, 1, 2)
    inverse = {}
    right = {}
    blocks = {}
    for group in range(N_LEAF):
        inverse[(0, group)] = leaf_inverse[group]
        right[(0, group)] = leaf_rhs[group]
        blocks[(0, group)] = leaf_block[group]
        inverse[(1, group)] = unpack(sep_inverse, group)
        right[(1, group)] = unpack(rhs_cols, group).T
        blocks[(1, group)] = unpack(block_cols, group).T
    solved = {}
    for group in range(N_LEAF):
        solved[(0, group)] = times_rows(right[(0, group)], inverse[(0, group)].T)
    order_list = []
    for height in range(LEVELS):
        for group in range(1, N_LEAF):
            if lowest_bit(group) == height:
                order_list.append(group)
    order_list.append(0)
    for group in order_list:
        gathered = jnp.zeros((RHS, SN), jnp.float32)
        for child in children_of(group):
            update = times_rows(solved[child], blocks[child].T)
            gathered = gathered + jnp.zeros((RHS, SN), jnp.float32).at[:, pattern[child[0], child[1]]].add(update)
        solved[(1, group)] = times_rows(right[(1, group)] - gathered, inverse[(1, group)].T)
    result = {}
    picked = jnp.take(outer_solution, pattern[1, 0], axis=1)
    carried = times_rows(picked, blocks[(1, 0)])
    result[(1, 0)] = times_rows(solved[(1, 0)] - carried, inverse[(1, 0)])
    for group in reversed(order_list):
        for child in children_of(group):
            picked = jnp.take(result[(1, group)], pattern[child[0], child[1]], axis=1)
            carried = times_rows(picked, blocks[child])
            result[child] = times_rows(solved[child] - carried, inverse[child])
    leaves = jnp.stack([result[(0, group)] for group in range(N_LEAF)])
    separators = jnp.stack([result[(1, group)] for group in range(N_LEAF)])
    return jnp.stack([leaves, separators])
```

```python
import functools
import jax
import jax.numpy as jnp
from jax import lax
from jax.experimental import pallas as pl
from jax.experimental.pallas import tpu as pltpu
from jax.sharding import PartitionSpec as P

HI = lax.Precision.HIGHEST


def nn(left, right):
    return lax.dot_general(
        left, right, (((1,), (0,)), ((), ())), precision=HI, preferred_element_type=jnp.float32
    )


def nt(left, right):
    return lax.dot_general(
        left, right, (((1,), (1,)), ((), ())), precision=HI, preferred_element_type=jnp.float32
    )


def exchange(block, axis, mask):
    count = lax.axis_size(axis)
    return lax.ppermute(block, axis, [(src, src ^ mask) for src in range(count)])


def call(kernel, outs, args, scratch=(), smem=()):
    specs = [
        pl.BlockSpec(memory_space=pltpu.SMEM if pos in smem else pltpu.VMEM)
        for pos in range(len(args))
    ]
    return pl.pallas_call(
        kernel,
        out_shape=[jax.ShapeDtypeStruct(shape, jnp.float32) for shape in outs],
        in_specs=specs,
        out_specs=[pl.BlockSpec(memory_space=pltpu.VMEM) for _ in outs],
        scratch_shapes=list(scratch),
        cost_estimate=pl.CostEstimate(flops=1000000, bytes_accessed=1000000, transcendentals=0),
    )(*args)


class Plan:
    def __init__(self, groups, fronts, rhs, upd, rows):
        self.groups, self.fronts, self.rhs, self.upd, self.rows = groups, fronts, rhs, upd, rows
        self.depth = groups.bit_length() - 1
        self.full = fronts * rows
        self.width = self.full + 128
        self.share, self.offset, self.base, self.blocks = {}, {}, {}, {}
        base = 0
        for level in range(1, self.depth + 2):
            self.blocks[level] = 2 ** min(level, self.depth)
            self.share[level] = rows // self.blocks[level]
            self.offset[level] = rows - (rows >> level - 1)
            self.base[level] = base
            base += fronts * self.share[level]

    def label(self, level, group):
        if level > self.depth:
            return jnp.int32(0)
        return (group // 2**level) * 2**level + 2 ** (level - 1)


def pack_kernel(plan, lr, sr, li, si, lu, su, outer, leaf_out, sep_out):
    half = plan.rhs // 2
    full = plan.full
    leaf_out[:, :full] = li[0]
    leaf_out[:, full:] = jnp.concatenate([lr[0], lu[0], outer[:half]], axis=0).T
    sep_out[:, :full] = si[0]
    sep_out[:, full:] = jnp.concatenate([sr[0], su[0], outer[half:]], axis=0).T


def one_hot(plan, pattern, kind, label):
    ids = pattern[kind, pl.ds(label, 1), :]
    rows = lax.broadcasted_iota(jnp.int32, (plan.full, plan.upd), 0)
    return (rows == ids).astype(jnp.float32)


def gathered_kernel(plan, where, *refs):
    count = plan.fronts
    leafs, seps = refs[:count], refs[count : 2 * count]
    leaf_all, sep_all, x_part, y_part, update, y_leaf, outer_all, lanes = refs[2 * count :]
    front = where[0]
    for slot in range(count):
        at = pl.multiple_of((front ^ slot) * plan.rows, plan.rows)
        leaf_all[pl.ds(at, plan.rows), :] = leafs[slot][...]
        lanes[pl.ds(at, plan.rows), :] = seps[slot][:, plan.full :]
        for level in range(1, plan.depth + 2):
            share, offset = plan.share[level], plan.offset[level]
            piece = seps[slot][offset : offset + share, :]
            dest = pl.multiple_of(plan.base[level] + (front ^ slot) * share, share)
            sep_all[pl.ds(dest, share), :] = piece
            if level >= 2:
                x_part[pl.ds(pl.multiple_of(dest - plan.base[2], share), share), :] = piece
            if level >= 3:
                y_part[pl.ds(pl.multiple_of(dest - plan.base[3], share), share), :] = piece
    flipped = leaf_all[:, plan.full :].T
    leaf_y = nt(flipped[: plan.rhs], leaf_all[:, : plan.full])
    y_leaf[...] = leaf_y
    update[...] = nt(leaf_y, flipped[plan.rhs : plan.rhs + plan.upd])
    half = plan.rhs // 2
    outer_all[:half] = flipped[plan.rhs + plan.upd :]
    outer_all[half:] = lanes[...].T[plan.rhs + plan.upd :]


def assemble(plan, level, group, parts, out):
    share, blocks = plan.share[level], plan.blocks[level]
    for slot in range(blocks):
        ref, start = parts[slot]
        inner = (group & (blocks - 1)) ^ slot
        for front in range(plan.fronts):
            dest = pl.multiple_of(front * plan.rows + inner * share, share)
            out[pl.ds(dest, share), :] = ref[start + front * share : start + (front + 1) * share, :]


def forward_step(plan, level, group, whole, pattern, mine, other):
    kind = 0 if level == 1 else 1
    if level == 1:
        labels = (group, group ^ 1)
    else:
        labels = (plan.label(level - 1, group), plan.label(level - 1, group ^ 2 ** (level - 1)))
    flipped = whole[:, plan.full :].T
    right = flipped[: plan.rhs]
    block = flipped[plan.rhs : plan.rhs + plan.upd]
    right = right - nt(mine, one_hot(plan, pattern, kind, labels[0]))
    if other is not None:
        right = right - nt(other, one_hot(plan, pattern, kind, labels[1]))
    return nt(right, whole[:, : plan.full]), block


def level_kernel(plan, level, where, pattern, mine, other, *refs):
    blocks = plan.blocks[level]
    parts, (whole, y_out, u_out) = refs[:blocks], refs[blocks:]
    group = where[1]
    starts = [plan.base[level] - (0 if slot < 2 else plan.base[2]) for slot in range(blocks)]
    assemble(plan, level, group, list(zip(parts, starts)), whole)
    y_level, block = forward_step(plan, level, group, whole, pattern, mine[...], other[...])
    y_out[...] = y_level
    u_out[...] = nt(y_level, block)


def finish_kernel(plan, where, pattern, mine, other, *refs):
    parts = refs[:8]
    outer, leaf_all, y_leaf, whole1, y1, whole2, y2, out, whole3, whole4 = refs[8:]
    group, front = where[1], where[0]
    full = plan.full

    def starts(level):
        bases = [plan.base[1]] * 2 + [plan.base[2]] * 2 + [plan.base[3]] * 4
        return [(parts[slot], plan.base[level] - bases[slot]) for slot in range(8)]

    assemble(plan, 3, group, starts(3), whole3)
    assemble(plan, 4, group, starts(4), whole4)
    y3, block3 = forward_step(plan, 3, group, whole3, pattern, mine[...], other[...])
    u3 = nt(y3, block3)
    y4, block4 = forward_step(plan, 4, group, whole4, pattern, u3, None)
    picked = nn(outer[...], one_hot(plan, pattern, 1, 0))
    x4 = nn(y4 - nn(picked, block4), whole4[:, :full])
    picked = nn(x4, one_hot(plan, pattern, 1, plan.label(3, group)))
    x3 = nn(y3 - nn(picked, block3), whole3[:, :full])
    picked = nn(x3, one_hot(plan, pattern, 1, plan.label(2, group)))
    block2 = whole2[:, full:].T[plan.rhs : plan.rhs + plan.upd]
    x2 = nn(y2[...] - nn(picked, block2), whole2[:, :full])
    picked = nn(x2, one_hot(plan, pattern, 1, plan.label(1, group)))
    block1 = whole1[:, full:].T[plan.rhs : plan.rhs + plan.upd]
    x1 = nn(y1[...] - nn(picked, block1), whole1[:, :full])
    picked = nn(x1, one_hot(plan, pattern, 0, group))
    block0 = leaf_all[:, full:].T[plan.rhs : plan.rhs + plan.upd]
    x0 = nn(y_leaf[...] - nn(picked, block0), leaf_all[:, :full])
    sep_x = x4
    for level, value in ((3, x3), (2, x2), (1, x1)):
        sep_x = jnp.where(plan.label(level, group) == group, value, sep_x)

    def own_columns(value):
        result = value[:, : plan.rows]
        for slot in range(1, plan.fronts):
            result = jnp.where(front == slot, value[:, slot * plan.rows : (slot + 1) * plan.rows], result)
        return result

    out[0, 0] = own_columns(x0)
    out[1, 0] = own_columns(sep_x)


def partner(block, axis, distance):
    count = lax.axis_size(axis)
    route = []
    for low in range(count):
        high = low | 1 << distance
        if high != low and high < count:
            route += [(low, high), (high, low)]
    return lax.ppermute(block, axis, route)


def times_rows(vectors, matrix):
    return jnp.dot(
        vectors, matrix, precision=lax.Precision.HIGHEST, preferred_element_type=jnp.float32
    )


def against_rows(vectors, matrix):
    return lax.dot_general(
        vectors,
        matrix,
        (((1,), (1,)), ((), ())),
        precision=lax.Precision.HIGHEST,
        preferred_element_type=jnp.float32,
    )


def general(
    leaf_rhs, sep_rhs, leaf_inverse, sep_inverse, leaf_block, sep_block, pattern, outer_solution
):
    group_count = lax.axis_size("leaf")
    depth = group_count.bit_length() - 1
    group_pos = lax.axis_index("leaf")
    front_pos = lax.axis_index("front")
    local_rows = leaf_rhs.shape[-1]
    full_rows = leaf_inverse.shape[-1]
    vector_count = leaf_rhs.shape[1]
    leaf_r = leaf_rhs[0]
    leaf_inv = leaf_inverse[0]
    leaf_u = leaf_block[0]
    sep_r = sep_rhs[0]
    sep_inv = sep_inverse[0]
    sep_u = sep_block[0]
    all_rows = jnp.arange(full_rows, dtype=jnp.int32)

    def geometry(level):
        blocks = 2 ** min(level, depth)
        share = local_rows // blocks
        offset = local_rows - (local_rows >> level - 1)
        return (share, offset, group_pos % blocks)

    def label_of(level):
        if level > depth:
            return jnp.int32(0)
        return group_pos // 2**level * 2**level + 2 ** (level - 1)

    def ids_of(level):
        return lax.dynamic_index_in_dim(pattern[1], label_of(level), 0, keepdims=False)

    def block_sum(term, level):
        nbits = min(level, depth)
        if nbits == depth:
            return lax.psum(term, ("leaf", "front"))
        piece = lax.psum_scatter(term, "front", scatter_dimension=1, tiled=True)
        for bit in range(nbits):
            piece = piece + partner(piece, "leaf", bit)
        return lax.all_gather(piece, "front", axis=1, tiled=True)

    leaf_y = against_rows(lax.all_gather(leaf_r, "front", axis=1, tiled=True), leaf_inv)
    leaf_ids = lax.dynamic_index_in_dim(pattern[0], group_pos, 0, keepdims=False)
    child_part = against_rows(leaf_y, leaf_u)
    child_ids = leaf_ids
    solved = {}
    for level in range(1, depth + 2):
        share, offset, inner_pos = geometry(level)
        own_r = sep_r[:, offset : offset + share]
        start_col = front_pos * local_rows + inner_pos * share
        contribution = jnp.zeros((vector_count, full_rows), jnp.float32)
        contribution = lax.dynamic_update_slice(contribution, own_r, (jnp.int32(0), start_col))
        selector = (child_ids[:, None] == all_rows[None, :]).astype(jnp.float32)
        contribution = contribution - times_rows(child_part, selector)
        whole_v = block_sum(contribution, level)
        y_level = against_rows(whole_v, sep_inv[offset : offset + share, :])
        solved[level] = y_level
        if level <= depth:
            child_part = against_rows(y_level, sep_u[:, offset : offset + share])
            child_ids = ids_of(level)
    parent_x = lax.all_gather(outer_solution, "front", axis=1, tiled=True)
    sep_full = jnp.zeros((vector_count, full_rows), jnp.float32)
    for level in range(depth + 1, 0, -1):
        share, offset, inner_pos = geometry(level)
        picked = jnp.take(parent_x, ids_of(level), axis=1)
        rest = solved[level] - times_rows(picked, sep_u[:, offset : offset + share])
        term = times_rows(rest, sep_inv[offset : offset + share, :])
        parent_x = block_sum(term, level)
        sep_full = jnp.where(label_of(level) == group_pos, parent_x, sep_full)
    picked = jnp.take(parent_x, leaf_ids, axis=1)
    rest = leaf_y - times_rows(picked, leaf_u)
    leaf_x = lax.psum_scatter(times_rows(rest, leaf_inv), "front", scatter_dimension=1, tiled=True)
    sep_x = lax.dynamic_slice_in_dim(sep_full, front_pos * local_rows, local_rows, 1)
    return jnp.stack([leaf_x, sep_x])[:, None]


def chain(
    plan, leaf_rhs, sep_rhs, leaf_inverse, sep_inverse, leaf_block, sep_block, pattern, outer
):
    full, rows, rhs, upd, width = plan.full, plan.rows, plan.rhs, plan.upd, plan.width
    group = lax.axis_index("leaf")
    where = jnp.stack([lax.axis_index("front"), group]).astype(jnp.int32)
    leaf_pack, sep_pack = call(
        functools.partial(pack_kernel, plan),
        [(rows, width)] * 2,
        (leaf_rhs, sep_rhs, leaf_inverse, sep_inverse, leaf_block, sep_block, outer),
    )
    leafs, seps = [leaf_pack] + [None] * 3, [sep_pack] + [None] * 3
    for mask in (3, 2, 1):
        leafs[mask] = exchange(leaf_pack, "front", mask)
        seps[mask] = exchange(sep_pack, "front", mask)
    last = plan.fronts * rows
    leaf_all, sep_all, x_part, y_part, update, y_leaf, outer_all = call(
        functools.partial(gathered_kernel, plan),
        [
            (full, width),
            (full, width),
            (last - plan.base[2], width),
            (last - plan.base[3], width),
            (rhs, upd),
            (rhs, full),
            (rhs, full),
        ],
        (where, *leafs, *seps),
        scratch=[pltpu.VMEM((full, 128), jnp.float32)],
        smem=(0,),
    )
    update_other = exchange(update, "leaf", 1)
    sep_core = exchange(sep_all, "leaf", 1)
    by_x = exchange(x_part, "leaf", 2)
    by_y = exchange(y_part, "leaf", 4)
    by_xy = exchange(y_part, "leaf", 6)
    whole1, y1, u1 = call(
        functools.partial(level_kernel, plan, 1),
        [(full, width), (rhs, full), (rhs, upd)],
        (where, pattern, update, update_other, sep_all, sep_core),
        smem=(0,),
    )
    u1_other = exchange(u1, "leaf", 2)
    by_x_core = exchange(by_x, "leaf", 1)
    whole2, y2, u2 = call(
        functools.partial(level_kernel, plan, 2),
        [(full, width), (rhs, full), (rhs, upd)],
        (where, pattern, u1, u1_other, sep_all, sep_core, by_x, by_x_core),
        smem=(0,),
    )
    u2_other = exchange(u2, "leaf", 4)
    by_y_core = exchange(by_y, "leaf", 1)
    by_xy_core = exchange(by_xy, "leaf", 1)
    parts = (sep_all, sep_core, by_x, by_x_core, by_y, by_y_core, by_xy, by_xy_core)
    (out,) = call(
        functools.partial(finish_kernel, plan),
        [(2, 1, rhs, rows)],
        (where, pattern, u2, u2_other, *parts, outer_all, leaf_all, y_leaf, whole1, y1, whole2, y2),
        scratch=[pltpu.VMEM((full, width), jnp.float32)] * 2,
        smem=(0,),
    )
    return out


def body(*args):
    groups, fronts = lax.axis_size("leaf"), lax.axis_size("front")
    rhs, rows, upd = args[0].shape[1], args[0].shape[2], args[4].shape[1]
    plan = Plan(groups, fronts, rhs, upd, rows)
    if (groups, fronts) == (8, 4) and rows == 64 and rhs + upd + rhs // 2 == 128:
        return chain(plan, *args)
    return general(*args)


def solution(mesh):
    placed = (
        P("leaf", None, "front"),
        P("leaf", None, "front"),
        P("leaf", "front", None),
        P("leaf", "front", None),
        P("leaf", None, "front"),
        P("leaf", None, "front"),
        P(),
        P(None, "front"),
    )
    return jax.shard_map(
        body, mesh=mesh, in_specs=placed, out_specs=P(None, "leaf", None, "front"), check_vma=False
    )
```

```python
import functools
import jax
import jax.numpy as jnp
from jax import lax
from jax.experimental import pallas as pl
from jax.experimental.pallas import tpu as pltpu
from jax.sharding import PartitionSpec as P

def halves(value):
    high = value.astype(jnp.bfloat16)
    return high, (value - high.astype(jnp.float32)).astype(jnp.bfloat16)


def product(left, right, side):
    def term(one, two):
        return lax.dot_general(
            one, two, (((1,), (side,)), ((), ())), preferred_element_type=jnp.float32
        )

    (left_high, left_low), (right_high, right_low) = halves(left), halves(right)
    return term(left_high, right_high) + (term(left_high, right_low) + term(left_low, right_high))


def nn(left, right):
    return product(left, right, 0)


def nt(left, right):
    return product(left, right, 1)


def exchange(block, axis, mask):
    count = lax.axis_size(axis)
    return lax.ppermute(block, axis, [(src, src ^ mask) for src in range(count)])


def call(kernel, outs, args, scratch=(), chip=True, cost=1000):
    if chip:
        args = [
            pltpu.with_memory_space_constraint(arg, pltpu.VMEM)
            if arg.ndim == 2 and arg.dtype == jnp.float32
            else arg
            for arg in args
        ]
    return pl.pallas_call(
        kernel,
        out_shape=[
            pltpu.VMEM(shape, jnp.float32)
            if len(shape) < 4
            else jax.ShapeDtypeStruct(shape, jnp.float32)
            for shape in outs
        ],
        in_specs=[pl.BlockSpec(memory_space=pltpu.VMEM) for _ in args],
        out_specs=[pl.BlockSpec(memory_space=pltpu.VMEM) for _ in outs],
        scratch_shapes=list(scratch),
        compiler_params=pltpu.CompilerParams(vmem_limit_bytes=8 << 20) if chip else None,
        cost_estimate=pl.CostEstimate(flops=cost, bytes_accessed=cost, transcendentals=0),
    )(*args)


class Plan:
    def __init__(self, groups, fronts, rhs, upd, rows):
        self.groups, self.fronts, self.rhs, self.upd, self.rows = groups, fronts, rhs, upd, rows
        self.depth = groups.bit_length() - 1
        self.full = fronts * rows
        self.width = self.full + 128
        self.share, self.offset, self.base, self.blocks = {}, {}, {}, {}
        base = 0
        for level in range(1, self.depth + 2):
            self.blocks[level] = 2 ** min(level, self.depth)
            self.share[level] = rows // self.blocks[level]
            self.offset[level] = rows - (rows >> level - 1)
            self.base[level] = base
            base += fronts * self.share[level]

    def label(self, level, group):
        if level > self.depth:
            return jnp.int32(0)
        return (group // 2**level) * 2**level + 2 ** (level - 1)

    def child_ids(self, level, group, pattern):
        if level == 1:
            kind, labels = 0, (group, group ^ 1)
        elif level > self.depth:
            kind, labels = 1, (self.label(level - 1, group),)
        else:
            kind = 1
            labels = tuple(self.label(level - 1, far) for far in (group, group ^ 2 ** (level - 1)))
        return jnp.concatenate([pattern[kind, pl.ds(label, 1), :] for label in labels], axis=1)


def one_hot(ids, count, start=0):
    rows = lax.broadcasted_iota(jnp.int32, (count, ids.shape[1]), 0) + start
    return (rows == ids).astype(jnp.float32)


def own_columns(plan, front, value):
    rows = plan.rows
    result = value[:, :rows]
    for slot in range(1, plan.fronts):
        result = jnp.where(front == slot, value[:, slot * rows : (slot + 1) * rows], result)
    return result


def place():
    return lax.axis_index("front"), lax.axis_index("leaf")


def pack_kernel(plan, pattern, lr, sr, li, si, lu, su, outer, out):
    full, rhs, upd, rows = plan.full, plan.rhs, plan.upd, plan.rows
    front, _ = place()
    flat = jnp.concatenate([sr[0], su[0], jnp.zeros((upd, rows), jnp.float32), lr[0]], axis=0).T
    out[:rows, :full] = si[0]
    out[:rows, full:] = flat[:, :128]
    out[:rows, full + rhs + upd :] = nn(outer[...], one_hot(pattern[1, 0:1, :], rows, front * rows))
    out[rows:, :full] = nn(lu[0], li[0])
    out[rows:, full : full + rhs] = flat[: rows // 2, 128:]
    out[rows:, full + rhs :] = flat[rows // 2 :, 128:]


def spread_kernel(plan, *refs):
    count = plan.fronts
    packs = refs[:count]
    sep_all, x_part, y_part, picked, update, leaf_r, fold, turned = refs[count:]
    full, rhs, rows = plan.full, plan.rhs, plan.rows
    front, _ = place()
    for slot in range(count):
        at = pl.multiple_of((front ^ slot) * rows, rows)
        turned[pl.ds(at, rows // 2), :] = packs[slot][rows:, full : full + rhs]
        turned[pl.ds(at + rows // 2, rows // 2), :] = packs[slot][rows:, full + rhs :]
    folded = packs[0][rows:, :full]
    total = packs[0][:rows, full + rhs + plan.upd :]
    for slot in range(1, count):
        folded = folded + packs[slot][rows:, :full]
        total = total + packs[slot][:rows, full + rhs + plan.upd :]
    right = turned[...].T
    first = nt(right, folded)
    for slot in range(count):
        for level in range(1, plan.depth + 2):
            share, offset = plan.share[level], plan.offset[level]
            piece = packs[slot][offset : offset + share, :]
            dest = pl.multiple_of(plan.base[level] + (front ^ slot) * share, share)
            sep_all[pl.ds(dest, share), :] = piece
            if level >= 2:
                x_part[pl.ds(pl.multiple_of(dest - plan.base[2], share), share), :] = piece
            if level >= 3:
                y_part[pl.ds(pl.multiple_of(dest - plan.base[3], share), share), :] = piece
    sep_all[:rhs, full + rhs + plan.upd :] = first
    update[...] = first
    picked[...] = total
    leaf_r[...] = right
    fold[...] = own_columns(plan, front, folded)


def leaf_back_kernel(plan, leaf_r, matrix, keep, send):
    front, _ = place()
    term = nn(nt(leaf_r[...], matrix[0]), matrix[0])
    low, high = term[:, : plan.full // 2], term[:, plan.full // 2 :]
    upper = front // 2 == 1
    keep[...] = jnp.where(upper, high, low)
    send[...] = jnp.where(upper, low, high)


def leaf_part_kernel(plan, kept, got, keep, send):
    front, _ = place()
    term = kept[...] + got[...]
    low, high = term[:, : plan.rows], term[:, plan.rows :]
    upper = front % 2 == 1
    keep[...] = jnp.where(upper, high, low)
    send[...] = jnp.where(upper, low, high)


def level_kernel(plan, level, pattern, *refs):
    blocks, share = plan.blocks[level], plan.share[level]
    parts, (whole, cross, start) = refs[:blocks], refs[blocks:]
    _, group = place()
    bases = [1, 1, 2, 2, 3, 3, 3, 3]
    for slot in range(blocks):
        first = plan.base[level] - plan.base[bases[slot]]
        inner = (group & (blocks - 1)) ^ slot
        for front in range(plan.fronts):
            dest = pl.multiple_of(front * plan.rows + inner * share, share)
            whole[pl.ds(dest, share), :] = parts[slot][first + front * share : first + (front + 1) * share, :]
    flipped = whole[:, plan.full :].T
    folded = nn(flipped[plan.rhs : plan.rhs + plan.upd], whole[:, : plan.full])
    cross[...] = nn(folded, one_hot(plan.child_ids(level, group, pattern), plan.full))
    start[...] = nt(flipped[: plan.rhs], folded)


def back_kernel(plan, level, pattern, whole, picks, columns):
    front, group = place()
    ids = plan.child_ids(level, group, pattern)
    hot = one_hot(ids, plan.full)
    matrix = whole[:, : plan.full]
    flipped = whole[:, plan.full :].T
    ahead = nt(jnp.concatenate([flipped[: plan.rhs], hot.T], axis=0), matrix)
    both = nn(jnp.concatenate([ahead, flipped[plan.rhs : plan.rhs + plan.upd]], axis=0), matrix)
    picks[...] = nn(both, hot[:, : plan.upd])
    columns[...] = own_columns(plan, front, both)


def update_kernel(plan, start, cross, mine, other, out):
    upd = plan.upd
    out[...] = start[...] - nt(mine[...], cross[:, :upd]) - nt(other[...], cross[:, upd:])


def finish_kernel(plan, *refs):
    start3, cross3, top_s, fold, leaf_kept, leaf_got = refs[:6]
    updates = [(refs[6 + 2 * pos][...], refs[7 + 2 * pos][...]) for pos in range(3)]
    picks = [ref for ref in refs[12:16]]
    columns = [ref for ref in refs[16:20]]
    out = refs[20]
    rhs, upd = plan.rhs, plan.upd
    _, group = place()
    u3 = start3[...] - nt(updates[2][0], cross3[:, :upd]) - nt(updates[2][1], cross3[:, upd:])
    s_level = {4: top_s[...]}
    weights = {4: jnp.concatenate([u3, s_level[4]], axis=1)}
    s_level[3] = picks[3][:rhs] - nn(weights[4], picks[3][rhs:])
    for level in (3, 2, 1):
        weights[level] = jnp.concatenate([*updates[level - 1], s_level[level]], axis=1)
        s_level[level - 1] = picks[level - 1][:rhs] - nn(weights[level], picks[level - 1][rhs:])
    out[0, 0] = leaf_kept[...] + leaf_got[...] - nn(s_level[0], fold[...])
    empty = jnp.zeros((upd, plan.rows), jnp.float32)
    chosen = jnp.concatenate([columns[3][: rhs + upd], empty, columns[3][rhs + upd :]], axis=0)
    weight = jnp.concatenate([u3, jnp.zeros((rhs, upd), jnp.float32), s_level[4]], axis=1)
    for level in (3, 2, 1):
        here = plan.label(level, group) == group
        chosen = jnp.where(here, columns[level - 1][...], chosen)
        weight = jnp.where(here, weights[level], weight)
    out[1, 0] = chosen[:rhs] - nn(weight, chosen[rhs:])


def partner(block, axis, distance):
    count = lax.axis_size(axis)
    route = []
    for low in range(count):
        high = low | 1 << distance
        if high != low and high < count:
            route += [(low, high), (high, low)]
    return lax.ppermute(block, axis, route)


def times_rows(vectors, matrix):
    return jnp.dot(
        vectors, matrix, precision=lax.Precision.HIGHEST, preferred_element_type=jnp.float32
    )


def against_rows(vectors, matrix):
    return lax.dot_general(
        vectors,
        matrix,
        (((1,), (1,)), ((), ())),
        precision=lax.Precision.HIGHEST,
        preferred_element_type=jnp.float32,
    )


def general(
    leaf_rhs, sep_rhs, leaf_inverse, sep_inverse, leaf_block, sep_block, pattern, outer_solution
):
    group_count = lax.axis_size("leaf")
    depth = group_count.bit_length() - 1
    group_pos = lax.axis_index("leaf")
    front_pos = lax.axis_index("front")
    local_rows = leaf_rhs.shape[-1]
    full_rows = leaf_inverse.shape[-1]
    vector_count = leaf_rhs.shape[1]
    leaf_r = leaf_rhs[0]
    leaf_inv = leaf_inverse[0]
    leaf_u = leaf_block[0]
    sep_r = sep_rhs[0]
    sep_inv = sep_inverse[0]
    sep_u = sep_block[0]
    all_rows = jnp.arange(full_rows, dtype=jnp.int32)

    def geometry(level):
        blocks = 2 ** min(level, depth)
        share = local_rows // blocks
        offset = local_rows - (local_rows >> level - 1)
        return (share, offset, group_pos % blocks)

    def label_of(level):
        if level > depth:
            return jnp.int32(0)
        return group_pos // 2**level * 2**level + 2 ** (level - 1)

    def ids_of(level):
        return lax.dynamic_index_in_dim(pattern[1], label_of(level), 0, keepdims=False)

    def block_sum(term, level):
        nbits = min(level, depth)
        if nbits == depth:
            return lax.psum(term, ("leaf", "front"))
        piece = lax.psum_scatter(term, "front", scatter_dimension=1, tiled=True)
        for bit in range(nbits):
            piece = piece + partner(piece, "leaf", bit)
        return lax.all_gather(piece, "front", axis=1, tiled=True)

    leaf_y = against_rows(lax.all_gather(leaf_r, "front", axis=1, tiled=True), leaf_inv)
    leaf_ids = lax.dynamic_index_in_dim(pattern[0], group_pos, 0, keepdims=False)
    child_part = against_rows(leaf_y, leaf_u)
    child_ids = leaf_ids
    solved = {}
    for level in range(1, depth + 2):
        share, offset, inner_pos = geometry(level)
        own_r = sep_r[:, offset : offset + share]
        start_col = front_pos * local_rows + inner_pos * share
        contribution = jnp.zeros((vector_count, full_rows), jnp.float32)
        contribution = lax.dynamic_update_slice(contribution, own_r, (jnp.int32(0), start_col))
        selector = (child_ids[:, None] == all_rows[None, :]).astype(jnp.float32)
        contribution = contribution - times_rows(child_part, selector)
        whole_v = block_sum(contribution, level)
        y_level = against_rows(whole_v, sep_inv[offset : offset + share, :])
        solved[level] = y_level
        if level <= depth:
            child_part = against_rows(y_level, sep_u[:, offset : offset + share])
            child_ids = ids_of(level)
    parent_x = lax.all_gather(outer_solution, "front", axis=1, tiled=True)
    sep_full = jnp.zeros((vector_count, full_rows), jnp.float32)
    for level in range(depth + 1, 0, -1):
        share, offset, inner_pos = geometry(level)
        picked = jnp.take(parent_x, ids_of(level), axis=1)
        rest = solved[level] - times_rows(picked, sep_u[:, offset : offset + share])
        term = times_rows(rest, sep_inv[offset : offset + share, :])
        parent_x = block_sum(term, level)
        sep_full = jnp.where(label_of(level) == group_pos, parent_x, sep_full)
    picked = jnp.take(parent_x, leaf_ids, axis=1)
    rest = leaf_y - times_rows(picked, leaf_u)
    leaf_x = lax.psum_scatter(times_rows(rest, leaf_inv), "front", scatter_dimension=1, tiled=True)
    sep_x = lax.dynamic_slice_in_dim(sep_full, front_pos * local_rows, local_rows, 1)
    return jnp.stack([leaf_x, sep_x])[:, None]


def chain(
    plan, leaf_rhs, sep_rhs, leaf_inverse, sep_inverse, leaf_block, sep_block, pattern, outer
):
    full, rows, rhs, upd, width = plan.full, plan.rows, plan.rhs, plan.upd, plan.width

    def kernel(body, outs, *args, extra=(), **kw):
        return call(functools.partial(body, plan, *extra), outs, args, **kw)

    (pack,) = kernel(
        pack_kernel,
        [(rows + upd, width)],
        pattern, leaf_rhs, sep_rhs, leaf_inverse, sep_inverse, leaf_block, sep_block, outer,
        chip=False,
    )
    across = exchange(pack, "front", 3)
    beside = exchange(pack, "front", 1)
    beyond = exchange(across, "front", 1)
    sep_all, x_part, y_part, top_s, u0, leaf_r, fold = kernel(
        spread_kernel,
        [
            (full, width),
            (full - plan.base[2], width),
            (full - plan.base[3], width),
            (rhs, upd),
            (rhs, upd),
            (rhs, full),
            (upd, rows),
        ],
        pack, beside, beyond, across,
        scratch=[pltpu.VMEM((full, rhs), jnp.float32)],
    )
    sep_core = exchange(sep_all, "leaf", 1)
    by_x = exchange(x_part, "leaf", 2)
    by_y = exchange(y_part, "leaf", 4)
    by_xy = exchange(y_part, "leaf", 6)
    u0_far = sep_core[:rhs, full + rhs + upd :]

    def level_of(level, *parts):
        kids = 2 if level <= plan.depth else 1
        return kernel(
            level_kernel,
            [(full, width), (upd, kids * upd), (rhs, upd)],
            pattern, *parts,
            extra=(level,),
        )

    def back_of(level, whole):
        kids = 2 if level <= plan.depth else 1
        tall = rhs + (kids + 1) * upd
        return kernel(back_kernel, [(tall, upd), (tall, rows)], pattern, whole, extra=(level,))

    whole1, cross1, start1 = level_of(1, sep_all, sep_core)
    (u1,) = kernel(update_kernel, [(rhs, upd)], start1, cross1, u0, u0_far)
    u1_far = exchange(u1, "leaf", 2)
    leaf_r, _ = lax.optimization_barrier((leaf_r, u1))
    leaf_half, leaf_send = kernel(leaf_back_kernel, [(rhs, full // 2)] * 2, leaf_r, leaf_inverse)
    leaf_sent = exchange(leaf_send, "front", 2)
    picks1, columns1 = back_of(1, whole1)
    by_x, by_y, by_xy, u1_far, leaf_sent, picks1 = lax.optimization_barrier(
        (by_x, by_y, by_xy, u1_far, leaf_sent, picks1)
    )
    by_x_core = exchange(by_x, "leaf", 1)
    by_y_core, by_xy_core = exchange(by_y, "leaf", 1), exchange(by_xy, "leaf", 1)
    whole2, cross2, start2 = level_of(2, sep_all, sep_core, by_x, by_x_core)
    (u2,) = kernel(update_kernel, [(rhs, upd)], start2, cross2, u1, u1_far)
    u2_far = exchange(u2, "leaf", 4)
    leaf_sent, whole2, by_y, _ = lax.optimization_barrier((leaf_sent, whole2, by_y, u2))
    leaf_kept, leaf_send = kernel(leaf_part_kernel, [(rhs, rows)] * 2, leaf_half, leaf_sent)
    leaf_got = exchange(leaf_send, "front", 1)
    parts = (sep_all, sep_core, by_x, by_x_core, by_y, by_y_core, by_xy, by_xy_core)
    picks2, columns2 = back_of(2, whole2)
    whole3, cross3, start3 = level_of(3, *parts)
    picks3, columns3 = back_of(3, whole3)
    whole4, _, _ = level_of(4, *parts)
    picks4, columns4 = back_of(4, whole4)
    (out,) = kernel(
        finish_kernel,
        [(2, 1, rhs, rows)],
        start3, cross3, top_s, fold, leaf_kept, leaf_got, u0, u0_far, u1, u1_far, u2, u2_far,
        picks1, picks2, picks3, picks4, columns1, columns2, columns3, columns4,
    )
    return out


def body(*args):
    groups, fronts = lax.axis_size("leaf"), lax.axis_size("front")
    rhs, rows, upd = args[0].shape[1], args[0].shape[2], args[4].shape[1]
    plan = Plan(groups, fronts, rhs, upd, rows)
    if (groups, fronts) == (8, 4) and rows == 64 and rhs == 64 and upd == 32:
        return chain(plan, *args)
    return general(*args)


def solution(mesh):
    placed = (
        P("leaf", None, "front"),
        P("leaf", None, "front"),
        P("leaf", "front", None),
        P("leaf", "front", None),
        P("leaf", None, "front"),
        P("leaf", None, "front"),
        P(),
        P(None, "front"),
    )
    return jax.shard_map(
        body, mesh=mesh, in_specs=placed, out_specs=P(None, "leaf", None, "front"), check_vma=False
    )
```

```python
import functools
import jax
import jax.numpy as jnp
from jax import lax
from jax.experimental import pallas as pl
from jax.experimental.pallas import tpu as pltpu
from jax.sharding import PartitionSpec as P

def halves(value):
    high = value.astype(jnp.bfloat16)
    return high, (value - high.astype(jnp.float32)).astype(jnp.bfloat16)


def product(left, right, side):
    def term(one, two):
        return lax.dot_general(
            one, two, (((1,), (side,)), ((), ())), preferred_element_type=jnp.float32
        )

    (left_high, left_low), (right_high, right_low) = halves(left), halves(right)
    return term(left_high, right_high) + (term(left_high, right_low) + term(left_low, right_high))


def nn(left, right):
    return product(left, right, 0)


def nt(left, right):
    return product(left, right, 1)


def exchange(block, axis, mask):
    count = lax.axis_size(axis)
    return lax.ppermute(block, axis, [(src, src ^ mask) for src in range(count)])


def call(kernel, outs, args, scratch=(), chip=True, cost=1000):
    if chip:
        args = [
            pltpu.with_memory_space_constraint(arg, pltpu.VMEM)
            if arg.ndim == 2
            else arg
            for arg in args
        ]
    return pl.pallas_call(
        kernel,
        out_shape=[
            jax.ShapeDtypeStruct(out, jnp.float32)
            if len(out) == 4
            else pltpu.VMEM(*out)
            if isinstance(out[0], tuple)
            else pltpu.VMEM(out, jnp.float32)
            for out in outs
        ],
        in_specs=[pl.BlockSpec(memory_space=pltpu.VMEM) for _ in args],
        out_specs=[pl.BlockSpec(memory_space=pltpu.VMEM) for _ in outs],
        scratch_shapes=list(scratch),
        compiler_params=pltpu.CompilerParams(vmem_limit_bytes=8 << 20) if chip else None,
        cost_estimate=pl.CostEstimate(flops=cost, bytes_accessed=cost, transcendentals=0),
    )(*args)


class Plan:
    def __init__(self, groups, fronts, rhs, upd, rows):
        self.groups, self.fronts, self.rhs, self.upd, self.rows = groups, fronts, rhs, upd, rows
        self.depth = groups.bit_length() - 1
        self.full = fronts * rows
        self.width = self.full + 128
        self.share, self.offset, self.base, self.blocks = {}, {}, {}, {}
        base = 0
        for level in range(1, self.depth + 2):
            self.blocks[level] = 2 ** min(level, self.depth)
            self.share[level] = rows // self.blocks[level]
            self.offset[level] = rows - (rows >> level - 1)
            self.base[level] = base
            base += fronts * self.share[level]

    def label(self, level, group):
        if level > self.depth:
            return jnp.int32(0)
        return (group // 2**level) * 2**level + 2 ** (level - 1)

    def child_ids(self, level, group, pattern):
        if level == 1:
            kind, labels = 0, (group, group ^ 1)
        elif level > self.depth:
            kind, labels = 1, (self.label(level - 1, group),)
        else:
            kind = 1
            labels = tuple(self.label(level - 1, far) for far in (group, group ^ 2 ** (level - 1)))
        return jnp.concatenate([pattern[pl.ds(kind * self.groups + label, 1), :] for label in labels], axis=1)


def one_hot(ids, count, start=0):
    rows = lax.broadcasted_iota(jnp.int32, (count, ids.shape[1]), 0) + start
    return (rows == ids).astype(jnp.float32)


def own_columns(plan, front, value):
    rows = plan.rows
    result = value[:, :rows]
    for slot in range(1, plan.fronts):
        result = jnp.where(front == slot, value[:, slot * rows : (slot + 1) * rows], result)
    return result


def place():
    return lax.axis_index("front"), lax.axis_index("leaf")


def pack_kernel(plan, pattern, lr, sr, li, si, lu, su, outer, out, ids):
    full, rhs, upd, rows = plan.full, plan.rhs, plan.upd, plan.rows
    front, _ = place()
    ids[...] = pattern[...].reshape(ids.shape)
    empty = jnp.zeros((upd, rows), jnp.float32)
    out[:rows, :full] = si[0]
    out[:rows, full:] = jnp.concatenate([sr[0], su[0], empty], axis=0).T
    out[:rows, full + rhs + upd :] = nn(outer[...], one_hot(pattern[1, 0:1, :], rows, front * rows))
    out[rows:, :full] = li[0]
    out[rows:, full:] = jnp.concatenate([lr[0], lu[0], empty], axis=0).T


def fold_rows(plan, rows_of):
    step, full, edge = plan.rows, plan.full, plan.full + plan.rhs + plan.upd
    pieces = [rows_of(front)[:, : (front + 1) * step] for front in (3, 2, 0, 1)]
    pieces += [rows_of(front)[:, full:edge] for front in range(plan.fronts)]
    return jnp.concatenate(pieces, axis=1)


def unfold_rows(plan, folded):
    step, full, edge = plan.rows, plan.full, plan.rhs + plan.upd
    count = folded.shape[0]
    starts = {3: 0, 2: full, 0: full + 3 * step, 1: 2 * full}
    for front in range(plan.fronts):
        wide = (front + 1) * step
        side = 2 * full + 2 * step + front * edge
        pieces = [folded[:, starts[front] : starts[front] + wide]]
        if wide < full:
            pieces.append(jnp.zeros((count, full - wide), jnp.float32))
        pieces.append(folded[:, side : side + edge])
        pieces.append(jnp.zeros((count, plan.width - full - edge), jnp.float32))
        yield front, jnp.concatenate(pieces, axis=1)


def spread_kernel(plan, *refs):
    count = plan.fronts
    packs = refs[:count]
    all_part, late_part, high_part, picked, natural = refs[count:]
    rows, edge = plan.rows, plan.full + plan.rhs + plan.upd
    front, _ = place()
    for slot in range(count):
        at = pl.multiple_of((front ^ slot) * rows, rows)
        natural[pl.ds(at, rows), :] = packs[slot][:rows, :]
    total = packs[0][:rows, edge:]
    for slot in range(1, count):
        total = total + packs[slot][:rows, edge:]
    picked[...] = total
    at = 0
    for level in range(1, plan.depth + 2):
        offset, share = plan.offset[level], plan.share[level]
        piece = fold_rows(
            plan, lambda pos: natural[pos * rows + offset : pos * rows + offset + share, :]
        )
        all_part[at : at + share, :] = piece
        if level >= 2:
            late_part[at - plan.share[1] : at - plan.share[1] + share, :] = piece
        if level >= 3:
            low = at - plan.share[1] - plan.share[2]
            high_part[low : low + share, :] = piece
        at += share


def leaf_kernel(plan, *refs):
    count = plan.fronts
    packs, (whole, ahead, update) = refs[:count], refs[count:]
    front, _ = place()
    rhs, upd, full, rows = plan.rhs, plan.upd, plan.full, plan.rows
    for slot in range(count):
        at = pl.multiple_of((front ^ slot) * rows, rows)
        whole[pl.ds(at, rows), :] = packs[slot][rows:, :]
    flipped = whole[:, full:].T
    solved = nt(flipped[:rhs], whole[:, :full])
    ahead[:rhs, :] = solved
    ahead[rhs:, :] = flipped[rhs : rhs + upd]
    update[:rhs, :upd] = nt(solved, flipped[rhs : rhs + upd])


def assemble(plan, level, parts, whole):
    blocks, share = plan.blocks[level], plan.share[level]
    _, group = place()
    for slot in range(blocks):
        least = 1 if slot < 2 else 2 if slot < 4 else 3
        first = sum(plan.share[below] for below in range(least, level))
        inner = (group & (blocks - 1)) ^ slot
        for front, piece in unfold_rows(plan, parts[slot][first : first + share, :]):
            dest = pl.multiple_of(front * plan.rows + inner * share, share)
            whole[pl.ds(dest, share), :] = piece


def solve_level(plan, level, pattern, parts, whole):
    front, group = place()
    assemble(plan, level, parts, whole)
    hot = one_hot(plan.child_ids(level, group, pattern), plan.full)
    matrix = whole[:, : plan.full]
    flipped = whole[:, plan.full :].T
    right, block = flipped[: plan.rhs], flipped[plan.rhs : plan.rhs + plan.upd]
    ahead = nt(jnp.concatenate([right, hot.T], axis=0), matrix)
    both = nn(jnp.concatenate([ahead, block], axis=0), matrix)
    result = [nn(both, hot[:, : plan.upd]), own_columns(plan, front, both)]
    if level <= plan.depth:
        fold = both[plan.rhs + hot.shape[1] :]
        result = [nn(fold, hot), nt(right, fold)] + result
    return result


def level_kernel(plan, level, pattern, *refs):
    parts, outs = refs[: plan.blocks[level]], refs[plan.blocks[level] :]
    for out, value in zip(outs, solve_level(plan, level, pattern, parts, outs[-1])):
        out[...] = value


def upper_kernel(plan, pattern, leaf_all, leaf_ahead, top_s, *refs):
    rhs, upd, group = plan.rhs, plan.upd, place()[1]
    updates = [jnp.concatenate([refs[at][:rhs, :upd], refs[at + 1][:rhs, :upd]], axis=1) for at in (0, 2)]
    near = refs[4][:rhs, :upd]
    picks, columns = {1: refs[5][...], 2: refs[6][...]}, {1: refs[7][...], 2: refs[8][...]}
    parts, (out, whole3, whole4) = refs[9:17], refs[17:]
    cross, start, picks[3], columns[3] = solve_level(plan, 3, pattern, parts, whole3)
    picks[4], columns[4] = solve_level(plan, 4, pattern, parts, whole4)
    leaf_back = own_columns(plan, place()[0], nn(leaf_ahead[...], leaf_all[:, : plan.full]))
    none = jnp.zeros((upd, upd), jnp.float32)
    unit = one_hot(lax.broadcasted_iota(jnp.int32, (1, upd), 1), upd)

    def step(terms, part):
        known = jnp.concatenate([part[:rhs], jnp.zeros((upd, part.shape[1]), jnp.float32)], axis=0)
        return known - nn(jnp.concatenate(terms, axis=1), part[rhs:])

    gap = jnp.zeros((rhs, upd), jnp.float32)
    both = jnp.concatenate(
        [jnp.concatenate([near, gap], axis=1), jnp.concatenate([none, unit], axis=1)], axis=0
    )
    u3 = jnp.concatenate([start, none], axis=0) - nt(both, cross)
    fixed = [jnp.concatenate([pair, jnp.zeros((upd, 2 * upd), jnp.float32)], axis=0) for pair in updates]
    terms = {4: [u3, jnp.concatenate([top_s[...], none], axis=0)]}
    terms[3] = [both, step(terms[4], picks[4])]
    terms[2] = [fixed[1], step(terms[3], picks[3])]
    terms[1] = [fixed[0], step(terms[2], picks[2])]
    leaf_out = step([step(terms[1], picks[1])], leaf_back)
    gap = jnp.zeros((rhs + upd, upd), jnp.float32)
    chosen = jnp.concatenate([columns[4][: rhs + upd], none_wide(plan), columns[4][rhs + upd :]], axis=0)
    weight = jnp.concatenate([terms[4][0], gap, terms[4][1]], axis=1)
    for level in (3, 2, 1):
        here = plan.label(level, group) == group
        chosen = jnp.where(here, columns[level], chosen)
        weight = jnp.where(here, jnp.concatenate(terms[level], axis=1), weight)
    out[...] = jnp.concatenate([leaf_out, step([weight], chosen)], axis=1)


def none_wide(plan):
    return jnp.zeros((plan.upd, plan.rows), jnp.float32)


def finish_kernel(plan, base, far, out):
    rhs, upd, rows = plan.rhs, plan.upd, plan.rows
    total = base[:rhs] + nn(far[:rhs, :upd], base[rhs:])
    out[0, 0] = total[:, :rows]
    out[1, 0] = total[:, rows:]


def update_kernel(plan, start, cross, mine, other, out):
    rhs, upd = plan.rhs, plan.upd
    both = jnp.concatenate([mine[:rhs, :upd], other[:rhs, :upd]], axis=1)
    out[:rhs, :upd] = start[...] - nt(both, cross[...])


def partner(block, axis, distance):
    count = lax.axis_size(axis)
    route = []
    for low in range(count):
        high = low | 1 << distance
        if high != low and high < count:
            route += [(low, high), (high, low)]
    return lax.ppermute(block, axis, route)


def times_rows(vectors, matrix):
    return jnp.dot(
        vectors, matrix, precision=lax.Precision.HIGHEST, preferred_element_type=jnp.float32
    )


def against_rows(vectors, matrix):
    return lax.dot_general(
        vectors,
        matrix,
        (((1,), (1,)), ((), ())),
        precision=lax.Precision.HIGHEST,
        preferred_element_type=jnp.float32,
    )


def general(
    leaf_rhs, sep_rhs, leaf_inverse, sep_inverse, leaf_block, sep_block, pattern, outer_solution
):
    group_count = lax.axis_size("leaf")
    depth = group_count.bit_length() - 1
    group_pos = lax.axis_index("leaf")
    front_pos = lax.axis_index("front")
    local_rows = leaf_rhs.shape[-1]
    full_rows = leaf_inverse.shape[-1]
    vector_count = leaf_rhs.shape[1]
    leaf_r = leaf_rhs[0]
    leaf_inv = leaf_inverse[0]
    leaf_u = leaf_block[0]
    sep_r = sep_rhs[0]
    sep_inv = sep_inverse[0]
    sep_u = sep_block[0]
    all_rows = jnp.arange(full_rows, dtype=jnp.int32)

    def geometry(level):
        blocks = 2 ** min(level, depth)
        share = local_rows // blocks
        offset = local_rows - (local_rows >> level - 1)
        return (share, offset, group_pos % blocks)

    def label_of(level):
        if level > depth:
            return jnp.int32(0)
        return group_pos // 2**level * 2**level + 2 ** (level - 1)

    def ids_of(level):
        return lax.dynamic_index_in_dim(pattern[1], label_of(level), 0, keepdims=False)

    def block_sum(term, level):
        nbits = min(level, depth)
        if nbits == depth:
            return lax.psum(term, ("leaf", "front"))
        piece = lax.psum_scatter(term, "front", scatter_dimension=1, tiled=True)
        for bit in range(nbits):
            piece = piece + partner(piece, "leaf", bit)
        return lax.all_gather(piece, "front", axis=1, tiled=True)

    leaf_y = against_rows(lax.all_gather(leaf_r, "front", axis=1, tiled=True), leaf_inv)
    leaf_ids = lax.dynamic_index_in_dim(pattern[0], group_pos, 0, keepdims=False)
    child_part = against_rows(leaf_y, leaf_u)
    child_ids = leaf_ids
    solved = {}
    for level in range(1, depth + 2):
        share, offset, inner_pos = geometry(level)
        own_r = sep_r[:, offset : offset + share]
        start_col = front_pos * local_rows + inner_pos * share
        contribution = jnp.zeros((vector_count, full_rows), jnp.float32)
        contribution = lax.dynamic_update_slice(contribution, own_r, (jnp.int32(0), start_col))
        selector = (child_ids[:, None] == all_rows[None, :]).astype(jnp.float32)
        contribution = contribution - times_rows(child_part, selector)
        whole_v = block_sum(contribution, level)
        y_level = against_rows(whole_v, sep_inv[offset : offset + share, :])
        solved[level] = y_level
        if level <= depth:
            child_part = against_rows(y_level, sep_u[:, offset : offset + share])
            child_ids = ids_of(level)
    parent_x = lax.all_gather(outer_solution, "front", axis=1, tiled=True)
    sep_full = jnp.zeros((vector_count, full_rows), jnp.float32)
    for level in range(depth + 1, 0, -1):
        share, offset, inner_pos = geometry(level)
        picked = jnp.take(parent_x, ids_of(level), axis=1)
        rest = solved[level] - times_rows(picked, sep_u[:, offset : offset + share])
        term = times_rows(rest, sep_inv[offset : offset + share, :])
        parent_x = block_sum(term, level)
        sep_full = jnp.where(label_of(level) == group_pos, parent_x, sep_full)
    picked = jnp.take(parent_x, leaf_ids, axis=1)
    rest = leaf_y - times_rows(picked, leaf_u)
    leaf_x = lax.psum_scatter(times_rows(rest, leaf_inv), "front", scatter_dimension=1, tiled=True)
    sep_x = lax.dynamic_slice_in_dim(sep_full, front_pos * local_rows, local_rows, 1)
    return jnp.stack([leaf_x, sep_x])[:, None]


def chain(
    plan, leaf_rhs, sep_rhs, leaf_inverse, sep_inverse, leaf_block, sep_block, pattern, outer
):
    full, rows, rhs, upd, width = plan.full, plan.rows, plan.rhs, plan.upd, plan.width

    def kernel(body, outs, *args, extra=(), **kw):
        return call(functools.partial(body, plan, *extra), outs, args, **kw)

    pack, ids = kernel(
        pack_kernel,
        [(2 * rows, width), ((pattern.shape[0] * pattern.shape[1], upd), jnp.int32)],
        pattern, leaf_rhs, sep_rhs, leaf_inverse, sep_inverse, leaf_block, sep_block, outer,
        chip=False,
    )
    across = exchange(pack, "front", 3)
    beside = exchange(pack, "front", 1)
    beyond = exchange(across, "front", 1)
    wide = 4 * full
    all_part, late_part, high_part, top_s = kernel(
        spread_kernel,
        [
            (rows, wide),
            (rows - plan.share[1], wide),
            (plan.share[3] + plan.share[4], wide),
            (rhs, upd),
        ],
        pack, beside, beyond, across,
        scratch=[pltpu.VMEM((full, width), jnp.float32)],
    )
    all_core = exchange(all_part, "leaf", 1)
    by_x = exchange(late_part, "leaf", 2)
    by_y = exchange(high_part, "leaf", 4)
    by_xy = exchange(high_part, "leaf", 6)
    leaf_all, leaf_ahead, u0 = kernel(
        leaf_kernel,
        [(full, width), (rhs + upd, full), (rhs + 8, 128)],
        pack, beside, beyond, across,
    )
    u0_far = exchange(u0, "leaf", 1)

    def level_of(level, *parts):
        tall = rhs + 3 * upd
        return kernel(
            level_kernel,
            [(upd, 2 * upd), (rhs, upd), (tall, upd), (tall, rows)],
            ids, *parts,
            extra=(level,),
            scratch=[pltpu.VMEM((full, width), jnp.float32)],
        )

    cross1, start1, picks1, columns1 = level_of(1, all_part, all_core)
    (u1,) = kernel(update_kernel, [(rhs + 8, 128)], start1, cross1, u0, u0_far)
    u1_far = exchange(u1, "leaf", 2)
    by_x, by_y, by_xy, u1_far = lax.optimization_barrier((by_x, by_y, by_xy, u1_far))
    by_x_core = exchange(by_x, "leaf", 1)
    by_y_core, by_xy_core = exchange(by_y, "leaf", 1), exchange(by_xy, "leaf", 1)
    cross2, start2, picks2, columns2 = level_of(2, all_part, all_core, by_x, by_x_core)
    (u2,) = kernel(update_kernel, [(rhs + 8, 128)], start2, cross2, u1, u1_far)
    u2_far = exchange(u2, "leaf", 4)
    by_y, _ = lax.optimization_barrier((by_y, u2))
    (base,) = kernel(
        upper_kernel,
        [(rhs + upd, 2 * rows)],
        ids, leaf_all, leaf_ahead, top_s, u0, u0_far, u1, u1_far, u2,
        picks1, picks2, columns1, columns2,
        all_part, all_core, by_x, by_x_core, by_y, by_y_core, by_xy, by_xy_core,
        scratch=[pltpu.VMEM((full, width), jnp.float32)] * 2,
    )
    (out,) = kernel(finish_kernel, [(2, 1, rhs, rows)], base, u2_far)
    return out


def body(*args):
    groups, fronts = lax.axis_size("leaf"), lax.axis_size("front")
    rhs, rows, upd = args[0].shape[1], args[0].shape[2], args[4].shape[1]
    plan = Plan(groups, fronts, rhs, upd, rows)
    if (groups, fronts) == (8, 4) and rows == 64 and rhs == 64 and upd == 32:
        return chain(plan, *args)
    return general(*args)


def solution(mesh):
    placed = (
        P("leaf", None, "front"),
        P("leaf", None, "front"),
        P("leaf", "front", None),
        P("leaf", "front", None),
        P("leaf", None, "front"),
        P("leaf", None, "front"),
        P(),
        P(None, "front"),
    )
    return jax.shard_map(
        body, mesh=mesh, in_specs=placed, out_specs=P(None, "leaf", None, "front"), check_vma=False
    )
```

```python
import functools
import jax
import jax.numpy as jnp
from jax import lax
from jax.experimental import pallas as pl
from jax.experimental.pallas import tpu as pltpu
from jax.sharding import PartitionSpec as P

def halves(value):
    high = value.astype(jnp.bfloat16)
    return high, (value - high.astype(jnp.float32)).astype(jnp.bfloat16)


def product(left, right, side):
    def term(one, two):
        return lax.dot_general(
            one, two, (((1,), (side,)), ((), ())), preferred_element_type=jnp.float32
        )

    (left_high, left_low), (right_high, right_low) = halves(left), halves(right)
    return term(left_high, right_high) + (term(left_high, right_low) + term(left_low, right_high))


def nn(left, right):
    return product(left, right, 0)


def nt(left, right):
    return product(left, right, 1)


def exchange(block, axis, mask):
    count = lax.axis_size(axis)
    return lax.ppermute(block, axis, [(src, src ^ mask) for src in range(count)])


def call(kernel, outs, args, scratch=(), chip=True, cost=1000):
    if chip:
        args = [
            pltpu.with_memory_space_constraint(arg, pltpu.VMEM)
            if arg.ndim == 2
            else arg
            for arg in args
        ]
    return pl.pallas_call(
        kernel,
        out_shape=[
            jax.ShapeDtypeStruct(out, jnp.float32)
            if len(out) == 4
            else pltpu.VMEM(*out)
            if isinstance(out[0], tuple)
            else pltpu.VMEM(out, jnp.float32)
            for out in outs
        ],
        in_specs=[pl.BlockSpec(memory_space=pltpu.VMEM) for _ in args],
        out_specs=[pl.BlockSpec(memory_space=pltpu.VMEM) for _ in outs],
        scratch_shapes=list(scratch),
        compiler_params=pltpu.CompilerParams(vmem_limit_bytes=8 << 20) if chip else None,
        cost_estimate=pl.CostEstimate(flops=cost, bytes_accessed=cost, transcendentals=0),
    )(*args)


class Plan:
    def __init__(self, groups, fronts, rhs, upd, rows):
        self.groups, self.fronts, self.rhs, self.upd, self.rows = groups, fronts, rhs, upd, rows
        self.depth = groups.bit_length() - 1
        self.full = fronts * rows
        self.width = self.full + 128
        self.share, self.offset, self.base, self.blocks = {}, {}, {}, {}
        base = 0
        for level in range(1, self.depth + 2):
            self.blocks[level] = 2 ** min(level, self.depth)
            self.share[level] = rows // self.blocks[level]
            self.offset[level] = rows - (rows >> level - 1)
            self.base[level] = base
            base += fronts * self.share[level]

    def label(self, level, group):
        if level > self.depth:
            return jnp.int32(0)
        return (group // 2**level) * 2**level + 2 ** (level - 1)

    def child_ids(self, level, group, pattern):
        if level == 1:
            kind, labels = 0, (group, group ^ 1)
        elif level > self.depth:
            kind, labels = 1, (self.label(level - 1, group),)
        else:
            kind = 1
            labels = tuple(self.label(level - 1, far) for far in (group, group ^ 2 ** (level - 1)))
        return jnp.concatenate([pattern[pl.ds(kind * self.groups + label, 1), :] for label in labels], axis=1)


def one_hot(ids, count, start=0):
    rows = lax.broadcasted_iota(jnp.int32, (count, ids.shape[1]), 0) + start
    return (rows == ids).astype(jnp.float32)


def own_columns(plan, front, value):
    rows = plan.rows
    result = value[:, :rows]
    for slot in range(1, plan.fronts):
        result = jnp.where(front == slot, value[:, slot * rows : (slot + 1) * rows], result)
    return result


def dense(value):
    count = value.shape[0] // 4
    return jnp.concatenate([value[pos * count : (pos + 1) * count] for pos in range(4)], axis=1)


def undense(value):
    count = value.shape[1] // 4
    return jnp.concatenate([value[:, pos * count : (pos + 1) * count] for pos in range(4)], axis=0)


def place():
    return lax.axis_index("front"), lax.axis_index("leaf")


def pack_kernel(plan, pattern, lr, sr, li, si, lu, su, outer, out, ids):
    full, rhs, upd, rows = plan.full, plan.rhs, plan.upd, plan.rows
    front, _ = place()
    ids[...] = pattern[...].reshape(ids.shape)
    empty = jnp.zeros((upd, rows), jnp.float32)
    out[:rows, :full] = si[0]
    out[:rows, full:] = jnp.concatenate([sr[0], su[0], empty], axis=0).T
    out[rows:, :full] = li[0]
    out[rows:, full:] = jnp.concatenate([lr[0], lu[0], empty], axis=0).T
    out[:rhs, full + rhs + upd :] = nn(outer[...], one_hot(pattern[1, 0:1, :], rows, front * rows))


def fold_rows(plan, rows_of):
    step, full, edge = plan.rows, plan.full, plan.full + plan.rhs + plan.upd
    pieces = [rows_of(front)[:, : (front + 1) * step] for front in (3, 2, 0, 1)]
    pieces += [rows_of(front)[:, full:edge] for front in range(plan.fronts)]
    return jnp.concatenate(pieces, axis=1)


def unfold_rows(plan, folded):
    step, full, edge = plan.rows, plan.full, plan.rhs + plan.upd
    count = folded.shape[0]
    starts = {3: 0, 2: full, 0: full + 3 * step, 1: 2 * full}
    for front in range(plan.fronts):
        wide = (front + 1) * step
        side = 2 * full + 2 * step + front * edge
        pieces = [folded[:, starts[front] : starts[front] + wide]]
        if wide < full:
            pieces.append(jnp.zeros((count, full - wide), jnp.float32))
        pieces.append(folded[:, side : side + edge])
        pieces.append(jnp.zeros((count, plan.width - full - edge), jnp.float32))
        yield front, jnp.concatenate(pieces, axis=1)


def fold_levels(plan, packs, low, levels, natural):
    front, _ = place()
    count, base = natural.shape[0] // plan.fronts, plan.offset[levels[0]]
    for slot, pack in enumerate(packs):
        at = pl.multiple_of((front ^ slot) * count, count)
        natural[pl.ds(at, count), :] = pack[low[slot] : low[slot] + count, :]
    for level in levels:
        offset, share = plan.offset[level] - base, plan.share[level]
        yield offset, fold_rows(
            plan, lambda pos: natural[pos * count + offset : pos * count + offset + share, :]
        )


def spread_kernel(plan, *refs):
    packs = refs[: plan.fronts]
    all_part, late_part, high_part, picked, natural = refs[plan.fronts :]
    edge = plan.full + plan.rhs + plan.upd
    total = packs[0][: plan.rhs, edge:]
    for pack in packs[1:]:
        total = total + pack[: plan.rhs, edge:]
    picked[...] = total
    levels = range(1, plan.depth + 2)
    for at, piece in fold_levels(plan, packs, [0] * 4, levels, natural):
        for out, level in ((all_part, 1), (late_part, 2), (high_part, 3)):
            low = at - plan.offset[level]
            if low >= 0:
                out[low : low + piece.shape[0], :] = piece


def far_kernel(plan, high, all_core, out):
    count = high.shape[0]
    out[:count, :] = high[...]
    out[count:, :] = all_core[plan.offset[3] :, :]


def leaf_kernel(plan, *refs):
    count = plan.fronts
    packs, (whole, ahead, update) = refs[:count], refs[count:]
    front, _ = place()
    rhs, upd, full, rows = plan.rhs, plan.upd, plan.full, plan.rows
    low = rows
    for slot in range(count):
        at = pl.multiple_of((front ^ slot) * rows, rows)
        whole[pl.ds(at, rows), :] = packs[slot][low : low + rows, :]
    flipped = whole[:, full:].T
    solved = nt(flipped[:rhs], whole[:, :full])
    ahead[:rhs, :] = solved
    ahead[rhs:, :] = flipped[rhs : rhs + upd]
    update[...] = dense(nt(solved, flipped[rhs : rhs + upd]))


def assemble(plan, level, parts, whole):
    blocks, share = plan.blocks[level], plan.share[level]
    _, group = place()
    for ref, first, slot in parts:
        inner = (group & (blocks - 1)) ^ slot
        for front, piece in unfold_rows(plan, ref[first : first + share, :]):
            dest = pl.multiple_of(front * plan.rows + inner * share, share)
            whole[pl.ds(dest, share), :] = piece


def upper_parts(plan, level, refs):
    own, own_core, by_x, by_x_core, far, far_core = refs
    _, group = place()
    at = plan.offset[level] - plan.offset[3]
    late = at + plan.share[2]
    half = plan.share[3] + plan.share[4]
    parts = [(own, plan.offset[level], 0), (own_core, plan.offset[level], 1)]
    parts += [(by_x, late, 2), (by_x_core, late, 3)]
    side = 4 + 2 * (group & 1)
    parts += [(far, at, side), (far, half + at, side ^ 1)]
    return parts + [(far_core, at, side ^ 3), (far_core, half + at, side ^ 2)]


def lead_level(plan, level, pattern, parts, whole):
    assemble(plan, level, parts, whole)
    flipped = whole[:, plan.full :].T
    right, block = flipped[: plan.rhs], flipped[plan.rhs : plan.rhs + plan.upd]
    fold = nn(block, whole[:, : plan.full])
    hot = one_hot(plan.child_ids(level, place()[1], pattern), plan.full)
    return nn(fold, hot), nt(right, fold)


def back_level(plan, level, pattern, whole):
    front, group = place()
    rhs = plan.rhs
    hot = one_hot(plan.child_ids(level, group, pattern), plan.full)
    matrix = whole[:, : plan.full]
    flipped = whole[:, plan.full :].T
    right, block = flipped[:rhs], flipped[rhs : rhs + plan.upd]
    ahead = nt(jnp.concatenate([right, hot.T], axis=0), matrix)
    stacked = jnp.concatenate([ahead, block], axis=0)
    result = [nt(stacked, ahead[rhs : rhs + plan.upd]), nn(stacked, own_columns(plan, front, matrix))]
    if level > plan.depth:
        return result
    return [nt(block, ahead[rhs:]), nt(ahead[:rhs], block)] + result


def lead_kernel(plan, level, pattern, *refs):
    blocks = plan.blocks[level]
    parts = [
        (ref, plan.offset[level] if slot < 2 else 0, slot) for slot, ref in enumerate(refs[:blocks])
    ]
    whole, cross, start = refs[blocks:]
    cross[...], start[...] = lead_level(plan, level, pattern, parts, whole)


def lower_kernel(plan, pattern, whole, leaf_all, leaf_ahead, near, far, own_part, leaf_part):
    rhs, upd = plan.rhs, plan.upd
    known = jnp.concatenate([undense(near[...]), undense(far[...])], axis=1)
    _, _, picks, columns = back_level(plan, 1, pattern, whole)
    leaf_back = nn(leaf_ahead[...], own_columns(plan, place()[0], leaf_all[:, : plan.full]))
    both = jnp.concatenate([columns, picks], axis=1)
    base = both[:rhs] - nn(known, both[rhs : rhs + 2 * upd])
    slope = both[rhs + 2 * upd :]
    own_part[:rhs] = base[:, : plan.rows]
    own_part[rhs : rhs + 2 * upd] = jnp.zeros((2 * upd, plan.rows), jnp.float32)
    own_part[rhs + 2 * upd :] = slope[:, : plan.rows]
    through = jnp.concatenate([base[:, plan.rows :], -slope[:, plan.rows :]], axis=0)
    through = nn(through, leaf_back[rhs:])
    leaf_part[:rhs] = leaf_back[:rhs] - through[:rhs]
    leaf_part[rhs:] = through[rhs:]


def upper_kernel(plan, pattern, leaf_part, top_s, *refs):
    rhs, upd, group = plan.rhs, plan.upd, place()[1]
    known = jnp.concatenate([undense(refs[0][...]), undense(refs[1][...])], axis=1)
    near = undense(refs[2][...])
    picks, columns = {}, {1: refs[3][...]}
    sources, (out, whole3, whole4) = refs[5:11], refs[11:]
    assemble(plan, 3, upper_parts(plan, 3, sources), whole3)
    assemble(plan, 4, upper_parts(plan, 4, sources), whole4)
    cross, start, picks[3], columns[3] = back_level(plan, 3, pattern, whole3)
    picks[4], columns[4] = back_level(plan, 4, pattern, whole4)
    _, _, picks[2], columns[2] = back_level(plan, 2, pattern, refs[4])
    none = jnp.zeros((upd, upd), jnp.float32)
    unit = one_hot(lax.broadcasted_iota(jnp.int32, (1, upd), 1), upd)

    def step(terms, part):
        known = jnp.concatenate([part[:rhs], jnp.zeros((upd, part.shape[1]), jnp.float32)], axis=0)
        return known - nn(jnp.concatenate(terms, axis=1), part[rhs:])

    gap = jnp.zeros((rhs, upd), jnp.float32)
    both = jnp.concatenate(
        [jnp.concatenate([near, gap], axis=1), jnp.concatenate([none, unit], axis=1)], axis=0
    )
    u3 = jnp.concatenate([start, none], axis=0) - nt(both, cross)
    fixed = jnp.concatenate([known, jnp.zeros((upd, 2 * upd), jnp.float32)], axis=0)
    terms = {4: [u3, jnp.concatenate([top_s[...], none], axis=0)]}
    terms[3] = [both, step(terms[4], picks[4])]
    terms[2] = [fixed, step(terms[3], picks[3])]
    last = step(terms[2], picks[2])
    terms[1] = [jnp.zeros((rhs + upd, 2 * upd), jnp.float32), last]
    leaf_out = step([last], leaf_part)
    gap = jnp.zeros((rhs + upd, upd), jnp.float32)
    chosen = jnp.concatenate([columns[4][: rhs + upd], none_wide(plan), columns[4][rhs + upd :]], axis=0)
    weight = jnp.concatenate([terms[4][0], gap, terms[4][1]], axis=1)
    for level in (3, 2, 1):
        here = plan.label(level, group) == group
        chosen = jnp.where(here, columns[level], chosen)
        weight = jnp.where(here, jnp.concatenate(terms[level], axis=1), weight)
    out[...] = jnp.concatenate([leaf_out, step([weight], chosen)], axis=1)


def none_wide(plan):
    return jnp.zeros((plan.upd, plan.rows), jnp.float32)


def finish_kernel(plan, base, far, out):
    rhs, upd, rows = plan.rhs, plan.upd, plan.rows
    total = base[:rhs] + nn(undense(far[...]), base[rhs:])
    out[0, 0] = total[:, :rows]
    out[1, 0] = total[:, rows:]


def update_kernel(plan, start, cross, mine, other, out):
    both = jnp.concatenate([undense(mine[...]), undense(other[...])], axis=1)
    out[...] = dense(start[...] - nt(both, cross[...]))


def partner(block, axis, distance):
    count = lax.axis_size(axis)
    route = []
    for low in range(count):
        high = low | 1 << distance
        if high != low and high < count:
            route += [(low, high), (high, low)]
    return lax.ppermute(block, axis, route)


def times_rows(vectors, matrix):
    return jnp.dot(
        vectors, matrix, precision=lax.Precision.HIGHEST, preferred_element_type=jnp.float32
    )


def against_rows(vectors, matrix):
    return lax.dot_general(
        vectors,
        matrix,
        (((1,), (1,)), ((), ())),
        precision=lax.Precision.HIGHEST,
        preferred_element_type=jnp.float32,
    )


def general(
    leaf_rhs, sep_rhs, leaf_inverse, sep_inverse, leaf_block, sep_block, pattern, outer_solution
):
    group_count = lax.axis_size("leaf")
    depth = group_count.bit_length() - 1
    group_pos = lax.axis_index("leaf")
    front_pos = lax.axis_index("front")
    local_rows = leaf_rhs.shape[-1]
    full_rows = leaf_inverse.shape[-1]
    vector_count = leaf_rhs.shape[1]
    leaf_r = leaf_rhs[0]
    leaf_inv = leaf_inverse[0]
    leaf_u = leaf_block[0]
    sep_r = sep_rhs[0]
    sep_inv = sep_inverse[0]
    sep_u = sep_block[0]
    all_rows = jnp.arange(full_rows, dtype=jnp.int32)

    def geometry(level):
        blocks = 2 ** min(level, depth)
        share = local_rows // blocks
        offset = local_rows - (local_rows >> level - 1)
        return (share, offset, group_pos % blocks)

    def label_of(level):
        if level > depth:
            return jnp.int32(0)
        return group_pos // 2**level * 2**level + 2 ** (level - 1)

    def ids_of(level):
        return lax.dynamic_index_in_dim(pattern[1], label_of(level), 0, keepdims=False)

    def block_sum(term, level):
        nbits = min(level, depth)
        if nbits == depth:
            return lax.psum(term, ("leaf", "front"))
        piece = lax.psum_scatter(term, "front", scatter_dimension=1, tiled=True)
        for bit in range(nbits):
            piece = piece + partner(piece, "leaf", bit)
        return lax.all_gather(piece, "front", axis=1, tiled=True)

    leaf_y = against_rows(lax.all_gather(leaf_r, "front", axis=1, tiled=True), leaf_inv)
    leaf_ids = lax.dynamic_index_in_dim(pattern[0], group_pos, 0, keepdims=False)
    child_part = against_rows(leaf_y, leaf_u)
    child_ids = leaf_ids
    solved = {}
    for level in range(1, depth + 2):
        share, offset, inner_pos = geometry(level)
        own_r = sep_r[:, offset : offset + share]
        start_col = front_pos * local_rows + inner_pos * share
        contribution = jnp.zeros((vector_count, full_rows), jnp.float32)
        contribution = lax.dynamic_update_slice(contribution, own_r, (jnp.int32(0), start_col))
        selector = (child_ids[:, None] == all_rows[None, :]).astype(jnp.float32)
        contribution = contribution - times_rows(child_part, selector)
        whole_v = block_sum(contribution, level)
        y_level = against_rows(whole_v, sep_inv[offset : offset + share, :])
        solved[level] = y_level
        if level <= depth:
            child_part = against_rows(y_level, sep_u[:, offset : offset + share])
            child_ids = ids_of(level)
    parent_x = lax.all_gather(outer_solution, "front", axis=1, tiled=True)
    sep_full = jnp.zeros((vector_count, full_rows), jnp.float32)
    for level in range(depth + 1, 0, -1):
        share, offset, inner_pos = geometry(level)
        picked = jnp.take(parent_x, ids_of(level), axis=1)
        rest = solved[level] - times_rows(picked, sep_u[:, offset : offset + share])
        term = times_rows(rest, sep_inv[offset : offset + share, :])
        parent_x = block_sum(term, level)
        sep_full = jnp.where(label_of(level) == group_pos, parent_x, sep_full)
    picked = jnp.take(parent_x, leaf_ids, axis=1)
    rest = leaf_y - times_rows(picked, leaf_u)
    leaf_x = lax.psum_scatter(times_rows(rest, leaf_inv), "front", scatter_dimension=1, tiled=True)
    sep_x = lax.dynamic_slice_in_dim(sep_full, front_pos * local_rows, local_rows, 1)
    return jnp.stack([leaf_x, sep_x])[:, None]


def chain(
    plan, leaf_rhs, sep_rhs, leaf_inverse, sep_inverse, leaf_block, sep_block, pattern, outer
):
    full, rows, rhs, upd, width = plan.full, plan.rows, plan.rhs, plan.upd, plan.width

    def kernel(body, outs, *args, extra=(), **kw):
        return call(functools.partial(body, plan, *extra), outs, args, **kw)

    pack, ids = kernel(
        pack_kernel,
        [(2 * rows, width), ((pattern.shape[0] * pattern.shape[1], upd), jnp.int32)],
        pattern, leaf_rhs, sep_rhs, leaf_inverse, sep_inverse, leaf_block, sep_block, outer,
        chip=False,
    )
    across = exchange(pack, "front", 3)
    beside = exchange(pack, "front", 1)
    beyond = exchange(across, "front", 1)
    wide = 4 * full
    all_part, late_part, high_part, top_s = kernel(
        spread_kernel,
        [
            (rows, wide),
            (rows - plan.share[1], wide),
            (plan.share[3] + plan.share[4], wide),
            (rhs, upd),
        ],
        pack, beside, beyond, across,
        scratch=[pltpu.VMEM((full, width), jnp.float32)],
    )
    all_core = exchange(all_part, "leaf", 1)
    by_x = exchange(late_part, "leaf", 2)
    leaf_beyond, _ = lax.optimization_barrier((beyond, top_s))
    leaf_all, leaf_ahead, u0 = kernel(
        leaf_kernel,
        [(full, width), (rhs + upd, full), (rhs // 4, 4 * upd)],
        pack, beside, leaf_beyond, across,
    )
    u0_far = exchange(u0, "leaf", 1)
    high_part, _ = lax.optimization_barrier((high_part, u0))
    (far_part,) = kernel(far_kernel, [(2 * high_part.shape[0], wide)], high_part, all_core)
    far = lax.ppermute(far_part, "leaf", [(src, src ^ (6 if src % 2 else 4)) for src in range(plan.groups)])
    def lead_of(level, *parts):
        return kernel(
            lead_kernel,
            [(full, width), (upd, 2 * upd), (rhs, upd)],
            ids, *parts,
            extra=(level,),
        )

    whole1, cross1, start1 = lead_of(1, all_part, all_core)
    (u1,) = kernel(update_kernel, [(rhs // 4, 4 * upd)], start1, cross1, u0, u0_far)
    u1_far = exchange(u1, "leaf", 2)

    whole1, _ = lax.optimization_barrier((whole1, u1))
    own_part, leaf_part = kernel(
        lower_kernel,
        [(rhs + 3 * upd, rows), (rhs + upd, rows)],
        ids, whole1, leaf_all, leaf_ahead, u0, u0_far,
    )
    by_x, far, u1_far, own_part = lax.optimization_barrier((by_x, far, u1_far, own_part))
    by_x_core = exchange(by_x, "leaf", 1)
    far_core = exchange(far, "leaf", 1)
    whole2, cross2, start2 = lead_of(2, all_part, all_core, by_x, by_x_core)
    (u2,) = kernel(
        update_kernel, [(rhs // 4, 4 * upd)], start2, cross2, u1, u1_far
    )
    u2_far = exchange(u2, "leaf", 4)
    (base,) = kernel(
        upper_kernel,
        [(rhs + upd, 2 * rows)],
        ids, leaf_part, top_s, u1, u1_far, u2, own_part, whole2,
        all_part, all_core, by_x, by_x_core, far, far_core,
        scratch=[pltpu.VMEM((full, width), jnp.float32)] * 2,
    )
    (out,) = kernel(finish_kernel, [(2, 1, rhs, rows)], base, u2_far)
    return out


def body(*args):
    groups, fronts = lax.axis_size("leaf"), lax.axis_size("front")
    rhs, rows, upd = args[0].shape[1], args[0].shape[2], args[4].shape[1]
    plan = Plan(groups, fronts, rhs, upd, rows)
    if (groups, fronts) == (8, 4) and rows == 64 and rhs == 64 and upd == 32:
        return chain(plan, *args)
    return general(*args)


def solution(mesh):
    placed = (
        P("leaf", None, "front"),
        P("leaf", None, "front"),
        P("leaf", "front", None),
        P("leaf", "front", None),
        P("leaf", None, "front"),
        P("leaf", None, "front"),
        P(),
        P(None, "front"),
    )
    return jax.shard_map(
        body, mesh=mesh, in_specs=placed, out_specs=P(None, "leaf", None, "front"), check_vma=False
    )
```

```python
import functools
import jax
import jax.numpy as jnp
from jax import lax
from jax.experimental import pallas as pl
from jax.experimental.pallas import tpu as pltpu
from jax.sharding import PartitionSpec as P

def halves(value):
    high = value.astype(jnp.bfloat16)
    return high, (value - high.astype(jnp.float32)).astype(jnp.bfloat16)


def product(left, right, side):
    def term(one, two):
        return lax.dot_general(
            one, two, (((1,), (side,)), ((), ())), preferred_element_type=jnp.float32
        )

    (left_high, left_low), (right_high, right_low) = halves(left), halves(right)
    return term(left_high, right_high) + (term(left_high, right_low) + term(left_low, right_high))


def nn(left, right):
    return product(left, right, 0)


def nt(left, right):
    return product(left, right, 1)


def exchange(block, axis, mask):
    count = lax.axis_size(axis)
    return lax.ppermute(block, axis, [(src, src ^ mask) for src in range(count)])


def call(kernel, outs, args, scratch=(), chip=True, cost=1000):
    if chip:
        args = [
            pltpu.with_memory_space_constraint(arg, pltpu.VMEM)
            if arg.ndim == 2
            else arg
            for arg in args
        ]
    return pl.pallas_call(
        kernel,
        out_shape=[
            jax.ShapeDtypeStruct(out, jnp.float32)
            if len(out) == 4
            else pltpu.VMEM(*out)
            if isinstance(out[0], tuple)
            else pltpu.VMEM(out, jnp.float32)
            for out in outs
        ],
        in_specs=[pl.BlockSpec(memory_space=pltpu.VMEM) for _ in args],
        out_specs=[pl.BlockSpec(memory_space=pltpu.VMEM) for _ in outs],
        scratch_shapes=list(scratch),
        compiler_params=pltpu.CompilerParams(vmem_limit_bytes=8 << 20) if chip else None,
        cost_estimate=pl.CostEstimate(flops=cost, bytes_accessed=cost, transcendentals=0),
    )(*args)


class Plan:
    def __init__(self, groups, fronts, rhs, upd, rows):
        self.groups, self.fronts, self.rhs, self.upd, self.rows = groups, fronts, rhs, upd, rows
        self.depth = groups.bit_length() - 1
        self.full = fronts * rows
        self.width = self.full + 128
        self.share, self.offset, self.base, self.blocks = {}, {}, {}, {}
        base = 0
        for level in range(1, self.depth + 2):
            self.blocks[level] = 2 ** min(level, self.depth)
            self.share[level] = rows // self.blocks[level]
            self.offset[level] = rows - (rows >> level - 1)
            self.base[level] = base
            base += fronts * self.share[level]

    def label(self, level, group):
        if level > self.depth:
            return jnp.int32(0)
        return (group // 2**level) * 2**level + 2 ** (level - 1)

    def child_ids(self, level, group, pattern):
        if level == 1:
            kind, labels = 0, (group, group ^ 1)
        elif level > self.depth:
            kind, labels = 1, (self.label(level - 1, group),)
        else:
            kind = 1
            labels = tuple(self.label(level - 1, far) for far in (group, group ^ 2 ** (level - 1)))
        return jnp.concatenate([pattern[pl.ds(kind * self.groups + label, 1), :] for label in labels], axis=1)


def one_hot(ids, count, start=0):
    rows = lax.broadcasted_iota(jnp.int32, (count, ids.shape[1]), 0) + start
    return (rows == ids).astype(jnp.float32)


def own_columns(plan, front, value):
    rows = plan.rows
    result = value[:, :rows]
    for slot in range(1, plan.fronts):
        result = jnp.where(front == slot, value[:, slot * rows : (slot + 1) * rows], result)
    return result


def dense(value):
    count = value.shape[0] // 4
    return jnp.concatenate([value[pos * count : (pos + 1) * count] for pos in range(4)], axis=1)


def undense(value):
    count = value.shape[1] // 4
    return jnp.concatenate([value[:, pos * count : (pos + 1) * count] for pos in range(4)], axis=0)


def place():
    return lax.axis_index("front"), lax.axis_index("leaf")


def pack_kernel(plan, pattern, lr, sr, li, si, lu, su, outer, out, ids):
    full, rows, half = plan.full, plan.rows, plan.rhs // 2
    ids[...] = pattern[...].reshape(ids.shape)
    out[:rows, :full] = si[0]
    out[:rows, full:] = jnp.concatenate([sr[0], su[0], outer[:half]], axis=0).T
    out[rows:, :full] = li[0]
    out[rows:, full:] = jnp.concatenate([lr[0], lu[0], outer[half:]], axis=0).T


def outer_kernel(plan, pattern, *refs):
    packs, (picked, natural) = refs[: plan.fronts], refs[plan.fronts :]
    front, _ = place()
    rows, full, edge = plan.rows, plan.full, plan.rhs + plan.upd
    for slot, pack in enumerate(packs):
        at = pl.multiple_of((front ^ slot) * rows, rows)
        natural[pl.ds(at, rows), :128] = pack[:rows, full:]
        natural[pl.ds(at, rows), 128:] = pack[rows:, full:]
    turned = natural[...].T
    outer = jnp.concatenate([turned[edge:128], turned[128 + edge :]], axis=0)
    picked[...] = nn(outer, one_hot(pattern[plan.groups : plan.groups + 1, :], full))


def fold_rows(plan, rows_of):
    step, full, edge = plan.rows, plan.full, plan.full + plan.rhs + plan.upd
    pieces = [rows_of(front)[:, : (front + 1) * step] for front in (3, 2, 0, 1)]
    pieces += [rows_of(front)[:, full:edge] for front in range(plan.fronts)]
    return jnp.concatenate(pieces, axis=1)


def unfold_rows(plan, folded):
    step, full, edge = plan.rows, plan.full, plan.rhs + plan.upd
    count = folded.shape[0]
    starts = {3: 0, 2: full, 0: full + 3 * step, 1: 2 * full}
    for front in range(plan.fronts):
        wide = (front + 1) * step
        side = 2 * full + 2 * step + front * edge
        pieces = [folded[:, starts[front] : starts[front] + wide]]
        if wide < full:
            pieces.append(jnp.zeros((count, full - wide), jnp.float32))
        pieces.append(folded[:, side : side + edge])
        pieces.append(jnp.zeros((count, plan.width - full - edge), jnp.float32))
        yield front, jnp.concatenate(pieces, axis=1)


def fold_levels(plan, packs, low, levels, natural):
    front, _ = place()
    count, base = natural.shape[0] // plan.fronts, plan.offset[levels[0]]
    for slot, pack in enumerate(packs):
        at = pl.multiple_of((front ^ slot) * count, count)
        natural[pl.ds(at, count), :] = pack[low[slot] : low[slot] + count, :]
    for level in levels:
        offset, share = plan.offset[level] - base, plan.share[level]
        yield offset, fold_rows(
            plan, lambda pos: natural[pos * count + offset : pos * count + offset + share, :]
        )


def spread_kernel(plan, *refs):
    packs = refs[: plan.fronts]
    all_part, late_part, high_part, natural = refs[plan.fronts :]
    levels = range(1, plan.depth + 2)
    for at, piece in fold_levels(plan, packs, [0] * 4, levels, natural):
        for out, level in ((all_part, 1), (late_part, 2), (high_part, 3)):
            low = at - plan.offset[level]
            if low >= 0:
                out[low : low + piece.shape[0], :] = piece


def far_kernel(plan, high, all_core, out):
    count = high.shape[0]
    out[:count, :] = high[...]
    out[count:, :] = all_core[plan.offset[3] :, :]


def leaf_kernel(plan, *refs):
    count = plan.fronts
    packs, (whole, ahead, update) = refs[:count], refs[count:]
    front, _ = place()
    rhs, upd, full, rows = plan.rhs, plan.upd, plan.full, plan.rows
    low = rows
    for slot in range(count):
        at = pl.multiple_of((front ^ slot) * rows, rows)
        whole[pl.ds(at, rows), :] = packs[slot][low : low + rows, :]
    flipped = whole[:, full:].T
    solved = nt(flipped[:rhs], whole[:, :full])
    ahead[:rhs, :] = solved
    ahead[rhs:, :] = flipped[rhs : rhs + upd]
    update[...] = dense(nt(solved, flipped[rhs : rhs + upd]))


def assemble(plan, level, parts, whole):
    blocks, share = plan.blocks[level], plan.share[level]
    _, group = place()
    for ref, first, slot in parts:
        inner = (group & (blocks - 1)) ^ slot
        for front, piece in unfold_rows(plan, ref[first : first + share, :]):
            dest = pl.multiple_of(front * plan.rows + inner * share, share)
            whole[pl.ds(dest, share), :] = piece


def upper_parts(plan, level, refs):
    own, own_core, by_x, by_x_core, far, far_core = refs
    _, group = place()
    at = plan.offset[level] - plan.offset[3]
    late = at + plan.share[2]
    half = plan.share[3] + plan.share[4]
    parts = [(own, plan.offset[level], 0), (own_core, plan.offset[level], 1)]
    parts += [(by_x, late, 2), (by_x_core, late, 3)]
    side = 4 + 2 * (group & 1)
    parts += [(far, at, side), (far, half + at, side ^ 1)]
    return parts + [(far_core, at, side ^ 3), (far_core, half + at, side ^ 2)]


def lead_level(plan, level, pattern, parts, whole):
    assemble(plan, level, parts, whole)
    flipped = whole[:, plan.full :].T
    right, block = flipped[: plan.rhs], flipped[plan.rhs : plan.rhs + plan.upd]
    fold = nn(block, whole[:, : plan.full])
    hot = one_hot(plan.child_ids(level, place()[1], pattern), plan.full)
    return nn(fold, hot), nt(right, fold)


def back_level(plan, level, pattern, whole):
    front, group = place()
    rhs = plan.rhs
    hot = one_hot(plan.child_ids(level, group, pattern), plan.full)
    matrix = whole[:, : plan.full]
    flipped = whole[:, plan.full :].T
    right, block = flipped[:rhs], flipped[rhs : rhs + plan.upd]
    ahead = nt(jnp.concatenate([right, hot.T], axis=0), matrix)
    stacked = jnp.concatenate([ahead, block], axis=0)
    result = [nt(stacked, ahead[rhs : rhs + plan.upd]), nn(stacked, own_columns(plan, front, matrix))]
    if level > plan.depth:
        return result
    return [nt(block, ahead[rhs:]), nt(ahead[:rhs], block)] + result


def lead_kernel(plan, level, pattern, *refs):
    blocks = plan.blocks[level]
    parts = [
        (ref, plan.offset[level] if slot < 2 else 0, slot) for slot, ref in enumerate(refs[:blocks])
    ]
    whole, cross, start = refs[blocks:]
    cross[...], start[...] = lead_level(plan, level, pattern, parts, whole)


def lower_kernel(plan, pattern, whole, leaf_all, leaf_ahead, near, far, own_part, leaf_part):
    rhs, upd = plan.rhs, plan.upd
    known = jnp.concatenate([undense(near[...]), undense(far[...])], axis=1)
    _, _, picks, columns = back_level(plan, 1, pattern, whole)
    leaf_back = nn(leaf_ahead[...], own_columns(plan, place()[0], leaf_all[:, : plan.full]))
    both = jnp.concatenate([columns, picks], axis=1)
    base = both[:rhs] - nn(known, both[rhs : rhs + 2 * upd])
    slope = both[rhs + 2 * upd :]
    own_part[:rhs] = base[:, : plan.rows]
    own_part[rhs : rhs + 2 * upd] = jnp.zeros((2 * upd, plan.rows), jnp.float32)
    own_part[rhs + 2 * upd :] = slope[:, : plan.rows]
    through = jnp.concatenate([base[:, plan.rows :], -slope[:, plan.rows :]], axis=0)
    through = nn(through, leaf_back[rhs:])
    leaf_part[:rhs] = leaf_back[:rhs] - through[:rhs]
    leaf_part[rhs:] = through[rhs:]


def upper_kernel(plan, pattern, leaf_part, top_s, *refs):
    rhs, upd, group = plan.rhs, plan.upd, place()[1]
    known = jnp.concatenate([undense(refs[0][...]), undense(refs[1][...])], axis=1)
    near = undense(refs[2][...])
    picks, columns = {}, {1: refs[3][...]}
    sources, (out, whole3, whole4) = refs[5:11], refs[11:]
    assemble(plan, 3, upper_parts(plan, 3, sources), whole3)
    assemble(plan, 4, upper_parts(plan, 4, sources), whole4)
    cross, start, picks[3], columns[3] = back_level(plan, 3, pattern, whole3)
    picks[4], columns[4] = back_level(plan, 4, pattern, whole4)
    _, _, picks[2], columns[2] = back_level(plan, 2, pattern, refs[4])
    none = jnp.zeros((upd, upd), jnp.float32)
    unit = one_hot(lax.broadcasted_iota(jnp.int32, (1, upd), 1), upd)

    def step(terms, part):
        known = jnp.concatenate([part[:rhs], jnp.zeros((upd, part.shape[1]), jnp.float32)], axis=0)
        return known - nn(jnp.concatenate(terms, axis=1), part[rhs:])

    gap = jnp.zeros((rhs, upd), jnp.float32)
    both = jnp.concatenate(
        [jnp.concatenate([near, gap], axis=1), jnp.concatenate([none, unit], axis=1)], axis=0
    )
    u3 = jnp.concatenate([start, none], axis=0) - nt(both, cross)
    fixed = jnp.concatenate([known, jnp.zeros((upd, 2 * upd), jnp.float32)], axis=0)
    terms = {4: [u3, jnp.concatenate([top_s[...], none], axis=0)]}
    terms[3] = [both, step(terms[4], picks[4])]
    terms[2] = [fixed, step(terms[3], picks[3])]
    last = step(terms[2], picks[2])
    terms[1] = [jnp.zeros((rhs + upd, 2 * upd), jnp.float32), last]
    leaf_out = step([last], leaf_part)
    gap = jnp.zeros((rhs + upd, upd), jnp.float32)
    chosen = jnp.concatenate([columns[4][: rhs + upd], none_wide(plan), columns[4][rhs + upd :]], axis=0)
    weight = jnp.concatenate([terms[4][0], gap, terms[4][1]], axis=1)
    for level in (3, 2, 1):
        here = plan.label(level, group) == group
        chosen = jnp.where(here, columns[level], chosen)
        weight = jnp.where(here, jnp.concatenate(terms[level], axis=1), weight)
    out[...] = jnp.concatenate([leaf_out, step([weight], chosen)], axis=1)


def none_wide(plan):
    return jnp.zeros((plan.upd, plan.rows), jnp.float32)


def finish_kernel(plan, base, far, out):
    rhs, upd, rows = plan.rhs, plan.upd, plan.rows
    total = base[:rhs] + nn(undense(far[...]), base[rhs:])
    out[0, 0] = total[:, :rows]
    out[1, 0] = total[:, rows:]


def update_kernel(plan, start, cross, mine, other, out):
    both = jnp.concatenate([undense(mine[...]), undense(other[...])], axis=1)
    out[...] = dense(start[...] - nt(both, cross[...]))


def partner(block, axis, distance):
    count = lax.axis_size(axis)
    route = []
    for low in range(count):
        high = low | 1 << distance
        if high != low and high < count:
            route += [(low, high), (high, low)]
    return lax.ppermute(block, axis, route)


def times_rows(vectors, matrix):
    return jnp.dot(
        vectors, matrix, precision=lax.Precision.HIGHEST, preferred_element_type=jnp.float32
    )


def against_rows(vectors, matrix):
    return lax.dot_general(
        vectors,
        matrix,
        (((1,), (1,)), ((), ())),
        precision=lax.Precision.HIGHEST,
        preferred_element_type=jnp.float32,
    )


def general(
    leaf_rhs, sep_rhs, leaf_inverse, sep_inverse, leaf_block, sep_block, pattern, outer_solution
):
    group_count = lax.axis_size("leaf")
    depth = group_count.bit_length() - 1
    group_pos = lax.axis_index("leaf")
    front_pos = lax.axis_index("front")
    local_rows = leaf_rhs.shape[-1]
    full_rows = leaf_inverse.shape[-1]
    vector_count = leaf_rhs.shape[1]
    leaf_r = leaf_rhs[0]
    leaf_inv = leaf_inverse[0]
    leaf_u = leaf_block[0]
    sep_r = sep_rhs[0]
    sep_inv = sep_inverse[0]
    sep_u = sep_block[0]
    all_rows = jnp.arange(full_rows, dtype=jnp.int32)

    def geometry(level):
        blocks = 2 ** min(level, depth)
        share = local_rows // blocks
        offset = local_rows - (local_rows >> level - 1)
        return (share, offset, group_pos % blocks)

    def label_of(level):
        if level > depth:
            return jnp.int32(0)
        return group_pos // 2**level * 2**level + 2 ** (level - 1)

    def ids_of(level):
        return lax.dynamic_index_in_dim(pattern[1], label_of(level), 0, keepdims=False)

    def block_sum(term, level):
        nbits = min(level, depth)
        if nbits == depth:
            return lax.psum(term, ("leaf", "front"))
        piece = lax.psum_scatter(term, "front", scatter_dimension=1, tiled=True)
        for bit in range(nbits):
            piece = piece + partner(piece, "leaf", bit)
        return lax.all_gather(piece, "front", axis=1, tiled=True)

    leaf_y = against_rows(lax.all_gather(leaf_r, "front", axis=1, tiled=True), leaf_inv)
    leaf_ids = lax.dynamic_index_in_dim(pattern[0], group_pos, 0, keepdims=False)
    child_part = against_rows(leaf_y, leaf_u)
    child_ids = leaf_ids
    solved = {}
    for level in range(1, depth + 2):
        share, offset, inner_pos = geometry(level)
        own_r = sep_r[:, offset : offset + share]
        start_col = front_pos * local_rows + inner_pos * share
        contribution = jnp.zeros((vector_count, full_rows), jnp.float32)
        contribution = lax.dynamic_update_slice(contribution, own_r, (jnp.int32(0), start_col))
        selector = (child_ids[:, None] == all_rows[None, :]).astype(jnp.float32)
        contribution = contribution - times_rows(child_part, selector)
        whole_v = block_sum(contribution, level)
        y_level = against_rows(whole_v, sep_inv[offset : offset + share, :])
        solved[level] = y_level
        if level <= depth:
            child_part = against_rows(y_level, sep_u[:, offset : offset + share])
            child_ids = ids_of(level)
    parent_x = lax.all_gather(outer_solution, "front", axis=1, tiled=True)
    sep_full = jnp.zeros((vector_count, full_rows), jnp.float32)
    for level in range(depth + 1, 0, -1):
        share, offset, inner_pos = geometry(level)
        picked = jnp.take(parent_x, ids_of(level), axis=1)
        rest = solved[level] - times_rows(picked, sep_u[:, offset : offset + share])
        term = times_rows(rest, sep_inv[offset : offset + share, :])
        parent_x = block_sum(term, level)
        sep_full = jnp.where(label_of(level) == group_pos, parent_x, sep_full)
    picked = jnp.take(parent_x, leaf_ids, axis=1)
    rest = leaf_y - times_rows(picked, leaf_u)
    leaf_x = lax.psum_scatter(times_rows(rest, leaf_inv), "front", scatter_dimension=1, tiled=True)
    sep_x = lax.dynamic_slice_in_dim(sep_full, front_pos * local_rows, local_rows, 1)
    return jnp.stack([leaf_x, sep_x])[:, None]


def chain(
    plan, leaf_rhs, sep_rhs, leaf_inverse, sep_inverse, leaf_block, sep_block, pattern, outer
):
    full, rows, rhs, upd, width = plan.full, plan.rows, plan.rhs, plan.upd, plan.width

    def kernel(body, outs, *args, extra=(), **kw):
        return call(functools.partial(body, plan, *extra), outs, args, **kw)

    pack, ids = kernel(
        pack_kernel,
        [(2 * rows, width), ((pattern.shape[0] * pattern.shape[1], upd), jnp.int32)],
        pattern, leaf_rhs, sep_rhs, leaf_inverse, sep_inverse, leaf_block, sep_block, outer,
        chip=False,
    )
    across = exchange(pack, "front", 3)
    beside = exchange(pack, "front", 1)
    beyond = exchange(across, "front", 1)
    wide = 4 * full
    all_part, late_part, high_part = kernel(
        spread_kernel,
        [
            (rows, wide),
            (rows - plan.share[1], wide),
            (plan.share[3] + plan.share[4], wide),
        ],
        pack, beside, beyond, across,
        scratch=[pltpu.VMEM((full, width), jnp.float32)],
    )
    all_core = exchange(all_part, "leaf", 1)
    by_x = exchange(late_part, "leaf", 2)
    leaf_beyond, _ = lax.optimization_barrier((beyond, all_part))
    leaf_all, leaf_ahead, u0 = kernel(
        leaf_kernel,
        [(full, width), (rhs + upd, full), (rhs // 4, 4 * upd)],
        pack, beside, leaf_beyond, across,
    )
    u0_far = exchange(u0, "leaf", 1)
    high_part, _ = lax.optimization_barrier((high_part, u0))
    (far_part,) = kernel(far_kernel, [(2 * high_part.shape[0], wide)], high_part, all_core)
    far = lax.ppermute(far_part, "leaf", [(src, src ^ (6 if src % 2 else 4)) for src in range(plan.groups)])
    def lead_of(level, *parts):
        return kernel(
            lead_kernel,
            [(full, width), (upd, 2 * upd), (rhs, upd)],
            ids, *parts,
            extra=(level,),
        )

    whole1, cross1, start1 = lead_of(1, all_part, all_core)
    (u1,) = kernel(update_kernel, [(rhs // 4, 4 * upd)], start1, cross1, u0, u0_far)
    u1_far = exchange(u1, "leaf", 2)

    whole1, _ = lax.optimization_barrier((whole1, u1))
    own_part, leaf_part = kernel(
        lower_kernel,
        [(rhs + 3 * upd, rows), (rhs + upd, rows)],
        ids, whole1, leaf_all, leaf_ahead, u0, u0_far,
    )
    spare_beyond, _ = lax.optimization_barrier((beyond, u1))
    (top_s,) = kernel(
        outer_kernel,
        [(rhs, upd)],
        ids, pack, beside, spare_beyond, across,
        scratch=[pltpu.VMEM((full, 256), jnp.float32)],
    )
    by_x, far, u1_far, own_part, top_s = lax.optimization_barrier(
        (by_x, far, u1_far, own_part, top_s)
    )
    by_x_core = exchange(by_x, "leaf", 1)
    far_core = exchange(far, "leaf", 1)
    whole2, cross2, start2 = lead_of(2, all_part, all_core, by_x, by_x_core)
    (u2,) = kernel(
        update_kernel, [(rhs // 4, 4 * upd)], start2, cross2, u1, u1_far
    )
    u2_far = exchange(u2, "leaf", 4)
    (base,) = kernel(
        upper_kernel,
        [(rhs + upd, 2 * rows)],
        ids, leaf_part, top_s, u1, u1_far, u2, own_part, whole2,
        all_part, all_core, by_x, by_x_core, far, far_core,
        scratch=[pltpu.VMEM((full, width), jnp.float32)] * 2,
    )
    (out,) = kernel(finish_kernel, [(2, 1, rhs, rows)], base, u2_far)
    return out


def body(*args):
    groups, fronts = lax.axis_size("leaf"), lax.axis_size("front")
    rhs, rows, upd = args[0].shape[1], args[0].shape[2], args[4].shape[1]
    plan = Plan(groups, fronts, rhs, upd, rows)
    if (groups, fronts) == (8, 4) and rows == 64 and rhs == 64 and upd == 32:
        return chain(plan, *args)
    return general(*args)


def solution(mesh):
    placed = (
        P("leaf", None, "front"),
        P("leaf", None, "front"),
        P("leaf", "front", None),
        P("leaf", "front", None),
        P("leaf", None, "front"),
        P("leaf", None, "front"),
        P(),
        P(None, "front"),
    )
    return jax.shard_map(
        body, mesh=mesh, in_specs=placed, out_specs=P(None, "leaf", None, "front"), check_vma=False
    )
```

```python
import functools
import jax
import jax.numpy as jnp
from jax import lax
from jax.experimental import pallas as pl
from jax.experimental.pallas import tpu as pltpu
from jax.sharding import PartitionSpec as P

def halves(value):
    high = value.astype(jnp.bfloat16)
    return high, (value - high.astype(jnp.float32)).astype(jnp.bfloat16)


def product(left, right, side):
    def term(one, two):
        return lax.dot_general(
            one, two, (((1,), (side,)), ((), ())), preferred_element_type=jnp.float32
        )

    (left_high, left_low), (right_high, right_low) = halves(left), halves(right)
    return term(left_high, right_high) + (term(left_high, right_low) + term(left_low, right_high))


def nn(left, right):
    return product(left, right, 0)


def nt(left, right):
    return product(left, right, 1)


def exchange(block, axis, mask):
    count = lax.axis_size(axis)
    return lax.ppermute(block, axis, [(src, src ^ mask) for src in range(count)])


def call(kernel, outs, args, scratch=(), chip=True, cost=1000):
    if chip:
        args = [
            pltpu.with_memory_space_constraint(arg, pltpu.VMEM)
            if arg.ndim == 2
            else arg
            for arg in args
        ]
    return pl.pallas_call(
        kernel,
        out_shape=[
            jax.ShapeDtypeStruct(out, jnp.float32)
            if len(out) == 4
            else pltpu.VMEM(*out)
            if isinstance(out[0], tuple)
            else pltpu.VMEM(out, jnp.float32)
            for out in outs
        ],
        in_specs=[pl.BlockSpec(memory_space=pltpu.VMEM) for _ in args],
        out_specs=[pl.BlockSpec(memory_space=pltpu.VMEM) for _ in outs],
        scratch_shapes=list(scratch),
        compiler_params=pltpu.CompilerParams(vmem_limit_bytes=8 << 20) if chip else None,
        cost_estimate=pl.CostEstimate(flops=cost, bytes_accessed=cost, transcendentals=0),
    )(*args)


class Plan:
    def __init__(self, groups, fronts, rhs, upd, rows):
        self.groups, self.fronts, self.rhs, self.upd, self.rows = groups, fronts, rhs, upd, rows
        self.depth = groups.bit_length() - 1
        self.full = fronts * rows
        self.width = self.full + 128
        self.share, self.offset, self.base, self.blocks = {}, {}, {}, {}
        base = 0
        for level in range(1, self.depth + 2):
            self.blocks[level] = 2 ** min(level, self.depth)
            self.share[level] = rows // self.blocks[level]
            self.offset[level] = rows - (rows >> level - 1)
            self.base[level] = base
            base += fronts * self.share[level]

    def label(self, level, group):
        if level > self.depth:
            return jnp.int32(0)
        return (group // 2**level) * 2**level + 2 ** (level - 1)

    def child_ids(self, level, group, pattern):
        if level == 1:
            kind, labels = 0, (group, group ^ 1)
        elif level > self.depth:
            kind, labels = 1, (self.label(level - 1, group),)
        else:
            kind = 1
            labels = tuple(self.label(level - 1, far) for far in (group, group ^ 2 ** (level - 1)))
        return jnp.concatenate([pattern[pl.ds(kind * self.groups + label, 1), :] for label in labels], axis=1)


def one_hot(ids, count, start=0):
    rows = lax.broadcasted_iota(jnp.int32, (count, ids.shape[1]), 0) + start
    return (rows == ids).astype(jnp.float32)


def own_columns(plan, front, value):
    rows = plan.rows
    result = value[:, :rows]
    for slot in range(1, plan.fronts):
        result = jnp.where(front == slot, value[:, slot * rows : (slot + 1) * rows], result)
    return result


def dense(value):
    count = value.shape[0] // 4
    return jnp.concatenate([value[pos * count : (pos + 1) * count] for pos in range(4)], axis=1)


def undense(value):
    count = value.shape[1] // 4
    return jnp.concatenate([value[:, pos * count : (pos + 1) * count] for pos in range(4)], axis=0)


def place():
    return lax.axis_index("front"), lax.axis_index("leaf")


def pack_kernel(plan, pattern, lr, sr, li, si, lu, su, outer, out, main, ids):
    cut, full, rows, half = plan.full // 2, plan.full, plan.rows, plan.rhs // 2
    ids[...] = pattern[...].reshape(ids.shape)
    for low, inverse, pieces in (
        (0, si, (sr[0], su[0], outer[:half])),
        (rows, li, (lr[0], lu[0], outer[half:])),
    ):
        side = jnp.concatenate(pieces, axis=0).T
        out[low : low + rows, :cut] = inverse[0, :, :cut]
        out[low : low + rows, cut:full] = side
        out[low : low + rows, full:] = inverse[0, :, cut:]
        main[low : low + rows, :cut] = inverse[0, :, :cut]
        main[low : low + rows, cut:] = side


def onward_kernel(plan, pack, across, main, right):
    full = plan.full
    main[...] = across[:, :full]
    right[...] = jnp.where(place()[0] < plan.fronts // 2, across[:, full:], pack[:, full:])


def whole_rows(plan, packs, low, whole):
    front, _ = place()
    cut, full, rows = plan.full // 2, plan.full, plan.rows
    pack, _, _, across, second = packs
    rest = second[low : low + rows, :]
    lower = front < plan.fronts // 2
    rights = (
        pack[low : low + rows, full:],
        jnp.where(lower, 0.0, rest),
        jnp.where(lower, rest, 0.0),
        across[low : low + rows, full:],
    )
    for slot in range(plan.fronts):
        at = pl.multiple_of((front ^ slot) * rows, rows)
        whole[pl.ds(at, rows), :cut] = packs[slot][low : low + rows, :cut]
        whole[pl.ds(at, rows), cut:full] = rights[slot]
        whole[pl.ds(at, rows), full:] = packs[slot][low : low + rows, cut:full]


def outer_kernel(plan, pattern, *refs):
    packs, (picked, natural) = refs[: plan.fronts], refs[plan.fronts :]
    front, _ = place()
    rows, full, edge = plan.rows, plan.full, plan.rhs + plan.upd
    for slot, pack in enumerate(packs):
        at = pl.multiple_of((front ^ slot) * rows, rows)
        natural[pl.ds(at, rows), :128] = pack[:rows, full // 2 : full]
        natural[pl.ds(at, rows), 128:] = pack[rows:, full // 2 : full]
    turned = natural[...].T
    outer = jnp.concatenate([turned[edge:128], turned[128 + edge :]], axis=0)
    picked[...] = nn(outer, one_hot(pattern[plan.groups : plan.groups + 1, :], full))


def fold_rows(plan, rows_of):
    step, full, edge = plan.rows, plan.full, plan.full + plan.rhs + plan.upd
    pieces = [rows_of(front)[:, : (front + 1) * step] for front in (3, 2, 0, 1)]
    pieces += [rows_of(front)[:, full:edge] for front in range(plan.fronts)]
    return jnp.concatenate(pieces, axis=1)


def unfold_rows(plan, folded):
    step, full, edge = plan.rows, plan.full, plan.rhs + plan.upd
    count = folded.shape[0]
    starts = {3: 0, 2: full, 0: full + 3 * step, 1: 2 * full}
    for front in range(plan.fronts):
        wide = (front + 1) * step
        side = 2 * full + 2 * step + front * edge
        pieces = [folded[:, starts[front] : starts[front] + wide]]
        if wide < full:
            pieces.append(jnp.zeros((count, full - wide), jnp.float32))
        pieces.append(folded[:, side : side + edge])
        pieces.append(jnp.zeros((count, plan.width - full - edge), jnp.float32))
        yield front, jnp.concatenate(pieces, axis=1)


def fold_levels(plan, packs, natural):
    whole_rows(plan, packs, 0, natural)
    rows = plan.rows
    for level in range(1, plan.depth + 2):
        offset, share = plan.offset[level], plan.share[level]
        yield offset, fold_rows(
            plan, lambda pos: natural[pos * rows + offset : pos * rows + offset + share, :]
        )


def spread_kernel(plan, *refs):
    packs = refs[: plan.fronts + 1]
    all_part, late_part, high_part, natural = refs[plan.fronts + 1 :]
    for at, piece in fold_levels(plan, packs, natural):
        for out, level in ((all_part, 1), (late_part, 2), (high_part, 3)):
            low = at - plan.offset[level]
            if low >= 0:
                out[low : low + piece.shape[0], :] = piece


def far_kernel(plan, high, all_core, out):
    count = high.shape[0]
    out[:count, :] = high[...]
    out[count:, :] = all_core[plan.offset[3] :, :]


def leaf_kernel(plan, *refs):
    packs, (whole, ahead, update) = refs[: plan.fronts + 1], refs[plan.fronts + 1 :]
    rhs, upd, full = plan.rhs, plan.upd, plan.full
    whole_rows(plan, packs, plan.rows, whole)
    flipped = whole[:, full:].T
    solved = nt(flipped[:rhs], whole[:, :full])
    ahead[:rhs, :] = solved
    ahead[rhs:, :] = flipped[rhs : rhs + upd]
    update[...] = dense(nt(solved, flipped[rhs : rhs + upd]))


def assemble(plan, level, parts, whole):
    blocks, share = plan.blocks[level], plan.share[level]
    _, group = place()
    for ref, first, slot in parts:
        inner = (group & (blocks - 1)) ^ slot
        for front, piece in unfold_rows(plan, ref[first : first + share, :]):
            dest = pl.multiple_of(front * plan.rows + inner * share, share)
            whole[pl.ds(dest, share), :] = piece


def upper_parts(plan, level, refs):
    own, own_core, by_x, by_x_core, far, far_core = refs
    _, group = place()
    at = plan.offset[level] - plan.offset[3]
    late = at + plan.share[2]
    half = plan.share[3] + plan.share[4]
    parts = [(own, plan.offset[level], 0), (own_core, plan.offset[level], 1)]
    parts += [(by_x, late, 2), (by_x_core, late, 3)]
    side = 4 + 2 * (group & 1)
    parts += [(far, at, side), (far, half + at, side ^ 1)]
    return parts + [(far_core, at, side ^ 3), (far_core, half + at, side ^ 2)]


def lead_level(plan, level, pattern, parts, whole):
    assemble(plan, level, parts, whole)
    flipped = whole[:, plan.full :].T
    right, block = flipped[: plan.rhs], flipped[plan.rhs : plan.rhs + plan.upd]
    fold = nn(block, whole[:, : plan.full])
    hot = one_hot(plan.child_ids(level, place()[1], pattern), plan.full)
    return nn(fold, hot), nt(right, fold)


def back_level(plan, level, pattern, whole):
    front, group = place()
    rhs = plan.rhs
    hot = one_hot(plan.child_ids(level, group, pattern), plan.full)
    matrix = whole[:, : plan.full]
    flipped = whole[:, plan.full :].T
    right, block = flipped[:rhs], flipped[rhs : rhs + plan.upd]
    ahead = nt(jnp.concatenate([right, hot.T], axis=0), matrix)
    stacked = jnp.concatenate([ahead, block], axis=0)
    result = [nt(stacked, ahead[rhs : rhs + plan.upd]), nn(stacked, own_columns(plan, front, matrix))]
    if level > plan.depth:
        return result
    return [nt(block, ahead[rhs:]), nt(ahead[:rhs], block)] + result


def lead_kernel(plan, level, pattern, *refs):
    blocks = plan.blocks[level]
    parts = [
        (ref, plan.offset[level] if slot < 2 else 0, slot) for slot, ref in enumerate(refs[:blocks])
    ]
    whole, cross, start = refs[blocks:]
    cross[...], start[...] = lead_level(plan, level, pattern, parts, whole)


def lower_kernel(plan, pattern, whole, leaf_all, leaf_ahead, near, far, own_part, leaf_part):
    rhs, upd = plan.rhs, plan.upd
    known = jnp.concatenate([undense(near[...]), undense(far[...])], axis=1)
    _, _, picks, columns = back_level(plan, 1, pattern, whole)
    leaf_back = nn(leaf_ahead[...], own_columns(plan, place()[0], leaf_all[:, : plan.full]))
    both = jnp.concatenate([columns, picks], axis=1)
    base = both[:rhs] - nn(known, both[rhs : rhs + 2 * upd])
    slope = both[rhs + 2 * upd :]
    own_part[:rhs] = base[:, : plan.rows]
    own_part[rhs : rhs + 2 * upd] = jnp.zeros((2 * upd, plan.rows), jnp.float32)
    own_part[rhs + 2 * upd :] = slope[:, : plan.rows]
    through = jnp.concatenate([base[:, plan.rows :], -slope[:, plan.rows :]], axis=0)
    through = nn(through, leaf_back[rhs:])
    leaf_part[:rhs] = leaf_back[:rhs] - through[:rhs]
    leaf_part[rhs:] = through[rhs:]


def upper_kernel(plan, pattern, leaf_part, top_s, *refs):
    rhs, upd, group = plan.rhs, plan.upd, place()[1]
    known = jnp.concatenate([undense(refs[0][...]), undense(refs[1][...])], axis=1)
    near = undense(refs[2][...])
    picks, columns = {}, {1: refs[3][...]}
    sources, (out, whole3, whole4) = refs[5:11], refs[11:]
    assemble(plan, 3, upper_parts(plan, 3, sources), whole3)
    assemble(plan, 4, upper_parts(plan, 4, sources), whole4)
    cross, start, picks[3], columns[3] = back_level(plan, 3, pattern, whole3)
    picks[4], columns[4] = back_level(plan, 4, pattern, whole4)
    _, _, picks[2], columns[2] = back_level(plan, 2, pattern, refs[4])
    none = jnp.zeros((upd, upd), jnp.float32)
    unit = one_hot(lax.broadcasted_iota(jnp.int32, (1, upd), 1), upd)

    def step(terms, part):
        known = jnp.concatenate([part[:rhs], jnp.zeros((upd, part.shape[1]), jnp.float32)], axis=0)
        return known - nn(jnp.concatenate(terms, axis=1), part[rhs:])

    gap = jnp.zeros((rhs, upd), jnp.float32)
    both = jnp.concatenate(
        [jnp.concatenate([near, gap], axis=1), jnp.concatenate([none, unit], axis=1)], axis=0
    )
    u3 = jnp.concatenate([start, none], axis=0) - nt(both, cross)
    fixed = jnp.concatenate([known, jnp.zeros((upd, 2 * upd), jnp.float32)], axis=0)
    terms = {4: [u3, jnp.concatenate([top_s[...], none], axis=0)]}
    terms[3] = [both, step(terms[4], picks[4])]
    terms[2] = [fixed, step(terms[3], picks[3])]
    last = step(terms[2], picks[2])
    terms[1] = [jnp.zeros((rhs + upd, 2 * upd), jnp.float32), last]
    leaf_out = step([last], leaf_part)
    gap = jnp.zeros((rhs + upd, upd), jnp.float32)
    chosen = jnp.concatenate([columns[4][: rhs + upd], none_wide(plan), columns[4][rhs + upd :]], axis=0)
    weight = jnp.concatenate([terms[4][0], gap, terms[4][1]], axis=1)
    for level in (3, 2, 1):
        here = plan.label(level, group) == group
        chosen = jnp.where(here, columns[level], chosen)
        weight = jnp.where(here, jnp.concatenate(terms[level], axis=1), weight)
    out[...] = jnp.concatenate([leaf_out, step([weight], chosen)], axis=1)


def none_wide(plan):
    return jnp.zeros((plan.upd, plan.rows), jnp.float32)


def finish_kernel(plan, base, far, out):
    rhs, upd, rows = plan.rhs, plan.upd, plan.rows
    total = base[:rhs] + nn(undense(far[...]), base[rhs:])
    out[0, 0] = total[:, :rows]
    out[1, 0] = total[:, rows:]


def update_kernel(plan, start, cross, mine, other, out):
    both = jnp.concatenate([undense(mine[...]), undense(other[...])], axis=1)
    out[...] = dense(start[...] - nt(both, cross[...]))


def partner(block, axis, distance):
    count = lax.axis_size(axis)
    route = []
    for low in range(count):
        high = low | 1 << distance
        if high != low and high < count:
            route += [(low, high), (high, low)]
    return lax.ppermute(block, axis, route)


def times_rows(vectors, matrix):
    return jnp.dot(
        vectors, matrix, precision=lax.Precision.HIGHEST, preferred_element_type=jnp.float32
    )


def against_rows(vectors, matrix):
    return lax.dot_general(
        vectors,
        matrix,
        (((1,), (1,)), ((), ())),
        precision=lax.Precision.HIGHEST,
        preferred_element_type=jnp.float32,
    )


def general(
    leaf_rhs, sep_rhs, leaf_inverse, sep_inverse, leaf_block, sep_block, pattern, outer_solution
):
    group_count = lax.axis_size("leaf")
    depth = group_count.bit_length() - 1
    group_pos = lax.axis_index("leaf")
    front_pos = lax.axis_index("front")
    local_rows = leaf_rhs.shape[-1]
    full_rows = leaf_inverse.shape[-1]
    vector_count = leaf_rhs.shape[1]
    leaf_r = leaf_rhs[0]
    leaf_inv = leaf_inverse[0]
    leaf_u = leaf_block[0]
    sep_r = sep_rhs[0]
    sep_inv = sep_inverse[0]
    sep_u = sep_block[0]
    all_rows = jnp.arange(full_rows, dtype=jnp.int32)

    def geometry(level):
        blocks = 2 ** min(level, depth)
        share = local_rows // blocks
        offset = local_rows - (local_rows >> level - 1)
        return (share, offset, group_pos % blocks)

    def label_of(level):
        if level > depth:
            return jnp.int32(0)
        return group_pos // 2**level * 2**level + 2 ** (level - 1)

    def ids_of(level):
        return lax.dynamic_index_in_dim(pattern[1], label_of(level), 0, keepdims=False)

    def block_sum(term, level):
        nbits = min(level, depth)
        if nbits == depth:
            return lax.psum(term, ("leaf", "front"))
        piece = lax.psum_scatter(term, "front", scatter_dimension=1, tiled=True)
        for bit in range(nbits):
            piece = piece + partner(piece, "leaf", bit)
        return lax.all_gather(piece, "front", axis=1, tiled=True)

    leaf_y = against_rows(lax.all_gather(leaf_r, "front", axis=1, tiled=True), leaf_inv)
    leaf_ids = lax.dynamic_index_in_dim(pattern[0], group_pos, 0, keepdims=False)
    child_part = against_rows(leaf_y, leaf_u)
    child_ids = leaf_ids
    solved = {}
    for level in range(1, depth + 2):
        share, offset, inner_pos = geometry(level)
        own_r = sep_r[:, offset : offset + share]
        start_col = front_pos * local_rows + inner_pos * share
        contribution = jnp.zeros((vector_count, full_rows), jnp.float32)
        contribution = lax.dynamic_update_slice(contribution, own_r, (jnp.int32(0), start_col))
        selector = (child_ids[:, None] == all_rows[None, :]).astype(jnp.float32)
        contribution = contribution - times_rows(child_part, selector)
        whole_v = block_sum(contribution, level)
        y_level = against_rows(whole_v, sep_inv[offset : offset + share, :])
        solved[level] = y_level
        if level <= depth:
            child_part = against_rows(y_level, sep_u[:, offset : offset + share])
            child_ids = ids_of(level)
    parent_x = lax.all_gather(outer_solution, "front", axis=1, tiled=True)
    sep_full = jnp.zeros((vector_count, full_rows), jnp.float32)
    for level in range(depth + 1, 0, -1):
        share, offset, inner_pos = geometry(level)
        picked = jnp.take(parent_x, ids_of(level), axis=1)
        rest = solved[level] - times_rows(picked, sep_u[:, offset : offset + share])
        term = times_rows(rest, sep_inv[offset : offset + share, :])
        parent_x = block_sum(term, level)
        sep_full = jnp.where(label_of(level) == group_pos, parent_x, sep_full)
    picked = jnp.take(parent_x, leaf_ids, axis=1)
    rest = leaf_y - times_rows(picked, leaf_u)
    leaf_x = lax.psum_scatter(times_rows(rest, leaf_inv), "front", scatter_dimension=1, tiled=True)
    sep_x = lax.dynamic_slice_in_dim(sep_full, front_pos * local_rows, local_rows, 1)
    return jnp.stack([leaf_x, sep_x])[:, None]


def chain(
    plan, leaf_rhs, sep_rhs, leaf_inverse, sep_inverse, leaf_block, sep_block, pattern, outer
):
    full, rows, rhs, upd, width = plan.full, plan.rows, plan.rhs, plan.upd, plan.width

    def kernel(body, outs, *args, extra=(), **kw):
        return call(functools.partial(body, plan, *extra), outs, args, **kw)

    pack, main, ids = kernel(
        pack_kernel,
        [
            (2 * rows, width),
            (2 * rows, full),
            ((pattern.shape[0] * pattern.shape[1], upd), jnp.int32),
        ],
        pattern, leaf_rhs, sep_rhs, leaf_inverse, sep_inverse, leaf_block, sep_block, outer,
        chip=False,
    )
    across = exchange(pack, "front", 3)
    beside = exchange(main, "front", 1)
    onward, onward_second = kernel(
        onward_kernel, [(2 * rows, full), (2 * rows, full // 2)], pack, across
    )
    beyond = exchange(onward, "front", 1)
    second = exchange(onward_second, "front", 1)
    wide = 4 * full
    all_part, late_part, high_part = kernel(
        spread_kernel,
        [
            (rows, wide),
            (rows - plan.share[1], wide),
            (plan.share[3] + plan.share[4], wide),
        ],
        pack, beside, beyond, across, second,
        scratch=[pltpu.VMEM((full, width), jnp.float32)],
    )
    all_core = exchange(all_part, "leaf", 1)
    by_x = exchange(late_part, "leaf", 2)
    leaf_beyond, _ = lax.optimization_barrier((beyond, all_part))
    leaf_all, leaf_ahead, u0 = kernel(
        leaf_kernel,
        [(full, width), (rhs + upd, full), (rhs // 4, 4 * upd)],
        pack, beside, leaf_beyond, across, second,
    )
    u0_far = exchange(u0, "leaf", 1)
    high_part, _ = lax.optimization_barrier((high_part, u0))
    (far_part,) = kernel(far_kernel, [(2 * high_part.shape[0], wide)], high_part, all_core)
    far = lax.ppermute(far_part, "leaf", [(src, src ^ (6 if src % 2 else 4)) for src in range(plan.groups)])
    def lead_of(level, *parts):
        return kernel(
            lead_kernel,
            [(full, width), (upd, 2 * upd), (rhs, upd)],
            ids, *parts,
            extra=(level,),
        )

    whole1, cross1, start1 = lead_of(1, all_part, all_core)
    (u1,) = kernel(update_kernel, [(rhs // 4, 4 * upd)], start1, cross1, u0, u0_far)
    u1_far = exchange(u1, "leaf", 2)

    whole1, _ = lax.optimization_barrier((whole1, u1))
    own_part, leaf_part = kernel(
        lower_kernel,
        [(rhs + 3 * upd, rows), (rhs + upd, rows)],
        ids, whole1, leaf_all, leaf_ahead, u0, u0_far,
    )
    spare_beyond, _ = lax.optimization_barrier((beyond, u1))
    (top_s,) = kernel(
        outer_kernel,
        [(rhs, upd)],
        ids, pack, beside, spare_beyond, across,
        scratch=[pltpu.VMEM((full, 256), jnp.float32)],
    )
    by_x, far, u1_far, own_part, top_s = lax.optimization_barrier(
        (by_x, far, u1_far, own_part, top_s)
    )
    by_x_core = exchange(by_x, "leaf", 1)
    far_core = exchange(far, "leaf", 1)
    whole2, cross2, start2 = lead_of(2, all_part, all_core, by_x, by_x_core)
    (u2,) = kernel(
        update_kernel, [(rhs // 4, 4 * upd)], start2, cross2, u1, u1_far
    )
    u2_far = exchange(u2, "leaf", 4)
    (base,) = kernel(
        upper_kernel,
        [(rhs + upd, 2 * rows)],
        ids, leaf_part, top_s, u1, u1_far, u2, own_part, whole2,
        all_part, all_core, by_x, by_x_core, far, far_core,
        scratch=[pltpu.VMEM((full, width), jnp.float32)] * 2,
    )
    (out,) = kernel(finish_kernel, [(2, 1, rhs, rows)], base, u2_far)
    return out


def body(*args):
    groups, fronts = lax.axis_size("leaf"), lax.axis_size("front")
    rhs, rows, upd = args[0].shape[1], args[0].shape[2], args[4].shape[1]
    plan = Plan(groups, fronts, rhs, upd, rows)
    if (groups, fronts) == (8, 4) and rows == 64 and rhs == 64 and upd == 32:
        return chain(plan, *args)
    return general(*args)


def solution(mesh):
    placed = (
        P("leaf", None, "front"),
        P("leaf", None, "front"),
        P("leaf", "front", None),
        P("leaf", "front", None),
        P("leaf", None, "front"),
        P("leaf", None, "front"),
        P(),
        P(None, "front"),
    )
    return jax.shard_map(
        body, mesh=mesh, in_specs=placed, out_specs=P(None, "leaf", None, "front"), check_vma=False
    )
```

```python
import functools
import jax
import jax.numpy as jnp
from jax import lax
from jax.experimental import pallas as pl
from jax.experimental.pallas import tpu as pltpu
from jax.sharding import PartitionSpec as P

def halves(value):
    high = value.astype(jnp.bfloat16)
    return high, (value - high.astype(jnp.float32)).astype(jnp.bfloat16)


def product(left, right, side):
    def term(one, two):
        return lax.dot_general(
            one, two, (((1,), (side,)), ((), ())), preferred_element_type=jnp.float32
        )

    (left_high, left_low), (right_high, right_low) = halves(left), halves(right)
    return term(left_high, right_high) + (term(left_high, right_low) + term(left_low, right_high))


def nn(left, right):
    return product(left, right, 0)


def nt(left, right):
    return product(left, right, 1)


def exchange(block, axis, mask):
    count = lax.axis_size(axis)
    return lax.ppermute(block, axis, [(src, src ^ mask) for src in range(count)])


def call(kernel, outs, args, scratch=(), chip=True, cost=1000):
    if chip:
        args = [
            pltpu.with_memory_space_constraint(arg, pltpu.VMEM)
            if arg.ndim == 2
            else arg
            for arg in args
        ]
    return pl.pallas_call(
        kernel,
        out_shape=[
            jax.ShapeDtypeStruct(out, jnp.float32)
            if len(out) == 4
            else pltpu.VMEM(*out)
            if isinstance(out[0], tuple)
            else pltpu.VMEM(out, jnp.float32)
            for out in outs
        ],
        in_specs=[pl.BlockSpec(memory_space=pltpu.VMEM) for _ in args],
        out_specs=[pl.BlockSpec(memory_space=pltpu.VMEM) for _ in outs],
        scratch_shapes=list(scratch),
        compiler_params=pltpu.CompilerParams(vmem_limit_bytes=8 << 20) if chip else None,
        cost_estimate=pl.CostEstimate(flops=cost, bytes_accessed=cost, transcendentals=0),
    )(*args)


class Plan:
    def __init__(self, groups, fronts, rhs, upd, rows):
        self.groups, self.fronts, self.rhs, self.upd, self.rows = groups, fronts, rhs, upd, rows
        self.depth = groups.bit_length() - 1
        self.full = fronts * rows
        self.width = self.full + 128
        self.share, self.offset, self.base, self.blocks = {}, {}, {}, {}
        base = 0
        for level in range(1, self.depth + 2):
            self.blocks[level] = 2 ** min(level, self.depth)
            self.share[level] = rows // self.blocks[level]
            self.offset[level] = rows - (rows >> level - 1)
            self.base[level] = base
            base += fronts * self.share[level]

    def label(self, level, group):
        if level > self.depth:
            return jnp.int32(0)
        return (group // 2**level) * 2**level + 2 ** (level - 1)

    def child_ids(self, level, group, pattern):
        if level == 1:
            kind, labels = 0, (group, group ^ 1)
        elif level > self.depth:
            kind, labels = 1, (self.label(level - 1, group),)
        else:
            kind = 1
            labels = tuple(self.label(level - 1, far) for far in (group, group ^ 2 ** (level - 1)))
        return jnp.concatenate([pattern[pl.ds(kind * self.groups + label, 1), :] for label in labels], axis=1)


def one_hot(ids, count, start=0):
    rows = lax.broadcasted_iota(jnp.int32, (count, ids.shape[1]), 0) + start
    return (rows == ids).astype(jnp.float32)


def own_columns(plan, front, value):
    rows = plan.rows
    result = value[:, :rows]
    for slot in range(1, plan.fronts):
        result = jnp.where(front == slot, value[:, slot * rows : (slot + 1) * rows], result)
    return result


def dense(value):
    count = value.shape[0] // 4
    return jnp.concatenate([value[pos * count : (pos + 1) * count] for pos in range(4)], axis=1)


def undense(value):
    count = value.shape[1] // 4
    return jnp.concatenate([value[:, pos * count : (pos + 1) * count] for pos in range(4)], axis=0)


def place():
    return lax.axis_index("front"), lax.axis_index("leaf")


def pack_kernel(plan, pattern, lr, sr, li, si, lu, su, outer, out, main, ids):
    cut, full, rows, half = plan.full // 2, plan.full, plan.rows, plan.rhs // 2
    ids[...] = pattern[...].reshape(ids.shape)
    for low, inverse, pieces in (
        (0, si, (sr[0], su[0], outer[:half])),
        (rows, li, (lr[0], lu[0], outer[half:])),
    ):
        side = jnp.concatenate(pieces, axis=0).T
        out[low : low + rows, :cut] = inverse[0, :, :cut]
        out[low : low + rows, cut:full] = side
        out[low : low + rows, full:] = inverse[0, :, cut:]
        main[low : low + rows, :cut] = inverse[0, :, :cut]
        main[low : low + rows, cut:] = side


def onward_kernel(plan, pack, across, main, right):
    full = plan.full
    main[...] = across[:, :full]
    right[...] = jnp.where(place()[0] < plan.fronts // 2, across[:, full:], pack[:, full:])


def whole_rows(plan, packs, low, whole):
    front, _ = place()
    cut, full, rows = plan.full // 2, plan.full, plan.rows
    pack, _, _, across, second = packs
    rest = second[low : low + rows, :]
    lower = front < plan.fronts // 2
    rights = (
        pack[low : low + rows, full:],
        jnp.where(lower, 0.0, rest),
        jnp.where(lower, rest, 0.0),
        across[low : low + rows, full:],
    )
    for slot in range(plan.fronts):
        at = pl.multiple_of((front ^ slot) * rows, rows)
        whole[pl.ds(at, rows), :cut] = packs[slot][low : low + rows, :cut]
        whole[pl.ds(at, rows), cut:full] = rights[slot]
        whole[pl.ds(at, rows), full:] = packs[slot][low : low + rows, cut:full]


def outer_kernel(plan, pattern, *refs):
    packs, (picked, natural) = refs[: plan.fronts], refs[plan.fronts :]
    front, _ = place()
    rows, full, edge = plan.rows, plan.full, plan.rhs + plan.upd
    for slot, pack in enumerate(packs):
        at = pl.multiple_of((front ^ slot) * rows, rows)
        natural[pl.ds(at, rows), :128] = pack[:rows, full // 2 : full]
        natural[pl.ds(at, rows), 128:] = pack[rows:, full // 2 : full]
    turned = natural[...].T
    outer = jnp.concatenate([turned[edge:128], turned[128 + edge :]], axis=0)
    picked[...] = nn(outer, one_hot(pattern[plan.groups : plan.groups + 1, :], full))


def fold_rows(plan, rows_of):
    step, full, edge = plan.rows, plan.full, plan.full + plan.rhs + plan.upd
    pieces = [rows_of(front)[:, : (front + 1) * step] for front in (3, 2, 0, 1)]
    pieces += [rows_of(front)[:, full:edge] for front in range(plan.fronts)]
    return jnp.concatenate(pieces, axis=1)


def unfold_rows(plan, folded):
    step, full, edge = plan.rows, plan.full, plan.rhs + plan.upd
    count = folded.shape[0]
    starts = {3: 0, 2: full, 0: full + 3 * step, 1: 2 * full}
    for front in range(plan.fronts):
        wide = (front + 1) * step
        side = 2 * full + 2 * step + front * edge
        pieces = [folded[:, starts[front] : starts[front] + wide]]
        if wide < full:
            pieces.append(jnp.zeros((count, full - wide), jnp.float32))
        pieces.append(folded[:, side : side + edge])
        pieces.append(jnp.zeros((count, plan.width - full - edge), jnp.float32))
        yield front, jnp.concatenate(pieces, axis=1)


def fold_levels(plan, packs, natural):
    whole_rows(plan, packs, 0, natural)
    rows = plan.rows
    for level in range(1, plan.depth + 2):
        offset, share = plan.offset[level], plan.share[level]
        yield offset, fold_rows(
            plan, lambda pos: natural[pos * rows + offset : pos * rows + offset + share, :]
        )


def spread_kernel(plan, *refs):
    packs = refs[: plan.fronts + 1]
    all_part, late_part, high_part, natural = refs[plan.fronts + 1 :]
    for at, piece in fold_levels(plan, packs, natural):
        for out, level in ((all_part, 1), (late_part, 2), (high_part, 3)):
            low = at - plan.offset[level]
            if low >= 0:
                out[low : low + piece.shape[0], :] = piece


def far_kernel(plan, high, all_core, out):
    count = high.shape[0]
    out[:count, :] = high[...]
    out[count:, :] = all_core[plan.offset[3] :, : out.shape[1]]


def leaf_kernel(plan, *refs):
    packs, (all_part, whole, ahead, update, message) = refs[: plan.fronts + 1], refs[plan.fronts + 1 :]
    rhs, upd, full = plan.rhs, plan.upd, plan.full
    whole_rows(plan, packs, plan.rows, whole)
    flipped = whole[:, full:].T
    solved = nt(flipped[:rhs], whole[:, :full])
    ahead[:rhs, :] = solved
    ahead[rhs:, :] = flipped[rhs : rhs + upd]
    result = dense(nt(solved, flipped[rhs : rhs + upd]))
    update[...] = result
    wide = all_part.shape[1]
    message[:, :wide] = all_part[...]
    message[: result.shape[0], wide:] = result


def assemble(plan, level, parts, whole):
    blocks, share = plan.blocks[level], plan.share[level]
    _, group = place()
    for ref, first, slot in parts:
        inner = (group & (blocks - 1)) ^ slot
        for front, piece in unfold_rows(plan, ref[first : first + share, :]):
            dest = pl.multiple_of(front * plan.rows + inner * share, share)
            whole[pl.ds(dest, share), :] = piece


def upper_parts(plan, level, refs):
    own, own_core, by_x, by_x_core, far, far_core = refs
    _, group = place()
    at = plan.offset[level] - plan.offset[3]
    late = at + plan.share[2]
    half = plan.share[3] + plan.share[4]
    parts = [(own, plan.offset[level], 0), (own_core, plan.offset[level], 1)]
    parts += [(by_x, late, 2), (by_x_core, late, 3)]
    side = 4 + 2 * (group & 1)
    parts += [(far, at, side), (far, half + at, side ^ 1)]
    return parts + [(far_core, at, side ^ 3), (far_core, half + at, side ^ 2)]


def lead_level(plan, level, pattern, parts, whole):
    assemble(plan, level, parts, whole)
    flipped = whole[:, plan.full :].T
    right, block = flipped[: plan.rhs], flipped[plan.rhs : plan.rhs + plan.upd]
    fold = nn(block, whole[:, : plan.full])
    hot = one_hot(plan.child_ids(level, place()[1], pattern), plan.full)
    return nn(fold, hot), nt(right, fold)


def back_level(plan, level, pattern, whole):
    front, group = place()
    rhs = plan.rhs
    hot = one_hot(plan.child_ids(level, group, pattern), plan.full)
    matrix = whole[:, : plan.full]
    flipped = whole[:, plan.full :].T
    right, block = flipped[:rhs], flipped[rhs : rhs + plan.upd]
    ahead = nt(jnp.concatenate([right, hot.T], axis=0), matrix)
    stacked = jnp.concatenate([ahead, block], axis=0)
    result = [nt(stacked, ahead[rhs : rhs + plan.upd]), nn(stacked, own_columns(plan, front, matrix))]
    if level > plan.depth:
        return result
    return [nt(block, ahead[rhs:]), nt(ahead[:rhs], block)] + result


def lead_kernel(plan, level, pattern, *refs):
    blocks = plan.blocks[level]
    parts = [
        (ref, plan.offset[level] if slot < 2 else 0, slot) for slot, ref in enumerate(refs[:blocks])
    ]
    whole, cross, start = refs[blocks:]
    cross[...], start[...] = lead_level(plan, level, pattern, parts, whole)


def lower_kernel(plan, pattern, whole, leaf_all, leaf_ahead, near, far, own_part, leaf_part):
    rhs, upd = plan.rhs, plan.upd
    known = jnp.concatenate([undense(near[...]), undense(far[...])], axis=1)
    _, _, picks, columns = back_level(plan, 1, pattern, whole)
    leaf_back = nn(leaf_ahead[...], own_columns(plan, place()[0], leaf_all[:, : plan.full]))
    both = jnp.concatenate([columns, picks], axis=1)
    base = both[:rhs] - nn(known, both[rhs : rhs + 2 * upd])
    slope = both[rhs + 2 * upd :]
    own_part[:rhs] = base[:, : plan.rows]
    own_part[rhs : rhs + 2 * upd] = jnp.zeros((2 * upd, plan.rows), jnp.float32)
    own_part[rhs + 2 * upd :] = slope[:, : plan.rows]
    through = jnp.concatenate([base[:, plan.rows :], -slope[:, plan.rows :]], axis=0)
    through = nn(through, leaf_back[rhs:])
    leaf_part[:rhs] = leaf_back[:rhs] - through[:rhs]
    leaf_part[rhs:] = through[rhs:]


def upper_kernel(plan, pattern, leaf_part, top_s, *refs):
    rhs, upd, group = plan.rhs, plan.upd, place()[1]
    known = jnp.concatenate([undense(refs[0][...]), undense(refs[1][...])], axis=1)
    near = undense(refs[2][...])
    picks, columns = {}, {1: refs[3][...]}
    sources, (out, whole3, whole4) = refs[5:11], refs[11:]
    assemble(plan, 3, upper_parts(plan, 3, sources), whole3)
    assemble(plan, 4, upper_parts(plan, 4, sources), whole4)
    cross, start, picks[3], columns[3] = back_level(plan, 3, pattern, whole3)
    picks[4], columns[4] = back_level(plan, 4, pattern, whole4)
    _, _, picks[2], columns[2] = back_level(plan, 2, pattern, refs[4])
    none = jnp.zeros((upd, upd), jnp.float32)
    unit = one_hot(lax.broadcasted_iota(jnp.int32, (1, upd), 1), upd)

    def step(terms, part):
        known = jnp.concatenate([part[:rhs], jnp.zeros((upd, part.shape[1]), jnp.float32)], axis=0)
        return known - nn(jnp.concatenate(terms, axis=1), part[rhs:])

    gap = jnp.zeros((rhs, upd), jnp.float32)
    both = jnp.concatenate(
        [jnp.concatenate([near, gap], axis=1), jnp.concatenate([none, unit], axis=1)], axis=0
    )
    u3 = jnp.concatenate([start, none], axis=0) - nt(both, cross)
    fixed = jnp.concatenate([known, jnp.zeros((upd, 2 * upd), jnp.float32)], axis=0)
    terms = {4: [u3, jnp.concatenate([top_s[...], none], axis=0)]}
    terms[3] = [both, step(terms[4], picks[4])]
    terms[2] = [fixed, step(terms[3], picks[3])]
    last = step(terms[2], picks[2])
    terms[1] = [jnp.zeros((rhs + upd, 2 * upd), jnp.float32), last]
    leaf_out = step([last], leaf_part)
    gap = jnp.zeros((rhs + upd, upd), jnp.float32)
    chosen = jnp.concatenate([columns[4][: rhs + upd], none_wide(plan), columns[4][rhs + upd :]], axis=0)
    weight = jnp.concatenate([terms[4][0], gap, terms[4][1]], axis=1)
    for level in (3, 2, 1):
        here = plan.label(level, group) == group
        chosen = jnp.where(here, columns[level], chosen)
        weight = jnp.where(here, jnp.concatenate(terms[level], axis=1), weight)
    out[...] = jnp.concatenate([leaf_out, step([weight], chosen)], axis=1)


def none_wide(plan):
    return jnp.zeros((plan.upd, plan.rows), jnp.float32)


def finish_kernel(plan, base, far, out):
    rhs, upd, rows = plan.rhs, plan.upd, plan.rows
    total = base[:rhs] + nn(undense(far[...]), base[rhs:])
    out[0, 0] = total[:, :rows]
    out[1, 0] = total[:, rows:]


def first_update_kernel(plan, start, cross, mine, message, out, other):
    count, wide = mine.shape
    other[...] = message[:count, message.shape[1] - wide :]
    both = jnp.concatenate([undense(mine[...]), undense(other[...])], axis=1)
    out[...] = dense(start[...] - nt(both, cross[...]))


def update_kernel(plan, start, cross, mine, other, out):
    both = jnp.concatenate([undense(mine[...]), undense(other[...])], axis=1)
    out[...] = dense(start[...] - nt(both, cross[...]))


def partner(block, axis, distance):
    count = lax.axis_size(axis)
    route = []
    for low in range(count):
        high = low | 1 << distance
        if high != low and high < count:
            route += [(low, high), (high, low)]
    return lax.ppermute(block, axis, route)


def times_rows(vectors, matrix):
    return jnp.dot(
        vectors, matrix, precision=lax.Precision.HIGHEST, preferred_element_type=jnp.float32
    )


def against_rows(vectors, matrix):
    return lax.dot_general(
        vectors,
        matrix,
        (((1,), (1,)), ((), ())),
        precision=lax.Precision.HIGHEST,
        preferred_element_type=jnp.float32,
    )


def general(
    leaf_rhs, sep_rhs, leaf_inverse, sep_inverse, leaf_block, sep_block, pattern, outer_solution
):
    group_count = lax.axis_size("leaf")
    depth = group_count.bit_length() - 1
    group_pos = lax.axis_index("leaf")
    front_pos = lax.axis_index("front")
    local_rows = leaf_rhs.shape[-1]
    full_rows = leaf_inverse.shape[-1]
    vector_count = leaf_rhs.shape[1]
    leaf_r = leaf_rhs[0]
    leaf_inv = leaf_inverse[0]
    leaf_u = leaf_block[0]
    sep_r = sep_rhs[0]
    sep_inv = sep_inverse[0]
    sep_u = sep_block[0]
    all_rows = jnp.arange(full_rows, dtype=jnp.int32)

    def geometry(level):
        blocks = 2 ** min(level, depth)
        share = local_rows // blocks
        offset = local_rows - (local_rows >> level - 1)
        return (share, offset, group_pos % blocks)

    def label_of(level):
        if level > depth:
            return jnp.int32(0)
        return group_pos // 2**level * 2**level + 2 ** (level - 1)

    def ids_of(level):
        return lax.dynamic_index_in_dim(pattern[1], label_of(level), 0, keepdims=False)

    def block_sum(term, level):
        nbits = min(level, depth)
        if nbits == depth:
            return lax.psum(term, ("leaf", "front"))
        piece = lax.psum_scatter(term, "front", scatter_dimension=1, tiled=True)
        for bit in range(nbits):
            piece = piece + partner(piece, "leaf", bit)
        return lax.all_gather(piece, "front", axis=1, tiled=True)

    leaf_y = against_rows(lax.all_gather(leaf_r, "front", axis=1, tiled=True), leaf_inv)
    leaf_ids = lax.dynamic_index_in_dim(pattern[0], group_pos, 0, keepdims=False)
    child_part = against_rows(leaf_y, leaf_u)
    child_ids = leaf_ids
    solved = {}
    for level in range(1, depth + 2):
        share, offset, inner_pos = geometry(level)
        own_r = sep_r[:, offset : offset + share]
        start_col = front_pos * local_rows + inner_pos * share
        contribution = jnp.zeros((vector_count, full_rows), jnp.float32)
        contribution = lax.dynamic_update_slice(contribution, own_r, (jnp.int32(0), start_col))
        selector = (child_ids[:, None] == all_rows[None, :]).astype(jnp.float32)
        contribution = contribution - times_rows(child_part, selector)
        whole_v = block_sum(contribution, level)
        y_level = against_rows(whole_v, sep_inv[offset : offset + share, :])
        solved[level] = y_level
        if level <= depth:
            child_part = against_rows(y_level, sep_u[:, offset : offset + share])
            child_ids = ids_of(level)
    parent_x = lax.all_gather(outer_solution, "front", axis=1, tiled=True)
    sep_full = jnp.zeros((vector_count, full_rows), jnp.float32)
    for level in range(depth + 1, 0, -1):
        share, offset, inner_pos = geometry(level)
        picked = jnp.take(parent_x, ids_of(level), axis=1)
        rest = solved[level] - times_rows(picked, sep_u[:, offset : offset + share])
        term = times_rows(rest, sep_inv[offset : offset + share, :])
        parent_x = block_sum(term, level)
        sep_full = jnp.where(label_of(level) == group_pos, parent_x, sep_full)
    picked = jnp.take(parent_x, leaf_ids, axis=1)
    rest = leaf_y - times_rows(picked, leaf_u)
    leaf_x = lax.psum_scatter(times_rows(rest, leaf_inv), "front", scatter_dimension=1, tiled=True)
    sep_x = lax.dynamic_slice_in_dim(sep_full, front_pos * local_rows, local_rows, 1)
    return jnp.stack([leaf_x, sep_x])[:, None]


def chain(
    plan, leaf_rhs, sep_rhs, leaf_inverse, sep_inverse, leaf_block, sep_block, pattern, outer
):
    full, rows, rhs, upd, width = plan.full, plan.rows, plan.rhs, plan.upd, plan.width

    def kernel(body, outs, *args, extra=(), **kw):
        return call(functools.partial(body, plan, *extra), outs, args, **kw)

    pack, main, ids = kernel(
        pack_kernel,
        [
            (2 * rows, width),
            (2 * rows, full),
            ((pattern.shape[0] * pattern.shape[1], upd), jnp.int32),
        ],
        pattern, leaf_rhs, sep_rhs, leaf_inverse, sep_inverse, leaf_block, sep_block, outer,
        chip=False,
    )
    across = exchange(pack, "front", 3)
    beside = exchange(main, "front", 1)
    onward, onward_second = kernel(
        onward_kernel, [(2 * rows, full), (2 * rows, full // 2)], pack, across
    )
    beyond = exchange(onward, "front", 1)
    second = exchange(onward_second, "front", 1)
    wide = 4 * full
    all_part, late_part, high_part = kernel(
        spread_kernel,
        [
            (rows, wide),
            (rows - plan.share[1], wide),
            (plan.share[3] + plan.share[4], wide),
        ],
        pack, beside, beyond, across, second,
        scratch=[pltpu.VMEM((full, width), jnp.float32)],
    )
    by_x = exchange(late_part, "leaf", 2)
    leaf_beyond, _ = lax.optimization_barrier((beyond, all_part))
    leaf_all, leaf_ahead, u0, message = kernel(
        leaf_kernel,
        [
            (full, width),
            (rhs + upd, full),
            (rhs // 4, 4 * upd),
            (rows, wide + 4 * upd),
        ],
        pack, beside, leaf_beyond, across, second, all_part,
    )
    all_core = exchange(message, "leaf", 1)
    high_part, _ = lax.optimization_barrier((high_part, u0))
    (far_part,) = kernel(far_kernel, [(2 * high_part.shape[0], wide)], high_part, all_core)
    far = lax.ppermute(far_part, "leaf", [(src, src ^ (6 if src % 2 else 4)) for src in range(plan.groups)])
    def lead_of(level, *parts):
        return kernel(
            lead_kernel,
            [(full, width), (upd, 2 * upd), (rhs, upd)],
            ids, *parts,
            extra=(level,),
        )

    whole1, cross1, start1 = lead_of(1, all_part, all_core)
    u1, u0_far = kernel(
        first_update_kernel, [(rhs // 4, 4 * upd)] * 2, start1, cross1, u0, all_core
    )
    u1_far = exchange(u1, "leaf", 2)

    whole1, _ = lax.optimization_barrier((whole1, u1))
    own_part, leaf_part = kernel(
        lower_kernel,
        [(rhs + 3 * upd, rows), (rhs + upd, rows)],
        ids, whole1, leaf_all, leaf_ahead, u0, u0_far,
    )
    spare_beyond, _ = lax.optimization_barrier((beyond, u1))
    (top_s,) = kernel(
        outer_kernel,
        [(rhs, upd)],
        ids, pack, beside, spare_beyond, across,
        scratch=[pltpu.VMEM((full, 256), jnp.float32)],
    )
    by_x, far, u1_far, own_part, top_s = lax.optimization_barrier(
        (by_x, far, u1_far, own_part, top_s)
    )
    by_x_core = exchange(by_x, "leaf", 1)
    far_core = exchange(far, "leaf", 1)
    whole2, cross2, start2 = lead_of(2, all_part, all_core, by_x, by_x_core)
    (u2,) = kernel(
        update_kernel, [(rhs // 4, 4 * upd)], start2, cross2, u1, u1_far
    )
    u2_far = exchange(u2, "leaf", 4)
    (base,) = kernel(
        upper_kernel,
        [(rhs + upd, 2 * rows)],
        ids, leaf_part, top_s, u1, u1_far, u2, own_part, whole2,
        all_part, all_core, by_x, by_x_core, far, far_core,
        scratch=[pltpu.VMEM((full, width), jnp.float32)] * 2,
    )
    (out,) = kernel(finish_kernel, [(2, 1, rhs, rows)], base, u2_far)
    return out


def body(*args):
    groups, fronts = lax.axis_size("leaf"), lax.axis_size("front")
    rhs, rows, upd = args[0].shape[1], args[0].shape[2], args[4].shape[1]
    plan = Plan(groups, fronts, rhs, upd, rows)
    if (groups, fronts) == (8, 4) and rows == 64 and rhs == 64 and upd == 32:
        return chain(plan, *args)
    return general(*args)


def solution(mesh):
    placed = (
        P("leaf", None, "front"),
        P("leaf", None, "front"),
        P("leaf", "front", None),
        P("leaf", "front", None),
        P("leaf", None, "front"),
        P("leaf", None, "front"),
        P(),
        P(None, "front"),
    )
    return jax.shard_map(
        body, mesh=mesh, in_specs=placed, out_specs=P(None, "leaf", None, "front"), check_vma=False
    )
```

```python
import functools
import jax
import jax.numpy as jnp
from jax import lax
from jax.experimental import pallas as pl
from jax.experimental.pallas import tpu as pltpu
from jax.sharding import PartitionSpec as P

def halves(value):
    high = value.astype(jnp.bfloat16)
    return high, (value - high.astype(jnp.float32)).astype(jnp.bfloat16)


def product(left, right, side):
    def term(one, two):
        return lax.dot_general(
            one, two, (((1,), (side,)), ((), ())), preferred_element_type=jnp.float32
        )

    (left_high, left_low), (right_high, right_low) = halves(left), halves(right)
    return term(left_high, right_high) + (term(left_high, right_low) + term(left_low, right_high))


def nn(left, right):
    return product(left, right, 0)


def nt(left, right):
    return product(left, right, 1)


def exchange(block, axis, mask):
    count = lax.axis_size(axis)
    return lax.ppermute(block, axis, [(src, src ^ mask) for src in range(count)])


def call(kernel, outs, args, scratch=(), chip=True, cost=1000):
    if chip:
        args = [
            pltpu.with_memory_space_constraint(arg, pltpu.VMEM)
            if arg.ndim == 2
            else arg
            for arg in args
        ]
    return pl.pallas_call(
        kernel,
        out_shape=[
            jax.ShapeDtypeStruct(out, jnp.float32)
            if len(out) == 4
            else pltpu.VMEM(*out)
            if isinstance(out[0], tuple)
            else pltpu.VMEM(out, jnp.float32)
            for out in outs
        ],
        in_specs=[pl.BlockSpec(memory_space=pltpu.VMEM) for _ in args],
        out_specs=[pl.BlockSpec(memory_space=pltpu.VMEM) for _ in outs],
        scratch_shapes=list(scratch),
        compiler_params=pltpu.CompilerParams(vmem_limit_bytes=8 << 20) if chip else None,
        cost_estimate=pl.CostEstimate(flops=cost, bytes_accessed=cost, transcendentals=0),
    )(*args)


class Plan:
    def __init__(self, groups, fronts, rhs, upd, rows):
        self.groups, self.fronts, self.rhs, self.upd, self.rows = groups, fronts, rhs, upd, rows
        self.depth = groups.bit_length() - 1
        self.full = fronts * rows
        self.width = self.full + 128
        self.share, self.offset, self.base, self.blocks = {}, {}, {}, {}
        base = 0
        for level in range(1, self.depth + 2):
            self.blocks[level] = 2 ** min(level, self.depth)
            self.share[level] = rows // self.blocks[level]
            self.offset[level] = rows - (rows >> level - 1)
            self.base[level] = base
            base += fronts * self.share[level]

    def label(self, level, group):
        if level > self.depth:
            return jnp.int32(0)
        return (group // 2**level) * 2**level + 2 ** (level - 1)

    def child_ids(self, level, group, pattern):
        if level == 1:
            kind, labels = 0, (group, group ^ 1)
        elif level > self.depth:
            kind, labels = 1, (self.label(level - 1, group),)
        else:
            kind = 1
            labels = tuple(self.label(level - 1, far) for far in (group, group ^ 2 ** (level - 1)))
        return jnp.concatenate([pattern[pl.ds(kind * self.groups + label, 1), :] for label in labels], axis=1)


def one_hot(ids, count, start=0):
    rows = lax.broadcasted_iota(jnp.int32, (count, ids.shape[1]), 0) + start
    return (rows == ids).astype(jnp.float32)


def own_columns(plan, front, value):
    rows = plan.rows
    result = value[:, :rows]
    for slot in range(1, plan.fronts):
        result = jnp.where(front == slot, value[:, slot * rows : (slot + 1) * rows], result)
    return result


def dense(value):
    count = value.shape[0] // 4
    return jnp.concatenate([value[pos * count : (pos + 1) * count] for pos in range(4)], axis=1)


def undense(value):
    count = value.shape[1] // 4
    return jnp.concatenate([value[:, pos * count : (pos + 1) * count] for pos in range(4)], axis=0)


def place():
    return lax.axis_index("front"), lax.axis_index("leaf")


def pack_kernel(plan, pattern, lr, sr, li, si, lu, su, outer, out, main, ids):
    cut, full, rows, half = plan.full // 2, plan.full, plan.rows, plan.rhs // 2
    ids[...] = pattern[...].reshape(ids.shape)
    for low, inverse, pieces in (
        (0, si, (sr[0], su[0], outer[:half])),
        (rows, li, (lr[0], lu[0], outer[half:])),
    ):
        side = jnp.concatenate(pieces, axis=0).T
        out[low : low + rows, :cut] = inverse[0, :, :cut]
        out[low : low + rows, cut:full] = side
        out[low : low + rows, full:] = inverse[0, :, cut:]
        main[low : low + rows, :cut] = inverse[0, :, :cut]
        main[low : low + rows, cut:] = side


def onward_kernel(plan, pack, across, main, right):
    full = plan.full
    main[...] = across[:, :full]
    right[...] = jnp.where(place()[0] < plan.fronts // 2, across[:, full:], pack[:, full:])


def whole_rows(plan, packs, low, whole):
    front, _ = place()
    cut, full, rows = plan.full // 2, plan.full, plan.rows
    pack, _, _, across, second = packs
    rest = second[low : low + rows, :]
    lower = front < plan.fronts // 2
    rights = (
        pack[low : low + rows, full:],
        jnp.where(lower, 0.0, rest),
        jnp.where(lower, rest, 0.0),
        across[low : low + rows, full:],
    )
    for slot in range(plan.fronts):
        at = pl.multiple_of((front ^ slot) * rows, rows)
        whole[pl.ds(at, rows), :cut] = packs[slot][low : low + rows, :cut]
        whole[pl.ds(at, rows), cut:full] = rights[slot]
        whole[pl.ds(at, rows), full:] = packs[slot][low : low + rows, cut:full]


def outer_kernel(plan, pattern, *refs):
    packs, (picked, natural) = refs[: plan.fronts], refs[plan.fronts :]
    front, _ = place()
    rows, full, edge = plan.rows, plan.full, plan.rhs + plan.upd
    for slot, pack in enumerate(packs):
        at = pl.multiple_of((front ^ slot) * rows, rows)
        natural[pl.ds(at, rows), :128] = pack[:rows, full // 2 : full]
        natural[pl.ds(at, rows), 128:] = pack[rows:, full // 2 : full]
    turned = natural[...].T
    outer = jnp.concatenate([turned[edge:128], turned[128 + edge :]], axis=0)
    picked[...] = nn(outer, one_hot(pattern[plan.groups : plan.groups + 1, :], full))


def fold_rows(plan, rows_of):
    step, full, edge = plan.rows, plan.full, plan.full + plan.rhs + plan.upd
    pieces = [rows_of(front)[:, : (front + 1) * step] for front in (3, 2, 0, 1)]
    pieces += [rows_of(front)[:, full:edge] for front in range(plan.fronts)]
    return jnp.concatenate(pieces, axis=1)


def unfold_rows(plan, folded):
    step, full, edge = plan.rows, plan.full, plan.rhs + plan.upd
    count = folded.shape[0]
    starts = {3: 0, 2: full, 0: full + 3 * step, 1: 2 * full}
    for front in range(plan.fronts):
        wide = (front + 1) * step
        side = 2 * full + 2 * step + front * edge
        pieces = [folded[:, starts[front] : starts[front] + wide]]
        if wide < full:
            pieces.append(jnp.zeros((count, full - wide), jnp.float32))
        pieces.append(folded[:, side : side + edge])
        pieces.append(jnp.zeros((count, plan.width - full - edge), jnp.float32))
        yield front, jnp.concatenate(pieces, axis=1)


def fold_levels(plan, packs, natural):
    whole_rows(plan, packs, 0, natural)
    rows = plan.rows
    for level in range(1, plan.depth + 2):
        offset, share = plan.offset[level], plan.share[level]
        yield offset, fold_rows(
            plan, lambda pos: natural[pos * rows + offset : pos * rows + offset + share, :]
        )


def spread_kernel(plan, *refs):
    packs = refs[: plan.fronts + 1]
    all_part, late_part, high_part, natural = refs[plan.fronts + 1 :]
    for at, piece in fold_levels(plan, packs, natural):
        for out, level in ((all_part, 1), (late_part, 2), (high_part, 3)):
            low = at - plan.offset[level]
            if low >= 0:
                out[low : low + piece.shape[0], :] = piece


def far_kernel(plan, high, all_core, out):
    count = high.shape[0]
    out[:count, :] = high[...]
    out[count:, :] = all_core[plan.offset[3] :, : out.shape[1]]


def leaf_kernel(plan, *refs):
    packs, (all_part, whole, ahead, update, message) = refs[: plan.fronts + 1], refs[plan.fronts + 1 :]
    rhs, upd, full = plan.rhs, plan.upd, plan.full
    whole_rows(plan, packs, plan.rows, whole)
    flipped = whole[:, full:].T
    solved = nt(flipped[:rhs], whole[:, :full])
    ahead[:rhs, :] = solved
    ahead[rhs:, :] = flipped[rhs : rhs + upd]
    result = dense(nt(solved, flipped[rhs : rhs + upd]))
    update[...] = result
    wide = all_part.shape[1]
    message[:, :wide] = all_part[...]
    message[: result.shape[0], wide:] = result


def assemble(plan, level, parts, whole):
    blocks, share = plan.blocks[level], plan.share[level]
    _, group = place()
    for ref, first, slot in parts:
        inner = (group & (blocks - 1)) ^ slot
        for front, piece in unfold_rows(plan, ref[first : first + share, :]):
            dest = pl.multiple_of(front * plan.rows + inner * share, share)
            whole[pl.ds(dest, share), :] = piece


def upper_parts(plan, level, refs):
    own, own_core, by_x, by_x_core, far, far_core = refs
    _, group = place()
    at = plan.offset[level] - plan.offset[3]
    late = at + plan.share[2]
    half = plan.share[3] + plan.share[4]
    parts = [(own, plan.offset[level], 0), (own_core, plan.offset[level], 1)]
    parts += [(by_x, late, 2), (by_x_core, late, 3)]
    side = 4 + 2 * (group & 1)
    parts += [(far, at, side), (far, half + at, side ^ 1)]
    return parts + [(far_core, at, side ^ 3), (far_core, half + at, side ^ 2)]


def lead_level(plan, level, pattern, parts, whole):
    assemble(plan, level, parts, whole)
    flipped = whole[:, plan.full :].T
    right, block = flipped[: plan.rhs], flipped[plan.rhs : plan.rhs + plan.upd]
    fold = nn(block, whole[:, : plan.full])
    hot = one_hot(plan.child_ids(level, place()[1], pattern), plan.full)
    return nn(fold, hot), nt(right, fold)


def back_level(plan, level, pattern, whole):
    front, group = place()
    rhs = plan.rhs
    hot = one_hot(plan.child_ids(level, group, pattern), plan.full)
    matrix = whole[:, : plan.full]
    flipped = whole[:, plan.full :].T
    right, block = flipped[:rhs], flipped[rhs : rhs + plan.upd]
    ahead = nt(jnp.concatenate([right, hot.T], axis=0), matrix)
    stacked = jnp.concatenate([ahead, block], axis=0)
    result = [nt(stacked, ahead[rhs : rhs + plan.upd]), nn(stacked, own_columns(plan, front, matrix))]
    if level > plan.depth:
        return result
    return [nt(block, ahead[rhs:]), nt(ahead[:rhs], block)] + result


def lead_kernel(plan, level, pattern, mine, other, *refs):
    blocks = plan.blocks[level]
    parts = [
        (ref, plan.offset[level] if slot < 2 else 0, slot) for slot, ref in enumerate(refs[:blocks])
    ]
    whole, out, far = refs[blocks:]
    cross, start = lead_level(plan, level, pattern, parts, whole)
    count, wide = mine.shape
    far[...] = other[:count, other.shape[1] - wide :]
    both = jnp.concatenate([undense(mine[...]), undense(far[...])], axis=1)
    out[...] = dense(start - nt(both, cross))


def lower_kernel(plan, pattern, whole, leaf_all, leaf_ahead, near, far, own_part, leaf_part):
    rhs, upd = plan.rhs, plan.upd
    known = jnp.concatenate([undense(near[...]), undense(far[...])], axis=1)
    _, _, picks, columns = back_level(plan, 1, pattern, whole)
    leaf_back = nn(leaf_ahead[...], own_columns(plan, place()[0], leaf_all[:, : plan.full]))
    both = jnp.concatenate([columns, picks], axis=1)
    base = both[:rhs] - nn(known, both[rhs : rhs + 2 * upd])
    slope = both[rhs + 2 * upd :]
    own_part[:rhs] = base[:, : plan.rows]
    own_part[rhs : rhs + 2 * upd] = jnp.zeros((2 * upd, plan.rows), jnp.float32)
    own_part[rhs + 2 * upd :] = slope[:, : plan.rows]
    through = jnp.concatenate([base[:, plan.rows :], -slope[:, plan.rows :]], axis=0)
    through = nn(through, leaf_back[rhs:])
    leaf_part[:rhs] = leaf_back[:rhs] - through[:rhs]
    leaf_part[rhs:] = through[rhs:]


def upper_kernel(plan, pattern, leaf_part, top_s, *refs):
    rhs, upd, group = plan.rhs, plan.upd, place()[1]
    known = jnp.concatenate([undense(refs[0][...]), undense(refs[1][...])], axis=1)
    near = undense(refs[2][...])
    picks, columns = {}, {1: refs[3][...]}
    sources, (out, whole3, whole4) = refs[5:11], refs[11:]
    assemble(plan, 3, upper_parts(plan, 3, sources), whole3)
    assemble(plan, 4, upper_parts(plan, 4, sources), whole4)
    cross, start, picks[3], columns[3] = back_level(plan, 3, pattern, whole3)
    picks[4], columns[4] = back_level(plan, 4, pattern, whole4)
    _, _, picks[2], columns[2] = back_level(plan, 2, pattern, refs[4])
    none = jnp.zeros((upd, upd), jnp.float32)
    unit = one_hot(lax.broadcasted_iota(jnp.int32, (1, upd), 1), upd)

    def step(terms, part):
        known = jnp.concatenate([part[:rhs], jnp.zeros((upd, part.shape[1]), jnp.float32)], axis=0)
        return known - nn(jnp.concatenate(terms, axis=1), part[rhs:])

    gap = jnp.zeros((rhs, upd), jnp.float32)
    both = jnp.concatenate(
        [jnp.concatenate([near, gap], axis=1), jnp.concatenate([none, unit], axis=1)], axis=0
    )
    u3 = jnp.concatenate([start, none], axis=0) - nt(both, cross)
    fixed = jnp.concatenate([known, jnp.zeros((upd, 2 * upd), jnp.float32)], axis=0)
    terms = {4: [u3, jnp.concatenate([top_s[...], none], axis=0)]}
    terms[3] = [both, step(terms[4], picks[4])]
    terms[2] = [fixed, step(terms[3], picks[3])]
    last = step(terms[2], picks[2])
    terms[1] = [jnp.zeros((rhs + upd, 2 * upd), jnp.float32), last]
    leaf_out = step([last], leaf_part)
    gap = jnp.zeros((rhs + upd, upd), jnp.float32)
    chosen = jnp.concatenate([columns[4][: rhs + upd], none_wide(plan), columns[4][rhs + upd :]], axis=0)
    weight = jnp.concatenate([terms[4][0], gap, terms[4][1]], axis=1)
    for level in (3, 2, 1):
        here = plan.label(level, group) == group
        chosen = jnp.where(here, columns[level], chosen)
        weight = jnp.where(here, jnp.concatenate(terms[level], axis=1), weight)
    out[...] = jnp.concatenate([leaf_out, step([weight], chosen)], axis=1)


def none_wide(plan):
    return jnp.zeros((plan.upd, plan.rows), jnp.float32)


def finish_kernel(plan, base, far, out):
    rhs, upd, rows = plan.rhs, plan.upd, plan.rows
    total = base[:rhs] + nn(undense(far[...]), base[rhs:])
    out[0, 0] = total[:, :rows]
    out[1, 0] = total[:, rows:]


def partner(block, axis, distance):
    count = lax.axis_size(axis)
    route = []
    for low in range(count):
        high = low | 1 << distance
        if high != low and high < count:
            route += [(low, high), (high, low)]
    return lax.ppermute(block, axis, route)


def times_rows(vectors, matrix):
    return jnp.dot(
        vectors, matrix, precision=lax.Precision.HIGHEST, preferred_element_type=jnp.float32
    )


def against_rows(vectors, matrix):
    return lax.dot_general(
        vectors,
        matrix,
        (((1,), (1,)), ((), ())),
        precision=lax.Precision.HIGHEST,
        preferred_element_type=jnp.float32,
    )


def general(
    leaf_rhs, sep_rhs, leaf_inverse, sep_inverse, leaf_block, sep_block, pattern, outer_solution
):
    group_count = lax.axis_size("leaf")
    depth = group_count.bit_length() - 1
    group_pos = lax.axis_index("leaf")
    front_pos = lax.axis_index("front")
    local_rows = leaf_rhs.shape[-1]
    full_rows = leaf_inverse.shape[-1]
    vector_count = leaf_rhs.shape[1]
    leaf_r = leaf_rhs[0]
    leaf_inv = leaf_inverse[0]
    leaf_u = leaf_block[0]
    sep_r = sep_rhs[0]
    sep_inv = sep_inverse[0]
    sep_u = sep_block[0]
    all_rows = jnp.arange(full_rows, dtype=jnp.int32)

    def geometry(level):
        blocks = 2 ** min(level, depth)
        share = local_rows // blocks
        offset = local_rows - (local_rows >> level - 1)
        return (share, offset, group_pos % blocks)

    def label_of(level):
        if level > depth:
            return jnp.int32(0)
        return group_pos // 2**level * 2**level + 2 ** (level - 1)

    def ids_of(level):
        return lax.dynamic_index_in_dim(pattern[1], label_of(level), 0, keepdims=False)

    def block_sum(term, level):
        nbits = min(level, depth)
        if nbits == depth:
            return lax.psum(term, ("leaf", "front"))
        piece = lax.psum_scatter(term, "front", scatter_dimension=1, tiled=True)
        for bit in range(nbits):
            piece = piece + partner(piece, "leaf", bit)
        return lax.all_gather(piece, "front", axis=1, tiled=True)

    leaf_y = against_rows(lax.all_gather(leaf_r, "front", axis=1, tiled=True), leaf_inv)
    leaf_ids = lax.dynamic_index_in_dim(pattern[0], group_pos, 0, keepdims=False)
    child_part = against_rows(leaf_y, leaf_u)
    child_ids = leaf_ids
    solved = {}
    for level in range(1, depth + 2):
        share, offset, inner_pos = geometry(level)
        own_r = sep_r[:, offset : offset + share]
        start_col = front_pos * local_rows + inner_pos * share
        contribution = jnp.zeros((vector_count, full_rows), jnp.float32)
        contribution = lax.dynamic_update_slice(contribution, own_r, (jnp.int32(0), start_col))
        selector = (child_ids[:, None] == all_rows[None, :]).astype(jnp.float32)
        contribution = contribution - times_rows(child_part, selector)
        whole_v = block_sum(contribution, level)
        y_level = against_rows(whole_v, sep_inv[offset : offset + share, :])
        solved[level] = y_level
        if level <= depth:
            child_part = against_rows(y_level, sep_u[:, offset : offset + share])
            child_ids = ids_of(level)
    parent_x = lax.all_gather(outer_solution, "front", axis=1, tiled=True)
    sep_full = jnp.zeros((vector_count, full_rows), jnp.float32)
    for level in range(depth + 1, 0, -1):
        share, offset, inner_pos = geometry(level)
        picked = jnp.take(parent_x, ids_of(level), axis=1)
        rest = solved[level] - times_rows(picked, sep_u[:, offset : offset + share])
        term = times_rows(rest, sep_inv[offset : offset + share, :])
        parent_x = block_sum(term, level)
        sep_full = jnp.where(label_of(level) == group_pos, parent_x, sep_full)
    picked = jnp.take(parent_x, leaf_ids, axis=1)
    rest = leaf_y - times_rows(picked, leaf_u)
    leaf_x = lax.psum_scatter(times_rows(rest, leaf_inv), "front", scatter_dimension=1, tiled=True)
    sep_x = lax.dynamic_slice_in_dim(sep_full, front_pos * local_rows, local_rows, 1)
    return jnp.stack([leaf_x, sep_x])[:, None]


def chain(
    plan, leaf_rhs, sep_rhs, leaf_inverse, sep_inverse, leaf_block, sep_block, pattern, outer
):
    full, rows, rhs, upd, width = plan.full, plan.rows, plan.rhs, plan.upd, plan.width

    def kernel(body, outs, *args, extra=(), **kw):
        return call(functools.partial(body, plan, *extra), outs, args, **kw)

    pack, main, ids = kernel(
        pack_kernel,
        [
            (2 * rows, width),
            (2 * rows, full),
            ((pattern.shape[0] * pattern.shape[1], upd), jnp.int32),
        ],
        pattern, leaf_rhs, sep_rhs, leaf_inverse, sep_inverse, leaf_block, sep_block, outer,
        chip=False,
    )
    across = exchange(pack, "front", 3)
    beside = exchange(main, "front", 1)
    onward, onward_second = kernel(
        onward_kernel, [(2 * rows, full), (2 * rows, full // 2)], pack, across
    )
    beyond = exchange(onward, "front", 1)
    second = exchange(onward_second, "front", 1)
    wide = 4 * full
    all_part, late_part, high_part = kernel(
        spread_kernel,
        [
            (rows, wide),
            (rows - plan.share[1], wide),
            (plan.share[3] + plan.share[4], wide),
        ],
        pack, beside, beyond, across, second,
        scratch=[pltpu.VMEM((full, width), jnp.float32)],
    )
    by_x = exchange(late_part, "leaf", 2)
    leaf_beyond, _ = lax.optimization_barrier((beyond, all_part))
    leaf_all, leaf_ahead, u0, message = kernel(
        leaf_kernel,
        [
            (full, width),
            (rhs + upd, full),
            (rhs // 4, 4 * upd),
            (rows, wide + 4 * upd),
        ],
        pack, beside, leaf_beyond, across, second, all_part,
    )
    all_core = exchange(message, "leaf", 1)
    high_part, _ = lax.optimization_barrier((high_part, u0))
    (far_part,) = kernel(far_kernel, [(2 * high_part.shape[0], wide)], high_part, all_core)
    far = lax.ppermute(far_part, "leaf", [(src, src ^ (6 if src % 2 else 4)) for src in range(plan.groups)])
    def lead_of(level, mine, other, *parts):
        return kernel(
            lead_kernel,
            [(full, width)] + [(rhs // 4, 4 * upd)] * 2,
            ids, mine, other, *parts,
            extra=(level,),
        )

    whole1, u1, u0_far = lead_of(1, u0, all_core, all_part, all_core)
    u1_far = exchange(u1, "leaf", 2)

    whole1, _ = lax.optimization_barrier((whole1, u1))
    own_part, leaf_part = kernel(
        lower_kernel,
        [(rhs + 3 * upd, rows), (rhs + upd, rows)],
        ids, whole1, leaf_all, leaf_ahead, u0, u0_far,
    )
    spare_beyond, _ = lax.optimization_barrier((beyond, u1))
    (top_s,) = kernel(
        outer_kernel,
        [(rhs, upd)],
        ids, pack, beside, spare_beyond, across,
        scratch=[pltpu.VMEM((full, 256), jnp.float32)],
    )
    by_x, far, u1_far, own_part, top_s = lax.optimization_barrier(
        (by_x, far, u1_far, own_part, top_s)
    )
    by_x_core = exchange(by_x, "leaf", 1)
    far_core = exchange(far, "leaf", 1)
    whole2, u2, u1_far = lead_of(2, u1, u1_far, all_part, all_core, by_x, by_x_core)
    u2_far = exchange(u2, "leaf", 4)
    (base,) = kernel(
        upper_kernel,
        [(rhs + upd, 2 * rows)],
        ids, leaf_part, top_s, u1, u1_far, u2, own_part, whole2,
        all_part, all_core, by_x, by_x_core, far, far_core,
        scratch=[pltpu.VMEM((full, width), jnp.float32)] * 2,
    )
    (out,) = kernel(finish_kernel, [(2, 1, rhs, rows)], base, u2_far)
    return out


def body(*args):
    groups, fronts = lax.axis_size("leaf"), lax.axis_size("front")
    rhs, rows, upd = args[0].shape[1], args[0].shape[2], args[4].shape[1]
    plan = Plan(groups, fronts, rhs, upd, rows)
    if (groups, fronts) == (8, 4) and rows == 64 and rhs == 64 and upd == 32:
        return chain(plan, *args)
    return general(*args)


def solution(mesh):
    placed = (
        P("leaf", None, "front"),
        P("leaf", None, "front"),
        P("leaf", "front", None),
        P("leaf", "front", None),
        P("leaf", None, "front"),
        P("leaf", None, "front"),
        P(),
        P(None, "front"),
    )
    return jax.shard_map(
        body, mesh=mesh, in_specs=placed, out_specs=P(None, "leaf", None, "front"), check_vma=False
    )
```

```python
import functools
import jax
import jax.numpy as jnp
from jax import lax
from jax.experimental import pallas as pl
from jax.experimental.pallas import tpu as pltpu
from jax.sharding import PartitionSpec as P

def halves(value):
    high = value.astype(jnp.bfloat16)
    return high, (value - high.astype(jnp.float32)).astype(jnp.bfloat16)


def product(left, right, side):
    def term(one, two):
        return lax.dot_general(
            one, two, (((1,), (side,)), ((), ())), preferred_element_type=jnp.float32
        )

    (left_high, left_low), (right_high, right_low) = halves(left), halves(right)
    return term(left_high, right_high) + (term(left_high, right_low) + term(left_low, right_high))


def nn(left, right):
    return product(left, right, 0)


def nt(left, right):
    return product(left, right, 1)


def exchange(block, axis, mask):
    count = lax.axis_size(axis)
    return lax.ppermute(block, axis, [(src, src ^ mask) for src in range(count)])


def call(kernel, outs, args, scratch=(), chip=True, cost=1000):
    if chip:
        args = [
            pltpu.with_memory_space_constraint(arg, pltpu.VMEM)
            if arg.ndim == 2
            else arg
            for arg in args
        ]
    return pl.pallas_call(
        kernel,
        out_shape=[
            jax.ShapeDtypeStruct(out, jnp.float32)
            if len(out) == 4
            else pltpu.VMEM(*out)
            if isinstance(out[0], tuple)
            else pltpu.VMEM(out, jnp.float32)
            for out in outs
        ],
        in_specs=[pl.BlockSpec(memory_space=pltpu.VMEM) for _ in args],
        out_specs=[pl.BlockSpec(memory_space=pltpu.VMEM) for _ in outs],
        scratch_shapes=list(scratch),
        compiler_params=pltpu.CompilerParams(vmem_limit_bytes=8 << 20) if chip else None,
        cost_estimate=pl.CostEstimate(flops=cost, bytes_accessed=cost, transcendentals=0),
    )(*args)


class Plan:
    def __init__(self, groups, fronts, rhs, upd, rows):
        self.groups, self.fronts, self.rhs, self.upd, self.rows = groups, fronts, rhs, upd, rows
        self.depth = groups.bit_length() - 1
        self.full = fronts * rows
        self.width = self.full + 128
        self.share, self.offset, self.base, self.blocks = {}, {}, {}, {}
        base = 0
        for level in range(1, self.depth + 2):
            self.blocks[level] = 2 ** min(level, self.depth)
            self.share[level] = rows // self.blocks[level]
            self.offset[level] = rows - (rows >> level - 1)
            self.base[level] = base
            base += fronts * self.share[level]

    def label(self, level, group):
        if level > self.depth:
            return jnp.int32(0)
        return (group // 2**level) * 2**level + 2 ** (level - 1)

    def child_ids(self, level, group, pattern):
        if level == 1:
            kind, labels = 0, (group, group ^ 1)
        elif level > self.depth:
            kind, labels = 1, (self.label(level - 1, group),)
        else:
            kind = 1
            labels = tuple(self.label(level - 1, far) for far in (group, group ^ 2 ** (level - 1)))
        return jnp.concatenate([pattern[pl.ds(kind * self.groups + label, 1), :] for label in labels], axis=1)


def one_hot(ids, count, start=0):
    rows = lax.broadcasted_iota(jnp.int32, (count, ids.shape[1]), 0) + start
    return (rows == ids).astype(jnp.float32)


def own_columns(plan, front, value):
    rows = plan.rows
    result = value[:, :rows]
    for slot in range(1, plan.fronts):
        result = jnp.where(front == slot, value[:, slot * rows : (slot + 1) * rows], result)
    return result


def dense(value):
    count = value.shape[0] // 4
    return jnp.concatenate([value[pos * count : (pos + 1) * count] for pos in range(4)], axis=1)


def undense(value):
    count = value.shape[1] // 4
    return jnp.concatenate([value[:, pos * count : (pos + 1) * count] for pos in range(4)], axis=0)


def place():
    return lax.axis_index("front"), lax.axis_index("leaf")


def pack_kernel(plan, pattern, lr, sr, li, si, lu, su, outer, out, main, ids):
    cut, full, rows, half = plan.full // 2, plan.full, plan.rows, plan.rhs // 2
    ids[...] = pattern[...].reshape(ids.shape)
    for low, inverse, pieces in (
        (0, si, (sr[0], su[0], outer[:half])),
        (rows, li, (lr[0], lu[0], outer[half:])),
    ):
        side = jnp.concatenate(pieces, axis=0).T
        out[low : low + rows, :cut] = inverse[0, :, :cut]
        out[low : low + rows, cut:full] = side
        out[low : low + rows, full:] = inverse[0, :, cut:]
        main[low : low + rows, :cut] = inverse[0, :, :cut]
        main[low : low + rows, cut:] = side


def onward_kernel(plan, pack, across, main, right):
    full = plan.full
    main[...] = across[:, :full]
    right[...] = jnp.where(place()[0] < plan.fronts // 2, across[:, full:], pack[:, full:])


def whole_rows(plan, packs, low, whole):
    front, _ = place()
    cut, full, rows = plan.full // 2, plan.full, plan.rows
    pack, _, _, across, second = packs
    rest = second[low : low + rows, :]
    lower = front < plan.fronts // 2
    rights = (
        pack[low : low + rows, full:],
        jnp.where(lower, 0.0, rest),
        jnp.where(lower, rest, 0.0),
        across[low : low + rows, full:],
    )
    for slot in range(plan.fronts):
        at = pl.multiple_of((front ^ slot) * rows, rows)
        whole[pl.ds(at, rows), :cut] = packs[slot][low : low + rows, :cut]
        whole[pl.ds(at, rows), cut:full] = rights[slot]
        whole[pl.ds(at, rows), full:] = packs[slot][low : low + rows, cut:full]


def outer_kernel(plan, pattern, *refs):
    packs, (picked, natural) = refs[: plan.fronts], refs[plan.fronts :]
    front, _ = place()
    rows, full, edge = plan.rows, plan.full, plan.rhs + plan.upd
    for slot, pack in enumerate(packs):
        at = pl.multiple_of((front ^ slot) * rows, rows)
        natural[pl.ds(at, rows), :128] = pack[:rows, full // 2 : full]
        natural[pl.ds(at, rows), 128:] = pack[rows:, full // 2 : full]
    turned = natural[...].T
    outer = jnp.concatenate([turned[edge:128], turned[128 + edge :]], axis=0)
    picked[...] = nn(outer, one_hot(pattern[plan.groups : plan.groups + 1, :], full))


def fold_rows(plan, rows_of):
    step, full, edge = plan.rows, plan.full, plan.full + plan.rhs + plan.upd
    pieces = [rows_of(front)[:, : (front + 1) * step] for front in (3, 2, 0, 1)]
    pieces += [rows_of(front)[:, full:edge] for front in range(plan.fronts)]
    return jnp.concatenate(pieces, axis=1)


def unfold_rows(plan, folded):
    step, full, edge = plan.rows, plan.full, plan.rhs + plan.upd
    count = folded.shape[0]
    starts = {3: 0, 2: full, 0: full + 3 * step, 1: 2 * full}
    for front in range(plan.fronts):
        wide = (front + 1) * step
        side = 2 * full + 2 * step + front * edge
        pieces = [folded[:, starts[front] : starts[front] + wide]]
        if wide < full:
            pieces.append(jnp.zeros((count, full - wide), jnp.float32))
        pieces.append(folded[:, side : side + edge])
        pieces.append(jnp.zeros((count, plan.width - full - edge), jnp.float32))
        yield front, jnp.concatenate(pieces, axis=1)


def fold_levels(plan, packs, natural):
    whole_rows(plan, packs, 0, natural)
    rows = plan.rows
    for level in range(1, plan.depth + 2):
        offset, share = plan.offset[level], plan.share[level]
        yield offset, fold_rows(
            plan, lambda pos: natural[pos * rows + offset : pos * rows + offset + share, :]
        )


def spread_kernel(plan, *refs):
    packs = refs[: plan.fronts + 1]
    all_part, late_part, high_part, natural = refs[plan.fronts + 1 :]
    for at, piece in fold_levels(plan, packs, natural):
        for out, level in ((all_part, 1), (late_part, 2), (high_part, 3)):
            low = at - plan.offset[level]
            if low >= 0:
                out[low : low + piece.shape[0], :] = piece


def far_kernel(plan, high, all_core, out):
    count = high.shape[0]
    out[:count, :] = high[...]
    out[count:, :] = all_core[plan.offset[3] :, : out.shape[1]]


def leaf_kernel(plan, *refs):
    packs, (all_part, whole, ahead, update, message) = refs[: plan.fronts + 1], refs[plan.fronts + 1 :]
    rhs, upd, full = plan.rhs, plan.upd, plan.full
    whole_rows(plan, packs, plan.rows, whole)
    flipped = whole[:, full:].T
    solved = nt(flipped[:rhs], whole[:, :full])
    ahead[:rhs, :] = solved
    ahead[rhs:, :] = flipped[rhs : rhs + upd]
    result = dense(nt(solved, flipped[rhs : rhs + upd]))
    update[...] = result
    wide = all_part.shape[1]
    message[:, :wide] = all_part[...]
    message[: result.shape[0], wide:] = result


def assemble(plan, level, parts, whole):
    blocks, share = plan.blocks[level], plan.share[level]
    _, group = place()
    for ref, first, slot in parts:
        inner = (group & (blocks - 1)) ^ slot
        for front, piece in unfold_rows(plan, ref[first : first + share, :]):
            dest = pl.multiple_of(front * plan.rows + inner * share, share)
            whole[pl.ds(dest, share), :] = piece


def upper_parts(plan, level, refs):
    own, own_core, by_x, by_x_core, far, far_core = refs
    _, group = place()
    at = plan.offset[level] - plan.offset[3]
    late = at + plan.share[2]
    half = plan.share[3] + plan.share[4]
    parts = [(own, plan.offset[level], 0), (own_core, plan.offset[level], 1)]
    parts += [(by_x, late, 2), (by_x_core, late, 3)]
    side = 4 + 2 * (group & 1)
    parts += [(far, at, side), (far, half + at, side ^ 1)]
    return parts + [(far_core, at, side ^ 3), (far_core, half + at, side ^ 2)]


def lead_level(plan, level, pattern, parts, whole):
    assemble(plan, level, parts, whole)
    flipped = whole[:, plan.full :].T
    right, block = flipped[: plan.rhs], flipped[plan.rhs : plan.rhs + plan.upd]
    fold = nn(block, whole[:, : plan.full])
    hot = one_hot(plan.child_ids(level, place()[1], pattern), plan.full)
    return nn(fold, hot), nt(right, fold)


def back_level(plan, level, pattern, whole):
    front, group = place()
    rhs = plan.rhs
    hot = one_hot(plan.child_ids(level, group, pattern), plan.full)
    matrix = whole[:, : plan.full]
    flipped = whole[:, plan.full :].T
    right, block = flipped[:rhs], flipped[rhs : rhs + plan.upd]
    ahead = nt(jnp.concatenate([right, hot.T], axis=0), matrix)
    stacked = jnp.concatenate([ahead, block], axis=0)
    result = [nt(stacked, ahead[rhs : rhs + plan.upd]), nn(stacked, own_columns(plan, front, matrix))]
    if level > plan.depth:
        return result
    return [nt(block, ahead[rhs:]), nt(ahead[:rhs], block)] + result


def lead_kernel(plan, level, pattern, *refs):
    blocks = plan.blocks[level]
    parts = [
        (ref, plan.offset[level] if slot < 2 else 0, slot) for slot, ref in enumerate(refs[:blocks])
    ]
    whole, cross, start = refs[blocks:]
    cross[...], start[...] = lead_level(plan, level, pattern, parts, whole)


def lower_kernel(plan, pattern, whole, leaf_all, leaf_ahead, near, far, own_part, leaf_part):
    rhs, upd = plan.rhs, plan.upd
    known = jnp.concatenate([undense(near[...]), undense(far[...])], axis=1)
    _, _, picks, columns = back_level(plan, 1, pattern, whole)
    leaf_back = nn(leaf_ahead[...], own_columns(plan, place()[0], leaf_all[:, : plan.full]))
    both = jnp.concatenate([columns, picks], axis=1)
    base = both[:rhs] - nn(known, both[rhs : rhs + 2 * upd])
    slope = both[rhs + 2 * upd :]
    own_part[:rhs] = base[:, : plan.rows]
    own_part[rhs : rhs + 2 * upd] = jnp.zeros((2 * upd, plan.rows), jnp.float32)
    own_part[rhs + 2 * upd :] = slope[:, : plan.rows]
    through = jnp.concatenate([base[:, plan.rows :], -slope[:, plan.rows :]], axis=0)
    through = nn(through, leaf_back[rhs:])
    leaf_part[:rhs] = leaf_back[:rhs] - through[:rhs]
    leaf_part[rhs:] = through[rhs:]


def upper_kernel(plan, pattern, leaf_part, top_s, *refs):
    rhs, upd, group = plan.rhs, plan.upd, place()[1]
    known = jnp.concatenate([undense(refs[0][...]), undense(refs[1][...])], axis=1)
    near = undense(refs[2][...])
    picks, columns = {}, {1: refs[3][...]}
    sources, (out, whole3, whole4) = refs[5:11], refs[11:]
    assemble(plan, 3, upper_parts(plan, 3, sources), whole3)
    assemble(plan, 4, upper_parts(plan, 4, sources), whole4)
    cross, start, picks[3], columns[3] = back_level(plan, 3, pattern, whole3)
    picks[4], columns[4] = back_level(plan, 4, pattern, whole4)
    _, _, picks[2], columns[2] = back_level(plan, 2, pattern, refs[4])
    none = jnp.zeros((upd, upd), jnp.float32)
    unit = one_hot(lax.broadcasted_iota(jnp.int32, (1, upd), 1), upd)

    def step(terms, part):
        known = jnp.concatenate([part[:rhs], jnp.zeros((upd, part.shape[1]), jnp.float32)], axis=0)
        return known - nn(jnp.concatenate(terms, axis=1), part[rhs:])

    gap = jnp.zeros((rhs, upd), jnp.float32)
    both = jnp.concatenate(
        [jnp.concatenate([near, gap], axis=1), jnp.concatenate([none, unit], axis=1)], axis=0
    )
    u3 = jnp.concatenate([start, none], axis=0) - nt(both, cross)
    fixed = jnp.concatenate([known, jnp.zeros((upd, 2 * upd), jnp.float32)], axis=0)
    terms = {4: [u3, jnp.concatenate([top_s[...], none], axis=0)]}
    terms[3] = [both, step(terms[4], picks[4])]
    terms[2] = [fixed, step(terms[3], picks[3])]
    last = step(terms[2], picks[2])
    terms[1] = [jnp.zeros((rhs + upd, 2 * upd), jnp.float32), last]
    leaf_out = step([last], leaf_part)
    gap = jnp.zeros((rhs + upd, upd), jnp.float32)
    chosen = jnp.concatenate([columns[4][: rhs + upd], none_wide(plan), columns[4][rhs + upd :]], axis=0)
    weight = jnp.concatenate([terms[4][0], gap, terms[4][1]], axis=1)
    for level in (3, 2, 1):
        here = plan.label(level, group) == group
        chosen = jnp.where(here, columns[level], chosen)
        weight = jnp.where(here, jnp.concatenate(terms[level], axis=1), weight)
    out[...] = jnp.concatenate([leaf_out, step([weight], chosen)], axis=1)


def none_wide(plan):
    return jnp.zeros((plan.upd, plan.rows), jnp.float32)


def finish_kernel(plan, base, far, out):
    rhs, upd, rows = plan.rhs, plan.upd, plan.rows
    total = base[:rhs] + nn(undense(far[...]), base[rhs:])
    out[0, 0] = total[:, :rows]
    out[1, 0] = total[:, rows:]


def first_update_kernel(plan, start, cross, mine, message, out, other):
    count, wide = mine.shape
    other[...] = message[:count, message.shape[1] - wide :]
    both = jnp.concatenate([undense(mine[...]), undense(other[...])], axis=1)
    out[...] = dense(start[...] - nt(both, cross[...]))


def update_kernel(plan, start, cross, mine, other, out):
    both = jnp.concatenate([undense(mine[...]), undense(other[...])], axis=1)
    out[...] = dense(start[...] - nt(both, cross[...]))


def partner(block, axis, distance):
    count = lax.axis_size(axis)
    route = []
    for low in range(count):
        high = low | 1 << distance
        if high != low and high < count:
            route += [(low, high), (high, low)]
    return lax.ppermute(block, axis, route)


def times_rows(vectors, matrix):
    return jnp.dot(
        vectors, matrix, precision=lax.Precision.HIGHEST, preferred_element_type=jnp.float32
    )


def against_rows(vectors, matrix):
    return lax.dot_general(
        vectors,
        matrix,
        (((1,), (1,)), ((), ())),
        precision=lax.Precision.HIGHEST,
        preferred_element_type=jnp.float32,
    )


def general(
    leaf_rhs, sep_rhs, leaf_inverse, sep_inverse, leaf_block, sep_block, pattern, outer_solution
):
    group_count = lax.axis_size("leaf")
    depth = group_count.bit_length() - 1
    group_pos = lax.axis_index("leaf")
    front_pos = lax.axis_index("front")
    local_rows = leaf_rhs.shape[-1]
    full_rows = leaf_inverse.shape[-1]
    vector_count = leaf_rhs.shape[1]
    leaf_r = leaf_rhs[0]
    leaf_inv = leaf_inverse[0]
    leaf_u = leaf_block[0]
    sep_r = sep_rhs[0]
    sep_inv = sep_inverse[0]
    sep_u = sep_block[0]
    all_rows = jnp.arange(full_rows, dtype=jnp.int32)

    def geometry(level):
        blocks = 2 ** min(level, depth)
        share = local_rows // blocks
        offset = local_rows - (local_rows >> level - 1)
        return (share, offset, group_pos % blocks)

    def label_of(level):
        if level > depth:
            return jnp.int32(0)
        return group_pos // 2**level * 2**level + 2 ** (level - 1)

    def ids_of(level):
        return lax.dynamic_index_in_dim(pattern[1], label_of(level), 0, keepdims=False)

    def block_sum(term, level):
        nbits = min(level, depth)
        if nbits == depth:
            return lax.psum(term, ("leaf", "front"))
        piece = lax.psum_scatter(term, "front", scatter_dimension=1, tiled=True)
        for bit in range(nbits):
            piece = piece + partner(piece, "leaf", bit)
        return lax.all_gather(piece, "front", axis=1, tiled=True)

    leaf_y = against_rows(lax.all_gather(leaf_r, "front", axis=1, tiled=True), leaf_inv)
    leaf_ids = lax.dynamic_index_in_dim(pattern[0], group_pos, 0, keepdims=False)
    child_part = against_rows(leaf_y, leaf_u)
    child_ids = leaf_ids
    solved = {}
    for level in range(1, depth + 2):
        share, offset, inner_pos = geometry(level)
        own_r = sep_r[:, offset : offset + share]
        start_col = front_pos * local_rows + inner_pos * share
        contribution = jnp.zeros((vector_count, full_rows), jnp.float32)
        contribution = lax.dynamic_update_slice(contribution, own_r, (jnp.int32(0), start_col))
        selector = (child_ids[:, None] == all_rows[None, :]).astype(jnp.float32)
        contribution = contribution - times_rows(child_part, selector)
        whole_v = block_sum(contribution, level)
        y_level = against_rows(whole_v, sep_inv[offset : offset + share, :])
        solved[level] = y_level
        if level <= depth:
            child_part = against_rows(y_level, sep_u[:, offset : offset + share])
            child_ids = ids_of(level)
    parent_x = lax.all_gather(outer_solution, "front", axis=1, tiled=True)
    sep_full = jnp.zeros((vector_count, full_rows), jnp.float32)
    for level in range(depth + 1, 0, -1):
        share, offset, inner_pos = geometry(level)
        picked = jnp.take(parent_x, ids_of(level), axis=1)
        rest = solved[level] - times_rows(picked, sep_u[:, offset : offset + share])
        term = times_rows(rest, sep_inv[offset : offset + share, :])
        parent_x = block_sum(term, level)
        sep_full = jnp.where(label_of(level) == group_pos, parent_x, sep_full)
    picked = jnp.take(parent_x, leaf_ids, axis=1)
    rest = leaf_y - times_rows(picked, leaf_u)
    leaf_x = lax.psum_scatter(times_rows(rest, leaf_inv), "front", scatter_dimension=1, tiled=True)
    sep_x = lax.dynamic_slice_in_dim(sep_full, front_pos * local_rows, local_rows, 1)
    return jnp.stack([leaf_x, sep_x])[:, None]


def chain(
    plan, leaf_rhs, sep_rhs, leaf_inverse, sep_inverse, leaf_block, sep_block, pattern, outer
):
    full, rows, rhs, upd, width = plan.full, plan.rows, plan.rhs, plan.upd, plan.width

    def kernel(body, outs, *args, extra=(), **kw):
        return call(functools.partial(body, plan, *extra), outs, args, **kw)

    pack, main, ids = kernel(
        pack_kernel,
        [
            (2 * rows, width),
            (2 * rows, full),
            ((pattern.shape[0] * pattern.shape[1], upd), jnp.int32),
        ],
        pattern, leaf_rhs, sep_rhs, leaf_inverse, sep_inverse, leaf_block, sep_block, outer,
        chip=False,
    )
    across = exchange(pack, "front", 3)
    beside = exchange(main, "front", 1)
    onward, onward_second = kernel(
        onward_kernel, [(2 * rows, full), (2 * rows, full // 2)], pack, across
    )
    beyond = exchange(onward, "front", 1)
    second = exchange(onward_second, "front", 1)
    wide = 4 * full
    all_part, late_part, high_part = kernel(
        spread_kernel,
        [
            (rows, wide),
            (rows - plan.share[1], wide),
            (plan.share[3] + plan.share[4], wide),
        ],
        pack, beside, beyond, across, second,
        scratch=[pltpu.VMEM((full, width), jnp.float32)],
    )
    by_x = exchange(late_part, "leaf", 2)
    leaf_beyond, _ = lax.optimization_barrier((beyond, all_part))
    leaf_all, leaf_ahead, u0, message = kernel(
        leaf_kernel,
        [
            (full, width),
            (rhs + upd, full),
            (rhs // 4, 4 * upd),
            (rows, wide + 4 * upd),
        ],
        pack, beside, leaf_beyond, across, second, all_part,
    )
    all_core = exchange(message, "leaf", 1)
    high_part, _ = lax.optimization_barrier((high_part, u0))
    (far_part,) = kernel(far_kernel, [(2 * high_part.shape[0], wide)], high_part, all_core)
    far = lax.ppermute(far_part, "leaf", [(src, src ^ (6 if src % 2 else 4)) for src in range(plan.groups)])
    def lead_of(level, *parts):
        return kernel(
            lead_kernel,
            [(full, width), (upd, 2 * upd), (rhs, upd)],
            ids, *parts,
            extra=(level,),
        )

    whole1, cross1, start1 = lead_of(1, all_part, all_core)
    u1, u0_far = kernel(
        first_update_kernel, [(rhs // 4, 4 * upd)] * 2, start1, cross1, u0, all_core
    )
    u1_far = exchange(u1, "leaf", 2)

    whole1, _ = lax.optimization_barrier((whole1, u1))
    own_part, leaf_part = kernel(
        lower_kernel,
        [(rhs + 3 * upd, rows), (rhs + upd, rows)],
        ids, whole1, leaf_all, leaf_ahead, u0, u0_far,
    )
    spare_beyond, _ = lax.optimization_barrier((beyond, u1))
    (top_s,) = kernel(
        outer_kernel,
        [(rhs, upd)],
        ids, pack, beside, spare_beyond, across,
        scratch=[pltpu.VMEM((full, 256), jnp.float32)],
    )
    by_x, far, u1_far, own_part, top_s = lax.optimization_barrier(
        (by_x, far, u1_far, own_part, top_s)
    )
    by_x_core = exchange(by_x, "leaf", 1)
    whole2, cross2, start2 = lead_of(2, all_part, all_core, by_x, by_x_core)
    far, _ = lax.optimization_barrier((far, cross2))
    far_core = exchange(far, "leaf", 1)
    (u2,) = kernel(
        update_kernel, [(rhs // 4, 4 * upd)], start2, cross2, u1, u1_far
    )
    u2_far = exchange(u2, "leaf", 4)
    (base,) = kernel(
        upper_kernel,
        [(rhs + upd, 2 * rows)],
        ids, leaf_part, top_s, u1, u1_far, u2, own_part, whole2,
        all_part, all_core, by_x, by_x_core, far, far_core,
        scratch=[pltpu.VMEM((full, width), jnp.float32)] * 2,
    )
    (out,) = kernel(finish_kernel, [(2, 1, rhs, rows)], base, u2_far)
    return out


def body(*args):
    groups, fronts = lax.axis_size("leaf"), lax.axis_size("front")
    rhs, rows, upd = args[0].shape[1], args[0].shape[2], args[4].shape[1]
    plan = Plan(groups, fronts, rhs, upd, rows)
    if (groups, fronts) == (8, 4) and rows == 64 and rhs == 64 and upd == 32:
        return chain(plan, *args)
    return general(*args)


def solution(mesh):
    placed = (
        P("leaf", None, "front"),
        P("leaf", None, "front"),
        P("leaf", "front", None),
        P("leaf", "front", None),
        P("leaf", None, "front"),
        P("leaf", None, "front"),
        P(),
        P(None, "front"),
    )
    return jax.shard_map(
        body, mesh=mesh, in_specs=placed, out_specs=P(None, "leaf", None, "front"), check_vma=False
    )
```
